512 devices in a mesh: sensor: 8 (over z_lo, x), cell: 64 (over z_hi, y, core).
Axes of the slice: x: 4, y: 8, z: 8 (z_hi: 4, z_lo: 2; z = z_hi * 2 + z_lo), core: 2. Of those that a mesh axis runs over, the one named last changes fastest.
Arguments:
- swath: float32 [8, 64, 32768], P('sensor', None, 'cell'), may hold values from -6 to 6
- enc_weight: float32 [8, 64, 192], P('sensor'), may hold values from -0.4375 to 0.4375
- key_weight: float32 [64, 64], replicated, may hold values from -0.75 to 0.75
- value_weight: float32 [64, 64], replicated, may hold values from -0.75 to 0.75
- cell_query: float32 [64, 16384], P(None, 'cell'), may hold values from -6 to 6
- quality: float32 [8, 32768], P('sensor', 'cell'), may hold values from -4 to 302
- sample_cell: int32 [8, 32768], P('sensor', 'cell'), may hold values from 0 to 255
- live: int32 [8, 64], P('sensor', 'cell'), may hold values from 128 to 512
- neighbours: int32 [8, 16384], P(None, 'cell'), may hold values from 0 to 16383, as said below
- hp_weight: float32 [64, 576], replicated, may hold values from -0.25 to 0.25
Outputs:
- joined: float32 [64, 16384], P('sensor', 'cell')
The draws below stay inside these ranges and needn't reach their ends.
Inputs may be any that keep to these rules, and one draw needn't show every extreme that they name: `neighbours`: a cell range is a patch of 16 x 16 cells, local index row * 16 + column; every neighbour lies within 257 cells of its own cell, either in the cell's own range or in an adjacent one, and then in the first column of the next range or the last column of the previous range.
All inputs are finite; a program needn't handle non-finite values.
Results may differ from the reference program's by a relative error of at most 0.0003.
Values sent between devices are 32-bit elements; how exact they have to be, the bound alone decides.
A program may use at most 64 MiB of HBM per device.

```python
import math
import jax
import jax.numpy as jnp
from jax import lax

C = 64
KT = 3
NB = 9
SIDE = 16
CELL_DEV = 256
SAMPLES_DEV = 512
RANGES = 64
SENSORS = 8
CELLS = 16384
SAMPLES = 32768


def cell_map(key):
    base = jax.random.fold_in(key, 11)
    first_key, second_key = jax.random.split(base)
    first = jax.random.randint(first_key, (SENSORS, SAMPLES), 0, CELL_DEV)
    second = jax.random.randint(second_key, (SENSORS, SAMPLES), 0, CELL_DEV)
    slots = jnp.arange(SAMPLES, dtype=jnp.int32)
    position = slots % SAMPLES_DEV
    offset = jnp.minimum(first, second)
    offset = jnp.where((position == 0)[None, :], 0, offset)
    offset = jnp.where((position == SAMPLES_DEV - 1)[None, :], CELL_DEV - 1, offset)
    return offset.astype(jnp.int32)


def draw_sample_cell(key, part):
    return cell_map(key)


def draw_quality(key, part):
    base = jax.random.fold_in(key, 23)
    normal_key = jax.random.fold_in(base, 3)
    return jnp.clip(jax.random.normal(normal_key, (SENSORS, SAMPLES), jnp.float32), -4.0, 4.0)


def draw_live(key, part):
    base = jax.random.fold_in(key, 37)
    count_key, top_key, step_key = jax.random.split(base, 3)
    lowest = SAMPLES_DEV // 4
    counts = jax.random.randint(count_key, (SENSORS, RANGES), lowest, SAMPLES_DEV + 1)
    top_col = jax.random.randint(top_key, (SENSORS, 1), 0, RANGES)
    low_col = (top_col + 1 + jax.random.randint(step_key, (SENSORS, 1), 0, RANGES - 1)) % RANGES
    column = jnp.arange(RANGES, dtype=jnp.int32)[None, :]
    counts = jnp.where(column == top_col, SAMPLES_DEV, counts)
    counts = jnp.where(column == low_col, lowest, counts)
    return counts.astype(jnp.int32)


def draw_neighbours(key, part):
    base = jax.random.fold_in(key, 53)
    cells = jnp.arange(CELLS, dtype=jnp.int32)
    range_id = cells // CELL_DEV
    local = cells % CELL_DEV
    row = local // SIDE
    column = local % SIDE
    row_steps = jnp.array([-1, -1, -1, 0, 0, 1, 1, 1], dtype=jnp.int32)
    col_steps = jnp.array([-1, 0, 1, -1, 1, -1, 0, 1], dtype=jnp.int32)
    scores = jax.random.randint(base, (NB - 1, CELLS), 0, 1 << 20) * 8 + jnp.arange(NB - 1, dtype=jnp.int32)[:, None]
    order = jnp.argsort(scores, axis=0).astype(jnp.int32)
    drow = row_steps[order]
    dcol = col_steps[order]
    new_row = jnp.clip(row[None, :] + drow, 0, SIDE - 1)
    raw_col = column[None, :] + dcol
    move = (raw_col >= SIDE).astype(jnp.int32) - (raw_col < 0).astype(jnp.int32)
    new_range = range_id[None, :] + move
    outside = (new_range < 0) | (new_range >= RANGES)
    new_col = jnp.where(outside, jnp.clip(raw_col, 0, SIDE - 1), raw_col - move * SIDE)
    new_range = jnp.where(outside, range_id[None, :], new_range)
    return (new_range * CELL_DEV + new_row * SIDE + new_col).astype(jnp.int32)


def block_scale(own_key, extent, pieces, least, top_value):
    def one(axis_at, parts):
        draws = jax.random.uniform(jax.random.fold_in(jax.random.fold_in(own_key, 6), axis_at), (parts,), jnp.float32, least / len(pieces), top_value / len(pieces))
        return jnp.repeat(jnp.exp(draws), extent[axis_at] // parts).reshape((-1,) + (1,) * (len(extent) - axis_at - 1))

    gain = one(*pieces[0])
    for cut in pieces[1:]:
        gain = gain * one(*cut)
    return gain


def gaussian(own_key, shape, spread, reach, shards=(), kind=jnp.bfloat16):
    values = spread * jax.random.normal(own_key, shape, jnp.float32)
    if shards:
        values = values * block_scale(own_key, shape, shards, -0.22, 0.18)
    return jnp.clip(values, -reach, reach).astype(kind)


def setup_inputs(seed: int = 0) -> dict:
    splits = jax.random.split(jax.random.key(seed), 11)
    swath = gaussian(splits[0], (SENSORS, C, SAMPLES), 1.0, 6.0, ((0, 8), (2, 64)), jnp.float32)
    enc_weight = gaussian(splits[1], (SENSORS, C, KT * C), (KT * C) ** -0.5, 0.4375, ((0, 8),), jnp.float32)
    key_weight = gaussian(splits[2], (C, C), C ** -0.5, 0.75, (), jnp.float32)
    value_weight = gaussian(splits[3], (C, C), C ** -0.5, 0.75, (), jnp.float32)
    cell_query = gaussian(splits[4], (C, CELLS), 1.0, 6.0, ((1, 64),), jnp.float32)
    quality = draw_quality(jax.random.fold_in(splits[10], 71), 0)
    sample_cell = draw_sample_cell(jax.random.fold_in(splits[10], 71), 0)
    live = draw_live(jax.random.fold_in(splits[10], 71), 0)
    neighbours = draw_neighbours(jax.random.fold_in(splits[10], 71), 0)
    hp_weight = gaussian(splits[9], (C, NB * C), (NB * C) ** -0.5, 0.25, (), jnp.float32)
    return dict(swath=swath, enc_weight=enc_weight, key_weight=key_weight, value_weight=value_weight, cell_query=cell_query, quality=quality, sample_cell=sample_cell, live=live, neighbours=neighbours, hp_weight=hp_weight)


floor_value = -1e+30
highest = lax.Precision.HIGHEST

def reference(swath, enc_weight, key_weight, value_weight, cell_query, quality, sample_cell, live, neighbours, hp_weight):
    inv_root = 1.0 / math.sqrt(C)
    slots = jnp.arange(SAMPLES, dtype=jnp.int32)
    position = slots % SAMPLES_DEV
    range_of = slots // SAMPLES_DEV
    range_first = (range_of * CELL_DEV).astype(jnp.int32)
    run_peak = jnp.full((CELLS,), floor_value, dtype=jnp.float32)
    run_total = jnp.zeros((CELLS,), dtype=jnp.float32)
    run_sum = jnp.zeros((C, CELLS), dtype=jnp.float32)
    for sensor_index in range(SENSORS):
        signal = swath[sensor_index]
        padded = jnp.pad(signal, ((0, 0), (2, 0)))
        stacked = jnp.concatenate([padded[:, 0:SAMPLES], padded[:, 1:SAMPLES + 1], padded[:, 2:SAMPLES + 2]], axis=0)
        encoded = jax.nn.gelu(jnp.dot(enc_weight[sensor_index], stacked, precision=highest), approximate=False)
        key_rows = jnp.dot(key_weight, encoded, precision=highest)
        value_rows = jnp.dot(value_weight, encoded, precision=highest)
        cell_ids = (sample_cell[sensor_index] + range_first).astype(jnp.int32)
        query_rows = jnp.take(cell_query, cell_ids, axis=1)
        score = lax.optimization_barrier(jnp.sum(query_rows * key_rows, axis=0)) * inv_root + quality[sensor_index]
        valid = position < live[sensor_index][range_of]
        peak = jnp.maximum(jax.ops.segment_max(jnp.where(valid, score, -jnp.inf), cell_ids, CELLS), floor_value)
        weights_exp = jnp.where(valid, jnp.exp(score - peak[cell_ids]), 0.0)
        total = jax.ops.segment_sum(weights_exp, cell_ids, CELLS)
        summed = jax.ops.segment_sum((value_rows * weights_exp[None, :]).T, cell_ids, CELLS).T
        joint = jnp.maximum(run_peak, peak)
        old_factor = jnp.exp(run_peak - joint)
        new_factor = jnp.exp(peak - joint)
        run_total = run_total * old_factor + total * new_factor
        run_sum = run_sum * old_factor[None, :] + summed * new_factor[None, :]
        run_peak = joint
    prior_key = jnp.dot(key_weight, cell_query, precision=highest)
    prior_value = jnp.dot(value_weight, cell_query, precision=highest)
    prior_score = lax.optimization_barrier(jnp.sum(cell_query * prior_key, axis=0)) * inv_root
    joint = jnp.maximum(run_peak, prior_score)
    pool_factor = jnp.exp(run_peak - joint)
    prior_factor = jnp.exp(prior_score - joint)
    pooled = (run_sum * pool_factor[None, :] + prior_value * prior_factor[None, :]) / (run_total * pool_factor + prior_factor)[None, :]
    hp_cube = hp_weight.reshape(C, NB, C)
    joined = jnp.dot(hp_cube[:, 0, :], pooled, precision=highest)
    for slot_index in range(NB - 1):
        joined = joined + jnp.dot(hp_cube[:, slot_index + 1, :], jnp.take(pooled, neighbours[slot_index], axis=1), precision=highest)
    return joined
```

```python
import jax
import jax.numpy as jnp
from jax import lax
from jax.experimental import pallas as pl
from jax.experimental.pallas import tpu as pltpu
from jax.sharding import PartitionSpec as P

MESH = pl.DeviceIdType.MESH
FLOOR = -1e30
HIGHEST = lax.Precision.HIGHEST
OFFSETS = ((1, 2), (0, 2), (1, 1), (1, 3), (0, 1), (0, 3), (1, 0))


def dot(a, b, dims=((1,), (0,)), precision=HIGHEST):
    return lax.dot_general(
        a, b, (dims, ((), ())), precision=precision, preferred_element_type=jnp.float32
    )


def lanes(values, index):
    return jnp.take_along_axis(values, index, axis=1, mode="promise_in_bounds")


def split3(x):
    high = x.astype(jnp.bfloat16)
    rest = x - high.astype(jnp.float32)
    mid = rest.astype(jnp.bfloat16)
    low = (rest - mid.astype(jnp.float32)).astype(jnp.bfloat16)
    return jnp.concatenate([high, mid, low], axis=0)


def gelu(x):
    return 0.5 * x * (1.0 + lax.erf(x * 0.7071067811865476))


def kernel(
    swath_ref,
    enc_ref,
    key_ref,
    value_ref,
    query_ref,
    quality_ref,
    cell_ref,
    live_ref,
    near_ref,
    hp_ref,
    out_ref,
    x_s,
    enc_s,
    key_s,
    value_s,
    query_s,
    quality_s,
    cell_s,
    live_s,
    near_s,
    hp_s,
    tail_s,
    send_s,
    part_s,
    pool_s,
    prev_s,
    next_s,
    in_sem,
    tail_sem,
    part_out,
    part_in,
    pool_out,
    pool_in,
    up_out,
    up_in,
    down_out,
    down_in,
):
    s = lax.axis_index("sensor")
    c = lax.axis_index("cell")
    z, x = s // 4, s % 4
    up, down = (c + 1) % 64, (c + 63) % 64

    def partner(dz, dx):
        return ((z + dz) % 2) * 4 + (x + dx) % 4

    loads = [
        pltpu.make_async_copy(source, target, in_sem.at[i])
        for i, (source, target) in enumerate(
            (
                (cell_ref, cell_s),
                (query_ref, query_s),
                (key_ref, key_s),
                (enc_ref.at[0], enc_s),
                (swath_ref.at[0], x_s),
                (quality_ref, quality_s),
                (live_ref, live_s),
                (hp_ref.at[pl.ds(pl.multiple_of(s * 8, 8), 8)], hp_s),
                (value_ref, value_s),
                (near_ref, near_s),
            )
        )
    ]
    for load in loads:
        load.start()

    barrier = pltpu.get_barrier_semaphore()
    for target in (up, down):
        pl.semaphore_signal(barrier, inc=1, device_id=(s, target), device_id_type=MESH)
    for dz, dx in OFFSETS:
        pl.semaphore_signal(
            barrier, inc=1, device_id=(partner(dz, dx), c), device_id_type=MESH
        )
    pl.semaphore_wait(barrier, 9)

    tail = pltpu.make_async_remote_copy(
        src_ref=swath_ref.at[0, :, pl.ds(384, 128)],
        dst_ref=tail_s,
        send_sem=tail_sem.at[0],
        recv_sem=tail_sem.at[1],
        device_id=(s, up),
        device_id_type=MESH,
    )
    tail.start()

    for i in range(3):
        loads[i].wait()
    query = query_s[...]
    bilinear = dot(key_s[...], query, ((0,), (0,))) * 0.125
    prior = jnp.sum(query * bilinear, axis=0, keepdims=True)
    cell = cell_s[...]
    asked = []
    for b in range(4):
        index = jnp.broadcast_to(cell[:, b * 128 : (b + 1) * 128], (64, 128))
        asked.append(
            jnp.where(
                index >= 128,
                lanes(bilinear[:, 128:], index & 127),
                lanes(bilinear[:, :128], index & 127),
            )
        )
    hot = lax.broadcasted_iota(jnp.int32, (256, 512), 0) == cell

    for i in range(3, 7):
        loads[i].wait()
    enc = enc_s[...]
    taps = jnp.concatenate([enc[:, 0:64], enc[:, 64:128], enc[:, 128:192]], axis=0)
    mixed = dot(taps, x_s[...])
    two, one, zero = mixed[0:64], mixed[64:128], mixed[128:192]
    rest = zero + pltpu.roll(one, 1, 1) + pltpu.roll(two, 2, 1)
    quality = quality_s[...]
    valid = lax.broadcasted_iota(jnp.int32, (1, 512), 1) < live_s[0, 0]

    def scored(encoded, b):
        return (
            jnp.sum(encoded * asked[b], axis=0, keepdims=True)
            + quality[:, b * 128 : (b + 1) * 128]
        )

    encoded = [None] + [gelu(rest[:, b * 128 : (b + 1) * 128]) for b in range(1, 4)]
    score = [None] + [scored(encoded[b], b) for b in range(1, 4)]

    for i in range(7, 10):
        loads[i].wait()
    hp = hp_s[...]
    stacked = jnp.concatenate([hp[:, k * 64 : (k + 1) * 64] for k in range(9)], axis=0)
    stencil = dot(stacked, value_s[...])
    near = near_s[...] - c * 256
    near_edge = ((near >> 4) & 15) + jnp.where(near < 0, 16, 0)
    near_side = (near < 0) | (near >= 256)

    tail.wait_recv()
    lane = lax.broadcasted_iota(jnp.int32, (64, 128), 1)
    before = dot(taps[0:128], jnp.where(c > 0, tail_s[...], 0.0))
    first = (
        zero[:, :128]
        + pltpu.roll(jnp.where(lane == 127, before[64:128], one[:, :128]), 1, 1)
        + pltpu.roll(jnp.where(lane >= 126, before[0:64], two[:, :128]), 2, 1)
    )
    encoded[0] = gelu(first)
    score[0] = scored(encoded[0], 0)

    encoded = jnp.concatenate(encoded, axis=1)
    score = jnp.concatenate(score, axis=1)
    peak = jnp.max(
        jnp.where(hot, jnp.where(valid, score, FLOOR), FLOOR), axis=1, keepdims=True
    )
    own_peak = jnp.max(jnp.where(hot, peak, FLOOR), axis=0, keepdims=True)
    weight = jnp.where(valid, jnp.exp(score - own_peak), 0.0)
    weighted = jnp.concatenate(
        [encoded * weight, jnp.broadcast_to(weight, (8, 512))], axis=0
    )
    sums = dot(
        split3(weighted),
        jnp.where(hot, 1.0, 0.0).astype(jnp.bfloat16),
        ((1,), (1,)),
        None,
    )
    sums = sums[0:72] + (sums[72:144] + sums[144:216])
    eye = lax.broadcasted_iota(jnp.int32, (256, 256), 0) == lax.broadcasted_iota(
        jnp.int32, (256, 256), 1
    )
    peak_row = jnp.max(jnp.where(eye, peak, FLOOR), axis=0, keepdims=True)
    extra = jnp.concatenate([peak_row, sums[64:65]], axis=0)
    for k in range(8):
        send_s[k, 0:8] = sums[k * 8 : (k + 1) * 8]
        send_s[k, 8:10] = extra

    parts = []
    for dz, dx in OFFSETS:
        slot = dz * 4 + dx
        copy = pltpu.make_async_remote_copy(
            src_ref=send_s.at[partner(dz, dx)],
            dst_ref=part_s.at[slot],
            send_sem=part_out.at[slot],
            recv_sem=part_in.at[slot],
            device_id=(partner(dz, dx), c),
            device_id_type=MESH,
        )
        copy.start()
        parts.append(copy)
    own = send_s[s]
    for copy in parts:
        copy.wait_recv()
    blocks = [own] + [part_s[k] for k in range(1, 8)]
    peaks = jnp.concatenate([block[8:9] for block in blocks], axis=0)
    totals = jnp.concatenate([block[9:10] for block in blocks], axis=0)
    joint = jnp.maximum(jnp.max(peaks, axis=0, keepdims=True), prior)
    factor = jnp.exp(peaks - joint)
    prior_factor = jnp.exp(prior - joint)
    below = jnp.sum(totals * factor, axis=0, keepdims=True) + prior_factor
    above = query_s[pl.ds(pl.multiple_of(s * 8, 8), 8), :] * prior_factor
    for k in range(8):
        above = above + blocks[k][0:8] * factor[k : k + 1]
    pooled = above / below
    edge = lax.broadcasted_iota(jnp.int32, (8, 128), 1)
    edge_cell = (edge & 15) * 16 + jnp.where((edge & 16) > 0, 15, 0)
    pool_s[s, :, 0:256] = pooled
    pool_s[s, :, 256:384] = jnp.where(
        edge_cell >= 128,
        lanes(pooled[:, 128:], edge_cell & 127),
        lanes(pooled[:, :128], edge_cell & 127),
    )

    ups, downs, pools = [], [], []
    for dz, dx in OFFSETS + ((0, 0),):
        slot = dz * 4 + dx
        to = partner(dz, dx)
        for cell_to, target, out, into, kept in (
            (up, prev_s, up_out, up_in, ups),
            (down, next_s, down_out, down_in, downs),
        ):
            copy = pltpu.make_async_remote_copy(
                src_ref=pool_s.at[s, :, pl.ds(256, 128)],
                dst_ref=target.at[s],
                send_sem=out.at[slot],
                recv_sem=into.at[slot],
                device_id=(to, cell_to),
                device_id_type=MESH,
            )
            copy.start()
            kept.append(copy)
        if slot:
            copy = pltpu.make_async_remote_copy(
                src_ref=pool_s.at[s, :, pl.ds(0, 256)],
                dst_ref=pool_s.at[s, :, pl.ds(0, 256)],
                send_sem=pool_out.at[slot],
                recv_sem=pool_in.at[slot],
                device_id=(to, c),
                device_id_type=MESH,
            )
            copy.start()
            pools.append(copy)
    for copy in pools:
        copy.wait_recv()
    inner = dot(stencil, pool_s[:, :, 0:256].reshape(64, 256))
    joined = inner[0:8]
    picked = []
    for k in range(8):
        index = jnp.broadcast_to(near[k : k + 1], (8, 256))
        row = inner[8 + k * 8 : 16 + k * 8]
        halves = []
        for h in range(2):
            part = index[:, h * 128 : (h + 1) * 128]
            halves.append(
                jnp.where(
                    (part & 128) > 0,
                    lanes(row[:, 128:], part & 127),
                    lanes(row[:, :128], part & 127),
                )
            )
        picked.append(halves)
    for copy in ups + downs:
        copy.wait_recv()
    sides = jnp.where(
        lane < 16, next_s[...].reshape(64, 128), prev_s[...].reshape(64, 128)
    )
    outer = dot(stencil[8:72], sides)
    for h in range(2):
        total = joined[:, h * 128 : (h + 1) * 128]
        for k in range(8):
            cut = slice(h * 128, (h + 1) * 128)
            index = jnp.broadcast_to(near_edge[k : k + 1, cut], (8, 128))
            side = jnp.broadcast_to(near_side[k : k + 1, cut], (8, 128))
            total = total + jnp.where(
                side, lanes(outer[k * 8 : (k + 1) * 8], index), picked[k][h]
            )
        out_ref[:, h * 128 : (h + 1) * 128] = total

    tail.wait_send()
    for copy in parts + pools + ups + downs:
        copy.wait_send()


def on_device(*operands):
    f32, i32 = jnp.float32, jnp.int32
    dma = pltpu.SemaphoreType.DMA
    return pl.pallas_call(
        kernel,
        out_shape=jax.ShapeDtypeStruct((8, 256), f32),
        in_specs=[pl.BlockSpec(memory_space=pltpu.HBM)] * 10,
        out_specs=pl.BlockSpec(memory_space=pltpu.VMEM),
        scratch_shapes=[
            pltpu.VMEM((64, 512), f32),
            pltpu.VMEM((64, 192), f32),
            pltpu.VMEM((64, 64), f32),
            pltpu.VMEM((64, 64), f32),
            pltpu.VMEM((64, 256), f32),
            pltpu.VMEM((1, 512), f32),
            pltpu.VMEM((1, 512), i32),
            pltpu.SMEM((1, 1), i32),
            pltpu.VMEM((8, 256), i32),
            pltpu.VMEM((8, 576), f32),
            pltpu.VMEM((64, 128), f32),
            pltpu.VMEM((8, 10, 256), f32),
            pltpu.VMEM((8, 10, 256), f32),
            pltpu.VMEM((8, 8, 384), f32),
            pltpu.VMEM((8, 8, 128), f32),
            pltpu.VMEM((8, 8, 128), f32),
            dma((10,)),
            dma((2,)),
        ]
        + [dma((8,))] * 8,
        compiler_params=pltpu.CompilerParams(collective_id=0, has_side_effects=True),
    )(*operands)


def solution(mesh):
    in_specs = (
        P("sensor", None, "cell"),
        P("sensor", None, None),
        P(),
        P(),
        P(None, "cell"),
        P("sensor", "cell"),
        P("sensor", "cell"),
        P("sensor", "cell"),
        P(None, "cell"),
        P(),
    )
    return jax.shard_map(
        on_device,
        mesh=mesh,
        in_specs=in_specs,
        out_specs=P("sensor", "cell"),
        check_vma=False,
    )
```

```python
import jax
import jax.numpy as jnp
from jax import lax
from jax.experimental import pallas as pl
from jax.experimental.pallas import tpu as pltpu
from jax.sharding import PartitionSpec as P

MESH = pl.DeviceIdType.MESH
FLOOR = -1e30
HIGHEST = lax.Precision.HIGHEST
OFFSETS = ((1, 2), (0, 2), (1, 1), (1, 3), (0, 1), (0, 3), (1, 0))


def dot(a, b, dims=((1,), (0,)), precision=HIGHEST):
    return lax.dot_general(
        a, b, (dims, ((), ())), precision=precision, preferred_element_type=jnp.float32
    )


def lanes(values, index):
    return jnp.take_along_axis(values, index, axis=1, mode="promise_in_bounds")


def split3(x):
    high = x.astype(jnp.bfloat16)
    rest = x - high.astype(jnp.float32)
    mid = rest.astype(jnp.bfloat16)
    low = (rest - mid.astype(jnp.float32)).astype(jnp.bfloat16)
    return jnp.concatenate([high, mid, low], axis=0)


def gelu(x):
    return 0.5 * x * (1.0 + lax.erf(x * 0.7071067811865476))


def kernel(
    swath_ref,
    enc_ref,
    key_ref,
    value_ref,
    query_ref,
    quality_ref,
    cell_ref,
    live_ref,
    near_ref,
    hp_ref,
    out_ref,
    x_s,
    enc_s,
    key_s,
    value_s,
    query_s,
    quality_s,
    cell_s,
    near_s,
    hp_s,
    tail_s,
    send_s,
    part_s,
    pool_s,
    prev_s,
    next_s,
    in_sem,
    tail_sem,
    part_out,
    part_in,
    pool_out,
    pool_in,
    up_out,
    up_in,
    down_out,
    down_in,
):
    s = lax.axis_index("sensor")
    c = lax.axis_index("cell")
    z, x = s // 4, s % 4
    up, down = c + 1, c - 1
    has_up, has_down = c < 63, c > 0

    def partner(dz, dx):
        return ((z + dz) % 2) * 4 + (x + dx) % 4

    loads = [
        pltpu.make_async_copy(source, target, in_sem.at[i])
        for i, (source, target) in enumerate(
            (
                (cell_ref, cell_s),
                (query_ref, query_s),
                (key_ref, key_s),
                (enc_ref.at[0], enc_s),
                (swath_ref.at[0], x_s),
                (quality_ref, quality_s),
                (hp_ref.at[pl.ds(pl.multiple_of(s * 8, 8), 8)], hp_s),
                (value_ref, value_s),
                (near_ref, near_s),
            )
        )
    ]
    for load in loads:
        load.start()

    barrier = pltpu.get_barrier_semaphore()
    for target, there in ((up, has_up), (down, has_down)):

        @pl.when(there)
        def _():
            pl.semaphore_signal(
                barrier, inc=1, device_id=(s, target), device_id_type=MESH
            )

    for dz, dx in OFFSETS:
        pl.semaphore_signal(
            barrier, inc=1, device_id=(partner(dz, dx), c), device_id_type=MESH
        )
    pl.semaphore_wait(
        barrier, 7 + has_up.astype(jnp.int32) + has_down.astype(jnp.int32)
    )

    tail = pltpu.make_async_remote_copy(
        src_ref=swath_ref.at[0, :, pl.ds(384, 128)],
        dst_ref=tail_s,
        send_sem=tail_sem.at[0],
        recv_sem=tail_sem.at[1],
        device_id=(s, up),
        device_id_type=MESH,
    )

    @pl.when(has_up)
    def _():
        tail.start()

    @pl.when(jnp.logical_not(has_down))
    def _():
        tail_s[...] = jnp.zeros((64, 128), jnp.float32)
        prev_s[...] = jnp.zeros((8, 8, 128), jnp.float32)

    @pl.when(jnp.logical_not(has_up))
    def _():
        next_s[...] = jnp.zeros((8, 8, 128), jnp.float32)

    for i in range(3):
        loads[i].wait()
    query = query_s[...]
    bilinear = dot(key_s[...], query, ((0,), (0,))) * 0.125
    prior = jnp.sum(query * bilinear, axis=0, keepdims=True)
    cell = cell_s[...]
    asked = []
    for b in range(4):
        index = jnp.broadcast_to(cell[:, b * 128 : (b + 1) * 128], (64, 128))
        asked.append(
            jnp.where(
                index >= 128,
                lanes(bilinear[:, 128:], index & 127),
                lanes(bilinear[:, :128], index & 127),
            )
        )
    hot = lax.broadcasted_iota(jnp.int32, (256, 512), 0) == cell

    for i in range(3, 6):
        loads[i].wait()
    enc = enc_s[...]
    taps = jnp.concatenate([enc[:, 0:64], enc[:, 64:128], enc[:, 128:192]], axis=0)
    mixed = dot(taps, x_s[...])
    two, one, zero = mixed[0:64], mixed[64:128], mixed[128:192]
    rest = zero + pltpu.roll(one, 1, 1) + pltpu.roll(two, 2, 1)
    quality = quality_s[...]
    valid = lax.broadcasted_iota(jnp.int32, (1, 512), 1) < live_ref[0, 0]

    def scored(encoded, b):
        return (
            jnp.sum(encoded * asked[b], axis=0, keepdims=True)
            + quality[:, b * 128 : (b + 1) * 128]
        )

    encoded = [None] + [gelu(rest[:, b * 128 : (b + 1) * 128]) for b in range(1, 4)]
    score = [None] + [scored(encoded[b], b) for b in range(1, 4)]

    for i in range(6, 9):
        loads[i].wait()
    hp = hp_s[...]
    stacked = jnp.concatenate([hp[:, k * 64 : (k + 1) * 64] for k in range(9)], axis=0)
    stencil = dot(stacked, value_s[...])
    near = near_s[...] - c * 256
    near_edge = ((near >> 4) & 15) + jnp.where(near < 0, 16, 0)
    near_side = (near < 0) | (near >= 256)

    @pl.when(has_down)
    def _():
        tail.wait_recv()

    lane = lax.broadcasted_iota(jnp.int32, (64, 128), 1)
    before = dot(taps[0:128], tail_s[...])
    first = (
        zero[:, :128]
        + pltpu.roll(jnp.where(lane == 127, before[64:128], one[:, :128]), 1, 1)
        + pltpu.roll(jnp.where(lane >= 126, before[0:64], two[:, :128]), 2, 1)
    )
    encoded[0] = gelu(first)
    score[0] = scored(encoded[0], 0)

    encoded = jnp.concatenate(encoded, axis=1)
    score = jnp.concatenate(score, axis=1)
    peak = jnp.max(
        jnp.where(hot, jnp.where(valid, score, FLOOR), FLOOR), axis=1, keepdims=True
    )
    own_peak = jnp.max(jnp.where(hot, peak, FLOOR), axis=0, keepdims=True)
    weight = jnp.where(valid, jnp.exp(score - own_peak), 0.0)
    weighted = jnp.concatenate(
        [encoded * weight, jnp.broadcast_to(weight, (8, 512))], axis=0
    )
    sums = dot(
        split3(weighted),
        jnp.where(hot, 1.0, 0.0).astype(jnp.bfloat16),
        ((1,), (1,)),
        None,
    )
    sums = sums[0:72] + (sums[72:144] + sums[144:216])
    eye = lax.broadcasted_iota(jnp.int32, (256, 256), 0) == lax.broadcasted_iota(
        jnp.int32, (256, 256), 1
    )
    peak_row = jnp.max(jnp.where(eye, peak, FLOOR), axis=0, keepdims=True)
    extra = jnp.concatenate([peak_row, sums[64:65]], axis=0)
    for k in range(8):
        send_s[k, 0:8] = sums[k * 8 : (k + 1) * 8]
        send_s[k, 8:10] = extra

    parts = []
    for dz, dx in OFFSETS:
        slot = dz * 4 + dx
        copy = pltpu.make_async_remote_copy(
            src_ref=send_s.at[partner(dz, dx)],
            dst_ref=part_s.at[slot],
            send_sem=part_out.at[slot],
            recv_sem=part_in.at[slot],
            device_id=(partner(dz, dx), c),
            device_id_type=MESH,
        )
        copy.start()
        parts.append(copy)
    own = send_s[s]
    for copy in parts:
        copy.wait_recv()
    blocks = [own] + [part_s[k] for k in range(1, 8)]
    peaks = jnp.concatenate([block[8:9] for block in blocks], axis=0)
    totals = jnp.concatenate([block[9:10] for block in blocks], axis=0)
    joint = jnp.maximum(jnp.max(peaks, axis=0, keepdims=True), prior)
    factor = jnp.exp(peaks - joint)
    prior_factor = jnp.exp(prior - joint)
    below = jnp.sum(totals * factor, axis=0, keepdims=True) + prior_factor
    above = query_s[pl.ds(pl.multiple_of(s * 8, 8), 8), :] * prior_factor
    for k in range(8):
        above = above + blocks[k][0:8] * factor[k : k + 1]
    pooled = above / below
    edge = lax.broadcasted_iota(jnp.int32, (8, 128), 1)
    edge_cell = (edge & 15) * 16 + jnp.where((edge & 16) > 0, 15, 0)
    pool_s[s, :, 0:256] = pooled
    pool_s[s, :, 256:384] = jnp.where(
        edge_cell >= 128,
        lanes(pooled[:, 128:], edge_cell & 127),
        lanes(pooled[:, :128], edge_cell & 127),
    )

    ups, downs, pools = [], [], []
    for dz, dx in OFFSETS + ((0, 0),):
        slot = dz * 4 + dx
        to = partner(dz, dx)
        for cell_to, target, out, into, kept in (
            (up, prev_s, up_out, up_in, ups),
            (down, next_s, down_out, down_in, downs),
        ):
            kept.append(
                pltpu.make_async_remote_copy(
                    src_ref=pool_s.at[s, :, pl.ds(256, 128)],
                    dst_ref=target.at[s],
                    send_sem=out.at[slot],
                    recv_sem=into.at[slot],
                    device_id=(to, cell_to),
                    device_id_type=MESH,
                )
            )
        if slot:
            pools.append(
                pltpu.make_async_remote_copy(
                    src_ref=pool_s.at[s, :, pl.ds(0, 256)],
                    dst_ref=pool_s.at[s, :, pl.ds(0, 256)],
                    send_sem=pool_out.at[slot],
                    recv_sem=pool_in.at[slot],
                    device_id=(to, c),
                    device_id_type=MESH,
                )
            )

    @pl.when(has_up)
    def _():
        for copy in ups:
            copy.start()

    @pl.when(has_down)
    def _():
        for copy in downs:
            copy.start()

    for copy in pools:
        copy.start()
    for copy in pools:
        copy.wait_recv()
    inner = dot(stencil, pool_s[:, :, 0:256].reshape(64, 256))
    joined = inner[0:8]
    picked = []
    for k in range(8):
        index = jnp.broadcast_to(near[k : k + 1], (8, 256))
        row = inner[8 + k * 8 : 16 + k * 8]
        halves = []
        for h in range(2):
            part = index[:, h * 128 : (h + 1) * 128]
            halves.append(
                jnp.where(
                    (part & 128) > 0,
                    lanes(row[:, 128:], part & 127),
                    lanes(row[:, :128], part & 127),
                )
            )
        picked.append(halves)

    @pl.when(has_down)
    def _():
        for copy in ups:
            copy.wait_recv()

    @pl.when(has_up)
    def _():
        for copy in downs:
            copy.wait_recv()

    sides = jnp.where(
        lane < 16, next_s[...].reshape(64, 128), prev_s[...].reshape(64, 128)
    )
    outer = dot(stencil[8:72], sides)
    for h in range(2):
        total = joined[:, h * 128 : (h + 1) * 128]
        for k in range(8):
            cut = slice(h * 128, (h + 1) * 128)
            index = jnp.broadcast_to(near_edge[k : k + 1, cut], (8, 128))
            side = jnp.broadcast_to(near_side[k : k + 1, cut], (8, 128))
            total = total + jnp.where(
                side, lanes(outer[k * 8 : (k + 1) * 8], index), picked[k][h]
            )
        out_ref[:, h * 128 : (h + 1) * 128] = total

    @pl.when(has_up)
    def _():
        for copy in [tail] + ups:
            copy.wait_send()

    @pl.when(has_down)
    def _():
        for copy in downs:
            copy.wait_send()

    for copy in parts + pools:
        copy.wait_send()


def on_device(*operands):
    f32, i32 = jnp.float32, jnp.int32
    dma = pltpu.SemaphoreType.DMA
    return pl.pallas_call(
        kernel,
        out_shape=jax.ShapeDtypeStruct((8, 256), f32),
        in_specs=[
            pl.BlockSpec(memory_space=pltpu.SMEM if i == 7 else pltpu.HBM)
            for i in range(10)
        ],
        out_specs=pl.BlockSpec(memory_space=pltpu.VMEM),
        scratch_shapes=[
            pltpu.VMEM((64, 512), f32),
            pltpu.VMEM((64, 192), f32),
            pltpu.VMEM((64, 64), f32),
            pltpu.VMEM((64, 64), f32),
            pltpu.VMEM((64, 256), f32),
            pltpu.VMEM((1, 512), f32),
            pltpu.VMEM((1, 512), i32),
            pltpu.VMEM((8, 256), i32),
            pltpu.VMEM((8, 576), f32),
            pltpu.VMEM((64, 128), f32),
            pltpu.VMEM((8, 10, 256), f32),
            pltpu.VMEM((8, 10, 256), f32),
            pltpu.VMEM((8, 8, 384), f32),
            pltpu.VMEM((8, 8, 128), f32),
            pltpu.VMEM((8, 8, 128), f32),
            dma((9,)),
            dma((2,)),
        ]
        + [dma((8,))] * 8,
        compiler_params=pltpu.CompilerParams(collective_id=0, has_side_effects=True),
    )(*operands)


def solution(mesh):
    in_specs = (
        P("sensor", None, "cell"),
        P("sensor", None, None),
        P(),
        P(),
        P(None, "cell"),
        P("sensor", "cell"),
        P("sensor", "cell"),
        P("sensor", "cell"),
        P(None, "cell"),
        P(),
    )
    return jax.shard_map(
        on_device,
        mesh=mesh,
        in_specs=in_specs,
        out_specs=P("sensor", "cell"),
        check_vma=False,
    )
```

```python
import functools

import jax
import jax.numpy as jnp
from jax import lax
from jax.experimental import pallas as pl
from jax.experimental.pallas import tpu as pltpu
from jax.sharding import PartitionSpec as P

MESH = pl.DeviceIdType.MESH
FLOOR = -1e30
HIGHEST = lax.Precision.HIGHEST
OFFSETS = ((1, 2), (0, 2), (1, 1), (1, 3), (0, 1), (0, 3), (1, 0))


def dot(a, b, dims=((1,), (0,)), precision=HIGHEST):
    return lax.dot_general(
        a, b, (dims, ((), ())), precision=precision, preferred_element_type=jnp.float32
    )


def lanes(values, index):
    return jnp.take_along_axis(values, index, axis=1, mode="promise_in_bounds")


def split3(x):
    high = x.astype(jnp.bfloat16)
    rest = x - high.astype(jnp.float32)
    mid = rest.astype(jnp.bfloat16)
    return high, mid, (rest - mid.astype(jnp.float32)).astype(jnp.bfloat16)


def gelu(x):
    return 0.5 * x * (1.0 + lax.erf(x * 0.7071067811865476))


def kernel(
    swath_ref,
    enc_ref,
    key_ref,
    value_ref,
    query_ref,
    quality_ref,
    cell_ref,
    live_ref,
    near_ref,
    hp_ref,
    out_ref,
    x_s,
    enc_s,
    key_s,
    value_s,
    query_s,
    quality_s,
    cell_s,
    near_s,
    hp_s,
    tail_s,
    head_s,
    send_s,
    span_s,
    edge_s,
    part_s,
    spans_s,
    pool_s,
    prev_s,
    next_s,
    in_sem,
    tail_sem,
    part_out,
    part_in,
    span_out,
    span_in,
    pool_out,
    pool_in,
    up_out,
    up_in,
    down_out,
    down_in,
    ready,
):
    s = lax.axis_index("sensor")
    c = lax.axis_index("cell")
    z, x = s // 4, s % 4
    up, down = c + 1, c - 1
    has_up, has_down = c < 63, c > 0

    def partner(dz, dx):
        return ((z + dz) % 2) * 4 + (x + dx) % 4

    loads = [
        pltpu.make_async_copy(source, target, in_sem.at[i])
        for i, (source, target) in enumerate(
            (
                (swath_ref.at[0], x_s),
                (cell_ref, cell_s),
                (query_ref, query_s),
                (key_ref, key_s),
                (enc_ref.at[0], enc_s),
                (quality_ref, quality_s),
                (hp_ref.at[pl.ds(pl.multiple_of(s * 8, 8), 8)], hp_s),
                (value_ref, value_s),
                (near_ref, near_s),
            )
        )
    ]
    for load in loads:
        load.start()

    barrier = pltpu.get_barrier_semaphore()
    for target, there in ((up, has_up), (down, has_down)):

        @pl.when(there)
        def _():
            pl.semaphore_signal(
                barrier, inc=1, device_id=(s, target), device_id_type=MESH
            )

    for dz, dx in OFFSETS:
        pl.semaphore_signal(
            barrier, inc=1, device_id=(partner(dz, dx), c), device_id_type=MESH
        )
    loads[0].wait()
    last = jnp.transpose(x_s[:, 384:512])
    row = lax.broadcasted_iota(jnp.int32, (8, 64), 0)
    head_s[...] = jnp.where(
        lax.broadcasted_iota(jnp.int32, (8, 128), 0) < 2,
        jnp.concatenate(
            [
                jnp.where(row == 0, last[126:127], last[127:128]),
                jnp.where(row == 0, last[127:128], 0.0),
            ],
            axis=1,
        ),
        0.0,
    )
    pl.semaphore_wait(
        barrier, 7 + has_up.astype(jnp.int32) + has_down.astype(jnp.int32)
    )
    tail = pltpu.make_async_remote_copy(
        src_ref=head_s,
        dst_ref=tail_s,
        send_sem=tail_sem.at[0],
        recv_sem=tail_sem.at[1],
        device_id=(s, up),
        device_id_type=MESH,
    )

    @pl.when(has_up)
    def _():
        tail.start()

    for dz, dx in OFFSETS:
        pl.semaphore_signal(
            ready, inc=1, device_id=(partner(dz, dx), c), device_id_type=MESH
        )

    @pl.when(jnp.logical_not(has_down))
    def _():
        tail_s[...] = jnp.zeros((8, 128), jnp.float32)
        prev_s[...] = jnp.ones((8, 16, 128), jnp.float32)

    @pl.when(jnp.logical_not(has_up))
    def _():
        next_s[...] = jnp.ones((8, 16, 128), jnp.float32)

    for i in range(1, 4):
        loads[i].wait()
    query = query_s[...]
    bilinear = dot(key_s[...], query, ((0,), (0,))) * 0.125
    prior = jnp.sum(query * bilinear, axis=0, keepdims=True)
    cell = cell_s[...]
    asked = []
    for b in range(4):
        index = jnp.broadcast_to(cell[:, b * 128 : (b + 1) * 128], (64, 128))
        asked.append(
            jnp.where(
                index >= 128,
                lanes(bilinear[:, 128:], index & 127),
                lanes(bilinear[:, :128], index & 127),
            )
        )
    hot = lax.broadcasted_iota(jnp.int32, (256, 512), 0) == cell

    def edge_cell(shape):
        row = lax.broadcasted_iota(jnp.int32, shape, 0)
        return (row & 15) * 16 + jnp.where(row >= 16, 15, 0)

    edge_hot = edge_cell((32, 512)) == cell
    chosen = edge_cell((32, 256)) == lax.broadcasted_iota(jnp.int32, (32, 256), 1)
    edge_query = dot(
        jnp.where(chosen, 1.0, 0.0),
        jnp.concatenate([query, jnp.ones((64, 256), jnp.float32)], axis=0),
        ((1,), (1,)),
    )
    edge_prior = jnp.max(jnp.where(chosen, prior, FLOOR), axis=1, keepdims=True)
    edge_prior = jnp.where(s == 0, edge_prior, FLOOR)

    for i in range(4, 6):
        loads[i].wait()
    enc = enc_s[...]
    taps = jnp.concatenate([enc[:, 0:64], enc[:, 64:128], enc[:, 128:192]], axis=0)
    mixed = dot(taps, x_s[...])
    two, one, zero = mixed[0:64], mixed[64:128], mixed[128:192]
    rest = zero + pltpu.roll(one, 1, 1) + pltpu.roll(two, 2, 1)
    lane = lax.broadcasted_iota(jnp.int32, (64, 128), 1)
    early = (
        zero[:, :128]
        + jnp.where(lane < 1, 0.0, pltpu.roll(one[:, :128], 1, 1))
        + jnp.where(lane < 2, 0.0, pltpu.roll(two[:, :128], 2, 1))
    )
    quality = quality_s[...]
    valid = lax.broadcasted_iota(jnp.int32, (1, 512), 1) < live_ref[0, 0]

    def scored(encoded, b):
        return (
            jnp.sum(encoded * asked[b], axis=0, keepdims=True)
            + quality[:, b * 128 : (b + 1) * 128]
        )

    encoded = [None] + [gelu(rest[:, b * 128 : (b + 1) * 128]) for b in range(1, 4)]
    score = [None] + [scored(encoded[b], b) for b in range(1, 4)]

    for i in range(6, 9):
        loads[i].wait()
    hp = hp_s[...]
    stacked = jnp.concatenate([hp[:, k * 64 : (k + 1) * 64] for k in range(9)], axis=0)
    stencil = dot(stacked, value_s[...])
    near = near_s[...] - c * 256
    near_edge = ((near >> 4) & 15) + jnp.where(near < 0, 16, 0)
    near_side = (near < 0) | (near >= 256)

    @pl.when(has_down)
    def _():
        tail.wait_recv()

    before = dot(enc[:, 0:128], tail_s[...], ((1,), (1,)))
    first = early + jnp.concatenate([before, jnp.zeros((64, 120), jnp.float32)], axis=1)
    encoded[0] = gelu(first)
    score[0] = scored(encoded[0], 0)

    encoded = jnp.concatenate(encoded, axis=1)
    score = jnp.concatenate(score, axis=1)
    masked = jnp.where(valid, score, FLOOR)
    peak = jnp.max(jnp.where(hot, masked, FLOOR), axis=1, keepdims=True)
    own_peak = jnp.max(jnp.where(hot, peak, FLOOR), axis=0, keepdims=True)
    weight = jnp.where(valid, jnp.exp(score - own_peak), 0.0)
    thirds = split3(encoded * weight)
    weights = split3(jnp.broadcast_to(weight, (8, 512)))
    one_hot = jnp.where(hot, 1.0, 0.0).astype(jnp.bfloat16)
    turned = ((1,), (1,))
    sums = sum(dot(third, one_hot, turned, None) for third in thirds)
    total = sum(dot(third, one_hot, turned, None) for third in weights)[0:1]
    eye = lax.broadcasted_iota(jnp.int32, (256, 256), 0) == lax.broadcasted_iota(
        jnp.int32, (256, 256), 1
    )
    peak_row = jnp.max(jnp.where(eye, peak, FLOOR), axis=0, keepdims=True)
    span = jnp.concatenate([peak_row, total], axis=0)
    span_s[...] = span
    send_s[...] = sums.reshape(8, 8, 256)

    parts = []
    for dz, dx in OFFSETS:
        slot = dz * 4 + dx
        to = partner(dz, dx)
        for source, target, out, into in (
            (send_s.at[to], part_s.at[slot], part_out, part_in),
            (span_s, spans_s.at[slot], span_out, span_in),
        ):
            copy = pltpu.make_async_remote_copy(
                src_ref=source,
                dst_ref=target,
                send_sem=out.at[slot],
                recv_sem=into.at[slot],
                device_id=(to, c),
                device_id_type=MESH,
            )
            copy.start()
            parts.append(copy)

    edge_peak = jnp.max(jnp.where(edge_hot, masked, FLOOR), axis=1, keepdims=True)
    edge_one_hot = jnp.where(edge_hot, 1.0, 0.0).astype(jnp.bfloat16)
    edge_sums = sum(
        dot(edge_one_hot, jnp.concatenate([third] + [extra] * 8, axis=0), turned, None)
        for third, extra in zip(thirds, weights)
    )
    edge_joint = jnp.maximum(edge_peak, edge_prior)
    edge_s[...] = jnp.where(
        lax.broadcasted_iota(jnp.int32, (32, 128), 1) < 96,
        edge_sums * jnp.exp(edge_peak - edge_joint)
        + edge_query * jnp.exp(edge_prior - edge_joint),
        edge_joint,
    )
    ups, downs = [], []
    for dz, dx in OFFSETS + ((0, 0),):
        slot = dz * 4 + dx
        for rows, cell_to, target, out, into, kept in (
            (16, up, prev_s, up_out, up_in, ups),
            (0, down, next_s, down_out, down_in, downs),
        ):
            kept.append(
                pltpu.make_async_remote_copy(
                    src_ref=edge_s.at[pl.ds(rows, 16)],
                    dst_ref=target.at[slot],
                    send_sem=out.at[slot],
                    recv_sem=into.at[slot],
                    device_id=(partner(dz, dx), cell_to),
                    device_id_type=MESH,
                )
            )

    pl.semaphore_wait(ready, 7)

    @pl.when(has_up)
    def _():
        for copy in ups:
            copy.start()

    @pl.when(has_down)
    def _():
        for copy in downs:
            copy.start()

    own = send_s[s]
    for copy in parts:
        copy.wait_recv()
    blocks = [own] + [part_s[k] for k in range(1, 8)]
    spans = [span] + [spans_s[k] for k in range(1, 8)]
    peaks = jnp.concatenate([one[0:1] for one in spans], axis=0)
    totals = jnp.concatenate([one[1:2] for one in spans], axis=0)
    joint = jnp.maximum(jnp.max(peaks, axis=0, keepdims=True), prior)
    factor = jnp.exp(peaks - joint)
    prior_factor = jnp.exp(prior - joint)
    below = jnp.sum(totals * factor, axis=0, keepdims=True) + prior_factor
    above = query_s[pl.ds(pl.multiple_of(s * 8, 8), 8), :] * prior_factor
    for k in range(8):
        above = above + blocks[k] * factor[k : k + 1]
    pool_s[s] = above / below

    pools = []
    for dz, dx in OFFSETS:
        slot = dz * 4 + dx
        copy = pltpu.make_async_remote_copy(
            src_ref=pool_s.at[s],
            dst_ref=pool_s.at[s],
            send_sem=pool_out.at[slot],
            recv_sem=pool_in.at[slot],
            device_id=(partner(dz, dx), c),
            device_id_type=MESH,
        )
        copy.start()
        pools.append(copy)

    @pl.when(has_down)
    def _():
        for copy in ups:
            copy.wait_recv()

    @pl.when(has_up)
    def _():
        for copy in downs:
            copy.wait_recv()

    edges = []
    for side in (next_s, prev_s):
        blocks = [side[k] for k in range(8)]
        joint = functools.reduce(jnp.maximum, blocks)[:, 96:97]
        whole = sum(block * jnp.exp(block[:, 96:97] - joint) for block in blocks)
        edges.append(whole[:, 0:64] / whole[:, 64:65])
    edges = jnp.concatenate(edges + [jnp.zeros((96, 64), jnp.float32)], axis=0)
    outer = dot(stencil[8:72], edges, turned)

    for copy in pools:
        copy.wait_recv()
    inner = dot(stencil, pool_s[...].reshape(64, 256))
    joined = inner[0:8]
    picked = []
    for k in range(8):
        index = jnp.broadcast_to(near[k : k + 1], (8, 256))
        row = inner[8 + k * 8 : 16 + k * 8]
        halves = []
        for h in range(2):
            part = index[:, h * 128 : (h + 1) * 128]
            halves.append(
                jnp.where(
                    (part & 128) > 0,
                    lanes(row[:, 128:], part & 127),
                    lanes(row[:, :128], part & 127),
                )
            )
        picked.append(halves)

    for h in range(2):
        total = joined[:, h * 128 : (h + 1) * 128]
        for k in range(8):
            cut = slice(h * 128, (h + 1) * 128)
            index = jnp.broadcast_to(near_edge[k : k + 1, cut], (8, 128))
            side = jnp.broadcast_to(near_side[k : k + 1, cut], (8, 128))
            total = total + jnp.where(
                side, lanes(outer[k * 8 : (k + 1) * 8], index), picked[k][h]
            )
        out_ref[:, h * 128 : (h + 1) * 128] = total

    @pl.when(has_up)
    def _():
        for copy in [tail] + ups:
            copy.wait_send()

    @pl.when(has_down)
    def _():
        for copy in downs:
            copy.wait_send()

    for copy in parts + pools:
        copy.wait_send()


def on_device(*operands):
    f32, i32 = jnp.float32, jnp.int32
    dma = pltpu.SemaphoreType.DMA
    return pl.pallas_call(
        kernel,
        out_shape=jax.ShapeDtypeStruct((8, 256), f32),
        in_specs=[
            pl.BlockSpec(memory_space=pltpu.SMEM if i == 7 else pltpu.HBM)
            for i in range(10)
        ],
        out_specs=pl.BlockSpec(memory_space=pltpu.VMEM),
        scratch_shapes=[
            pltpu.VMEM((64, 512), f32),
            pltpu.VMEM((64, 192), f32),
            pltpu.VMEM((64, 64), f32),
            pltpu.VMEM((64, 64), f32),
            pltpu.VMEM((64, 256), f32),
            pltpu.VMEM((1, 512), f32),
            pltpu.VMEM((1, 512), i32),
            pltpu.VMEM((8, 256), i32),
            pltpu.VMEM((8, 576), f32),
            pltpu.VMEM((8, 128), f32),
            pltpu.VMEM((8, 128), f32),
            pltpu.VMEM((8, 8, 256), f32),
            pltpu.VMEM((2, 256), f32),
            pltpu.VMEM((32, 128), f32),
            pltpu.VMEM((8, 8, 256), f32),
            pltpu.VMEM((8, 2, 256), f32),
            pltpu.VMEM((8, 8, 256), f32),
            pltpu.VMEM((8, 16, 128), f32),
            pltpu.VMEM((8, 16, 128), f32),
            dma((9,)),
            dma((2,)),
        ]
        + [dma((8,))] * 10
        + [pltpu.SemaphoreType.REGULAR],
        compiler_params=pltpu.CompilerParams(collective_id=0, has_side_effects=True),
    )(*operands)


def solution(mesh):
    in_specs = (
        P("sensor", None, "cell"),
        P("sensor", None, None),
        P(),
        P(),
        P(None, "cell"),
        P("sensor", "cell"),
        P("sensor", "cell"),
        P("sensor", "cell"),
        P(None, "cell"),
        P(),
    )
    return jax.shard_map(
        on_device,
        mesh=mesh,
        in_specs=in_specs,
        out_specs=P("sensor", "cell"),
        check_vma=False,
    )
```

```python
import functools

import jax
import jax.numpy as jnp
from jax import lax
from jax.experimental import pallas as pl
from jax.experimental.pallas import tpu as pltpu
from jax.sharding import PartitionSpec as P

MESH = pl.DeviceIdType.MESH
FLOOR = -1e30
HIGH, HIGHEST = lax.Precision.HIGH, lax.Precision.HIGHEST
OFFSETS = ((1, 2), (0, 2), (1, 1), (1, 3), (0, 1), (0, 3), (1, 0))


def dot(a, b, dims=((1,), (0,)), precision=HIGHEST):
    return lax.dot_general(
        a, b, (dims, ((), ())), precision=precision, preferred_element_type=jnp.float32
    )


def lanes(values, index):
    return jnp.take_along_axis(values, index, axis=1, mode="promise_in_bounds")


def gelu(x):
    return 0.5 * x * (1.0 + lax.erf(x * 0.7071067811865476))


def kernel(
    swath_ref,
    enc_ref,
    key_ref,
    value_ref,
    query_ref,
    quality_ref,
    cell_ref,
    live_ref,
    near_ref,
    hp_ref,
    out_ref,
    x_s,
    enc_s,
    key_s,
    value_s,
    query_s,
    quality_s,
    cell_s,
    near_s,
    hp_s,
    mixed_s,
    tail_s,
    head_s,
    send_s,
    span_s,
    edge_s,
    part_s,
    spans_s,
    pool_s,
    prev_s,
    next_s,
    in_sem,
    tail_sem,
    part_out,
    part_in,
    span_out,
    span_in,
    pool_out,
    pool_in,
    up_out,
    up_in,
    down_out,
    down_in,
    ready,
):
    s = lax.axis_index("sensor")
    c = lax.axis_index("cell")
    z, x = s // 4, s % 4
    up, down = c + 1, c - 1
    has_up, has_down = c < 63, c > 0

    def partner(dz, dx):
        return ((z + dz) % 2) * 4 + (x + dx) % 4

    loads = [
        pltpu.make_async_copy(source, target, in_sem.at[i])
        for i, (source, target) in enumerate(
            (
                (swath_ref.at[0], x_s),
                (cell_ref, cell_s),
                (query_ref, query_s),
                (key_ref, key_s),
                (enc_ref.at[0], enc_s),
                (quality_ref, quality_s),
                (hp_ref.at[pl.ds(pl.multiple_of(s * 8, 8), 8)], hp_s),
                (value_ref, value_s),
                (near_ref, near_s),
            )
        )
    ]
    for load in loads:
        load.start()

    barrier = pltpu.get_barrier_semaphore()
    for target, there in ((up, has_up), (down, has_down)):

        @pl.when(there)
        def _():
            pl.semaphore_signal(
                barrier, inc=1, device_id=(s, target), device_id_type=MESH
            )

    for dz, dx in OFFSETS:
        pl.semaphore_signal(
            barrier, inc=1, device_id=(partner(dz, dx), c), device_id_type=MESH
        )
    for i in range(6):
        loads[i].wait()
    last = jnp.transpose(x_s[:, 384:512])
    row = lax.broadcasted_iota(jnp.int32, (8, 64), 0)
    head_s[...] = jnp.where(
        lax.broadcasted_iota(jnp.int32, (8, 128), 0) < 2,
        jnp.concatenate(
            [
                jnp.where(row == 0, last[126:127], last[127:128]),
                jnp.where(row == 0, last[127:128], 0.0),
            ],
            axis=1,
        ),
        0.0,
    )

    query = query_s[...]
    bilinear = dot(key_s[...], query, ((0,), (0,))) * 0.125
    enc = enc_s[...]
    taps = jnp.concatenate([enc[:, 0:64], enc[:, 64:128], enc[:, 128:192]], axis=0)
    mixed = dot(taps, x_s[...])
    mixed_s[...] = mixed

    pl.semaphore_wait(
        barrier, 7 + has_up.astype(jnp.int32) + has_down.astype(jnp.int32)
    )
    tail = pltpu.make_async_remote_copy(
        src_ref=head_s,
        dst_ref=tail_s,
        send_sem=tail_sem.at[0],
        recv_sem=tail_sem.at[1],
        device_id=(s, up),
        device_id_type=MESH,
    )

    @pl.when(has_up)
    def _():
        tail.start()

    for dz, dx in OFFSETS:
        pl.semaphore_signal(
            ready, inc=1, device_id=(partner(dz, dx), c), device_id_type=MESH
        )

    @pl.when(jnp.logical_not(has_down))
    def _():
        tail_s[...] = jnp.zeros((8, 128), jnp.float32)
        prev_s[...] = jnp.ones((8, 16, 128), jnp.float32)

    @pl.when(jnp.logical_not(has_up))
    def _():
        next_s[...] = jnp.ones((8, 16, 128), jnp.float32)

    mixed = mixed_s[...]
    two, one, zero = mixed[0:64], mixed[64:128], mixed[128:192]
    slot = lax.broadcasted_iota(jnp.int32, (1, 512), 1)
    drawn = (
        zero
        + jnp.where(slot < 1, 0.0, pltpu.roll(one, 1, 1))
        + jnp.where(slot < 2, 0.0, pltpu.roll(two, 2, 1))
    )
    encoded = gelu(drawn)
    cell = cell_s[...]
    asked = []
    for b in range(4):
        index = jnp.broadcast_to(cell[:, b * 128 : (b + 1) * 128], (64, 128))
        asked.append(
            jnp.where(
                index >= 128,
                lanes(bilinear[:, 128:], index & 127),
                lanes(bilinear[:, :128], index & 127),
            )
        )
    quality = quality_s[...]
    live = live_ref[0, 0]
    score = jnp.sum(encoded * jnp.concatenate(asked, axis=1), axis=0, keepdims=True)
    score = score + quality
    valid = (slot < live) & (slot >= 2)

    hot = lax.broadcasted_iota(jnp.int32, (256, 512), 0) == cell
    masked = jnp.where(valid, score, FLOOR)
    peak = jnp.max(jnp.where(hot, masked, FLOOR), axis=1, keepdims=True)
    slot_peak = jnp.max(jnp.where(hot, peak, FLOOR), axis=0, keepdims=True)
    weight = jnp.where(valid, jnp.exp(score - slot_peak), 0.0)
    weighted = jnp.concatenate(
        [encoded * weight, jnp.broadcast_to(weight, (8, 512))], axis=0
    )
    one_hot = jnp.where(hot, 1.0, 0.0).astype(jnp.bfloat16)
    turned = ((1,), (1,))
    high = weighted.astype(jnp.bfloat16)
    low = (weighted - high.astype(jnp.float32)).astype(jnp.bfloat16)
    sums = dot(high, one_hot, turned, None) + dot(low, one_hot, turned, None)
    eye = lax.broadcasted_iota(jnp.int32, (256, 256), 0) == lax.broadcasted_iota(
        jnp.int32, (256, 256), 1
    )
    peak = jnp.max(jnp.where(eye, peak, FLOOR), axis=0, keepdims=True)
    prior = jnp.sum(query * bilinear, axis=0, keepdims=True)
    prior = jnp.where(s == 0, prior, FLOOR)
    joint = jnp.maximum(peak, prior)
    factor = jnp.exp(peak - joint)
    prior_factor = jnp.exp(prior - joint)
    total = sums[64:65] * factor + prior_factor
    sums = sums[0:64] * factor + query * prior_factor
    peak = joint

    @pl.when(has_down)
    def _():
        tail.wait_recv()

    before = dot(enc[:, 0:128], tail_s[...], turned)
    first = gelu(
        drawn[:, 0:128]
        + jnp.concatenate([before, jnp.zeros((64, 120), jnp.float32)], axis=1)
    )
    first_score = jnp.sum(first * asked[0], axis=0, keepdims=True) + quality[:, 0:128]
    cells = lax.broadcasted_iota(jnp.int32, (1, 256), 1)
    scores = [
        jnp.where(
            (cells == cell[:, t : t + 1]) & (t < live), first_score[:, t : t + 1], FLOOR
        )
        for t in range(2)
    ]
    joint = jnp.maximum(peak, jnp.maximum(scores[0], scores[1]))
    factor = jnp.exp(peak - joint)
    total, sums = total * factor, sums * factor
    for t in range(2):
        weight = jnp.where(
            (cells == cell[:, t : t + 1]) & (t < live), jnp.exp(scores[t] - joint), 0.0
        )
        total = total + weight
        sums = sums + first[:, t : t + 1] * weight
    span = jnp.concatenate([joint, total], axis=0)
    span_s[...] = span
    send_s[...] = sums.reshape(8, 8, 256)

    parts = []
    for dz, dx in OFFSETS:
        slot = dz * 4 + dx
        to = partner(dz, dx)
        for source, target, out, into in (
            (send_s.at[to], part_s.at[slot], part_out, part_in),
            (span_s, spans_s.at[slot], span_out, span_in),
        ):
            copy = pltpu.make_async_remote_copy(
                src_ref=source,
                dst_ref=target,
                send_sem=out.at[slot],
                recv_sem=into.at[slot],
                device_id=(to, c),
                device_id_type=MESH,
            )
            copy.start()
            parts.append(copy)

    row = lax.broadcasted_iota(jnp.int32, (32, 256), 0)
    chosen = lax.broadcasted_iota(jnp.int32, (32, 256), 1) == (
        (row & 15) * 16 + jnp.where(row >= 16, 15, 0)
    )
    edge_s[...] = dot(
        jnp.where(chosen, 1.0, 0.0),
        jnp.concatenate([sums, span, jnp.zeros((62, 256), jnp.float32)], axis=0),
        turned,
    )
    ups, downs = [], []
    for dz, dx in OFFSETS + ((0, 0),):
        slot = dz * 4 + dx
        for rows, cell_to, target, out, into, kept in (
            (16, up, prev_s, up_out, up_in, ups),
            (0, down, next_s, down_out, down_in, downs),
        ):
            kept.append(
                pltpu.make_async_remote_copy(
                    src_ref=edge_s.at[pl.ds(rows, 16)],
                    dst_ref=target.at[slot],
                    send_sem=out.at[slot],
                    recv_sem=into.at[slot],
                    device_id=(partner(dz, dx), cell_to),
                    device_id_type=MESH,
                )
            )
    pl.semaphore_wait(ready, 7)

    @pl.when(has_up)
    def _():
        for copy in ups:
            copy.start()

    @pl.when(has_down)
    def _():
        for copy in downs:
            copy.start()

    for i in range(6, 9):
        loads[i].wait()
    hp = hp_s[...]
    stacked = jnp.concatenate([hp[:, k * 64 : (k + 1) * 64] for k in range(9)], axis=0)
    stencil = dot(stacked, value_s[...])
    near = near_s[...] - c * 256
    near_edge = ((near >> 4) & 15) + jnp.where(near < 0, 16, 0)
    near_side = (near < 0) | (near >= 256)

    own = send_s[s]
    for copy in parts:
        copy.wait_recv()
    blocks = [own] + [part_s[k] for k in range(1, 8)]
    spans = [span] + [spans_s[k] for k in range(1, 8)]
    peaks = jnp.concatenate([one[0:1] for one in spans], axis=0)
    totals = jnp.concatenate([one[1:2] for one in spans], axis=0)
    factor = jnp.exp(peaks - jnp.max(peaks, axis=0, keepdims=True))
    below = jnp.sum(totals * factor, axis=0, keepdims=True)
    above = sum(blocks[k] * factor[k : k + 1] for k in range(8))
    pool_s[s] = above / below

    pools = []
    for dz, dx in OFFSETS:
        slot = dz * 4 + dx
        copy = pltpu.make_async_remote_copy(
            src_ref=pool_s.at[s],
            dst_ref=pool_s.at[s],
            send_sem=pool_out.at[slot],
            recv_sem=pool_in.at[slot],
            device_id=(partner(dz, dx), c),
            device_id_type=MESH,
        )
        copy.start()
        pools.append(copy)

    @pl.when(has_down)
    def _():
        for copy in ups:
            copy.wait_recv()

    @pl.when(has_up)
    def _():
        for copy in downs:
            copy.wait_recv()

    edges = []
    for side in (next_s, prev_s):
        blocks = [side[k] for k in range(8)]
        joint = functools.reduce(jnp.maximum, blocks)[:, 64:65]
        whole = sum(block * jnp.exp(block[:, 64:65] - joint) for block in blocks)
        edges.append(whole[:, 0:64] / whole[:, 65:66])
    edges = jnp.concatenate(edges + [jnp.zeros((96, 64), jnp.float32)], axis=0)
    outer = dot(stencil[8:72], edges, turned, HIGH)

    for copy in pools:
        copy.wait_recv()
    inner = dot(stencil, pool_s[...].reshape(64, 256), precision=HIGH)
    joined = inner[0:8]
    picked = []
    for k in range(8):
        index = jnp.broadcast_to(near[k : k + 1], (8, 256))
        row = inner[8 + k * 8 : 16 + k * 8]
        halves = []
        for h in range(2):
            part = index[:, h * 128 : (h + 1) * 128]
            halves.append(
                jnp.where(
                    (part & 128) > 0,
                    lanes(row[:, 128:], part & 127),
                    lanes(row[:, :128], part & 127),
                )
            )
        picked.append(halves)

    for h in range(2):
        total = joined[:, h * 128 : (h + 1) * 128]
        for k in range(8):
            cut = slice(h * 128, (h + 1) * 128)
            index = jnp.broadcast_to(near_edge[k : k + 1, cut], (8, 128))
            side = jnp.broadcast_to(near_side[k : k + 1, cut], (8, 128))
            total = total + jnp.where(
                side, lanes(outer[k * 8 : (k + 1) * 8], index), picked[k][h]
            )
        out_ref[:, h * 128 : (h + 1) * 128] = total

    @pl.when(has_up)
    def _():
        for copy in [tail] + ups:
            copy.wait_send()

    @pl.when(has_down)
    def _():
        for copy in downs:
            copy.wait_send()

    for copy in parts + pools:
        copy.wait_send()


def on_device(*operands):
    f32, i32 = jnp.float32, jnp.int32
    dma = pltpu.SemaphoreType.DMA
    return pl.pallas_call(
        kernel,
        out_shape=jax.ShapeDtypeStruct((8, 256), f32),
        in_specs=[
            pl.BlockSpec(memory_space=pltpu.SMEM if i == 7 else pltpu.HBM)
            for i in range(10)
        ],
        out_specs=pl.BlockSpec(memory_space=pltpu.VMEM),
        scratch_shapes=[
            pltpu.VMEM((64, 512), f32),
            pltpu.VMEM((64, 192), f32),
            pltpu.VMEM((64, 64), f32),
            pltpu.VMEM((64, 64), f32),
            pltpu.VMEM((64, 256), f32),
            pltpu.VMEM((1, 512), f32),
            pltpu.VMEM((1, 512), i32),
            pltpu.VMEM((8, 256), i32),
            pltpu.VMEM((8, 576), f32),
            pltpu.VMEM((192, 512), f32),
            pltpu.VMEM((8, 128), f32),
            pltpu.VMEM((8, 128), f32),
            pltpu.VMEM((8, 8, 256), f32),
            pltpu.VMEM((2, 256), f32),
            pltpu.VMEM((32, 128), f32),
            pltpu.VMEM((8, 8, 256), f32),
            pltpu.VMEM((8, 2, 256), f32),
            pltpu.VMEM((8, 8, 256), f32),
            pltpu.VMEM((8, 16, 128), f32),
            pltpu.VMEM((8, 16, 128), f32),
            dma((9,)),
            dma((2,)),
        ]
        + [dma((8,))] * 10
        + [pltpu.SemaphoreType.REGULAR],
        compiler_params=pltpu.CompilerParams(collective_id=0, has_side_effects=True),
    )(*operands)


def solution(mesh):
    in_specs = (
        P("sensor", None, "cell"),
        P("sensor", None, None),
        P(),
        P(),
        P(None, "cell"),
        P("sensor", "cell"),
        P("sensor", "cell"),
        P("sensor", "cell"),
        P(None, "cell"),
        P(),
    )
    return jax.shard_map(
        on_device,
        mesh=mesh,
        in_specs=in_specs,
        out_specs=P("sensor", "cell"),
        check_vma=False,
    )
```

```python
import functools

import jax
import jax.numpy as jnp
from jax import lax
from jax.experimental import pallas as pl
from jax.experimental.pallas import tpu as pltpu
from jax.sharding import PartitionSpec as P

MESH = pl.DeviceIdType.MESH
FLOOR = -1e30
HIGH, HIGHEST = lax.Precision.HIGH, lax.Precision.HIGHEST
OFFSETS = ((1, 2), (0, 2), (1, 1), (1, 3), (0, 1), (0, 3), (1, 0))


def dot(a, b, dims=((1,), (0,)), precision=HIGHEST):
    return lax.dot_general(
        a, b, (dims, ((), ())), precision=precision, preferred_element_type=jnp.float32
    )


def lanes(values, index):
    return jnp.take_along_axis(values, index, axis=1, mode="promise_in_bounds")


def split3(x):
    high = x.astype(jnp.bfloat16).astype(jnp.float32)
    mid = (x - high).astype(jnp.bfloat16).astype(jnp.float32)
    return high, mid, x - high - mid


def full_dot(a, b):
    a0, a1, a2 = split3(a)
    b0, b1, b2 = split3(b)
    left = jnp.concatenate([a0, a0, a1, a1, a0, a2], axis=1).astype(jnp.bfloat16)
    right = jnp.concatenate([b0, b1, b0, b1, b2, b0], axis=0).astype(jnp.bfloat16)
    return dot(left, right, precision=None)


def gelu(x):
    return 0.5 * x * (1.0 + lax.erf(x * 0.7071067811865476))


def kernel(
    swath_ref,
    enc_ref,
    key_ref,
    value_ref,
    query_ref,
    quality_ref,
    cell_ref,
    live_ref,
    near_ref,
    hp_ref,
    out_ref,
    x_s,
    enc_s,
    key_s,
    value_s,
    query_s,
    quality_s,
    cell_s,
    near_s,
    hp_s,
    mixed_s,
    hot_s,
    asked_s,
    prior_s,
    tail_s,
    head_s,
    send_s,
    span_s,
    edge_s,
    part_s,
    spans_s,
    pool_s,
    prev_s,
    next_s,
    in_sem,
    tail_sem,
    part_out,
    part_in,
    span_out,
    span_in,
    pool_out,
    pool_in,
    up_out,
    up_in,
    down_out,
    down_in,
    ready,
):
    s = lax.axis_index("sensor")
    c = lax.axis_index("cell")
    z, x = s // 4, s % 4
    up, down = c + 1, c - 1
    has_up, has_down = c < 63, c > 0

    def partner(dz, dx):
        return ((z + dz) % 2) * 4 + (x + dx) % 4

    loads = [
        pltpu.make_async_copy(source, target, in_sem.at[i])
        for i, (source, target) in enumerate(
            (
                (swath_ref.at[0], x_s),
                (cell_ref, cell_s),
                (query_ref, query_s),
                (key_ref, key_s),
                (enc_ref.at[0], enc_s),
                (quality_ref, quality_s),
                (hp_ref.at[pl.ds(pl.multiple_of(s * 8, 8), 8)], hp_s),
                (value_ref, value_s),
                (near_ref, near_s),
            )
        )
    ]
    for load in loads:
        load.start()

    barrier = pltpu.get_barrier_semaphore()
    for target, there in ((up, has_up), (down, has_down)):

        @pl.when(there)
        def _():
            pl.semaphore_signal(
                barrier, inc=1, device_id=(s, target), device_id_type=MESH
            )

    for dz, dx in OFFSETS:
        pl.semaphore_signal(
            barrier, inc=1, device_id=(partner(dz, dx), c), device_id_type=MESH
        )
    for i in range(6):
        loads[i].wait()
    last = jnp.transpose(x_s[:, 384:512])
    row = lax.broadcasted_iota(jnp.int32, (8, 64), 0)
    head_s[...] = jnp.where(
        lax.broadcasted_iota(jnp.int32, (8, 128), 0) < 2,
        jnp.concatenate(
            [
                jnp.where(row == 0, last[126:127], last[127:128]),
                jnp.where(row == 0, last[127:128], 0.0),
            ],
            axis=1,
        ),
        0.0,
    )

    query = query_s[...]
    bilinear = full_dot(jnp.transpose(key_s[...]) * 0.125, query)
    cell = cell_s[...]
    hot_s[...] = jnp.where(
        lax.broadcasted_iota(jnp.int32, (256, 512), 0) == cell, 1.0, 0.0
    ).astype(jnp.bfloat16)
    enc = enc_s[...]
    taps = jnp.concatenate([enc[:, 0:64], enc[:, 64:128], enc[:, 128:192]], axis=0)
    mixed_s[...] = full_dot(taps, x_s[...])
    for b in range(4):
        index = jnp.broadcast_to(cell[:, b * 128 : (b + 1) * 128], (64, 128))
        asked_s[:, b * 128 : (b + 1) * 128] = jnp.where(
            index >= 128,
            lanes(bilinear[:, 128:], index & 127),
            lanes(bilinear[:, :128], index & 127),
        )
    prior_s[...] = jnp.sum(query * bilinear, axis=0, keepdims=True)

    pl.semaphore_wait(
        barrier, 7 + has_up.astype(jnp.int32) + has_down.astype(jnp.int32)
    )
    tail = pltpu.make_async_remote_copy(
        src_ref=head_s,
        dst_ref=tail_s,
        send_sem=tail_sem.at[0],
        recv_sem=tail_sem.at[1],
        device_id=(s, up),
        device_id_type=MESH,
    )

    @pl.when(has_up)
    def _():
        tail.start()

    for dz, dx in OFFSETS:
        pl.semaphore_signal(
            ready, inc=1, device_id=(partner(dz, dx), c), device_id_type=MESH
        )

    @pl.when(jnp.logical_not(has_down))
    def _():
        tail_s[...] = jnp.zeros((8, 128), jnp.float32)
        prev_s[...] = jnp.ones((8, 16, 128), jnp.float32)

    @pl.when(jnp.logical_not(has_up))
    def _():
        next_s[...] = jnp.ones((8, 16, 128), jnp.float32)

    mixed = mixed_s[...]
    two, one, zero = mixed[0:64], mixed[64:128], mixed[128:192]
    slot = lax.broadcasted_iota(jnp.int32, (1, 512), 1)
    drawn = (
        zero
        + jnp.where(slot < 1, 0.0, pltpu.roll(one, 1, 1))
        + jnp.where(slot < 2, 0.0, pltpu.roll(two, 2, 1))
    )
    encoded = gelu(drawn)
    cell = cell_s[...]
    quality = quality_s[...]
    live = live_ref[0, 0]
    score = jnp.sum(encoded * asked_s[...], axis=0, keepdims=True)
    score = score + quality
    valid = (slot < live) & (slot >= 2)

    hot = lax.broadcasted_iota(jnp.int32, (256, 512), 0) == cell
    masked = jnp.where(valid, score, FLOOR)
    peak = jnp.max(jnp.where(hot, masked, FLOOR), axis=1, keepdims=True)
    eye = lax.broadcasted_iota(jnp.int32, (128, 128), 0) == lax.broadcasted_iota(
        jnp.int32, (128, 128), 1
    )
    halves = [
        jnp.max(
            jnp.where(eye, peak[h * 128 : (h + 1) * 128], FLOOR), axis=0, keepdims=True
        )
        for h in range(2)
    ]
    slot_peak = []
    for b in range(4):
        index = jnp.broadcast_to(cell[:, b * 128 : (b + 1) * 128], (8, 128))
        low, high = (lanes(jnp.broadcast_to(half, (8, 128)), index & 127) for half in halves)
        slot_peak.append(jnp.where(index >= 128, high, low)[0:1])
    slot_peak = jnp.concatenate(slot_peak, axis=1)
    peak = jnp.concatenate(halves, axis=1)
    weight = jnp.where(valid, jnp.exp(score - slot_peak), 0.0)
    weighted = jnp.concatenate(
        [encoded * weight, jnp.broadcast_to(weight, (8, 512))], axis=0
    )
    one_hot = hot_s[...]
    turned = ((1,), (1,))
    high = weighted.astype(jnp.bfloat16)
    low = (weighted - high.astype(jnp.float32)).astype(jnp.bfloat16)
    sums = dot(high, one_hot, turned, None) + dot(low, one_hot, turned, None)
    query = query_s[...]
    prior = prior_s[...]
    prior = jnp.where(s == 0, prior, FLOOR)
    joint = jnp.maximum(peak, prior)
    factor = jnp.exp(peak - joint)
    prior_factor = jnp.exp(prior - joint)
    total = sums[64:65] * factor + prior_factor
    sums = sums[0:64] * factor + query * prior_factor
    peak = joint

    @pl.when(has_down)
    def _():
        tail.wait_recv()

    parity = (lax.broadcasted_iota(jnp.int32, (64, 128), 1) & 1) == 0
    late = [
        jnp.sum(enc_s[:, 0:128] * tail_s[t : t + 1], axis=1, keepdims=True)
        + drawn[:, t : t + 1]
        for t in range(2)
    ]
    late = gelu(jnp.where(parity, late[0], late[1]))
    late_score = jnp.sum(
        late * jnp.where(parity, asked_s[:, 0:1], asked_s[:, 1:2]), axis=0, keepdims=True
    )
    cells = lax.broadcasted_iota(jnp.int32, (1, 256), 1)
    there = [(cells == cell[:, t : t + 1]) & (t < live) for t in range(2)]
    scores = [
        jnp.where(there[t], late_score[:, t : t + 1] + quality[:, t : t + 1], FLOOR)
        for t in range(2)
    ]
    joint = jnp.maximum(peak, jnp.maximum(scores[0], scores[1]))
    factor = jnp.exp(peak - joint)
    total, sums = total * factor, sums * factor
    for t in range(2):
        weight = jnp.where(there[t], jnp.exp(scores[t] - joint), 0.0)
        total = total + weight
        sums = sums + late[:, t : t + 1] * weight
    span = jnp.concatenate([joint, total], axis=0)
    span_s[...] = span
    send_s[...] = sums.reshape(8, 8, 256)

    parts = []
    for dz, dx in OFFSETS:
        slot = dz * 4 + dx
        to = partner(dz, dx)
        for source, target, out, into in (
            (send_s.at[to], part_s.at[slot], part_out, part_in),
            (span_s, spans_s.at[slot], span_out, span_in),
        ):
            copy = pltpu.make_async_remote_copy(
                src_ref=source,
                dst_ref=target,
                send_sem=out.at[slot],
                recv_sem=into.at[slot],
                device_id=(to, c),
                device_id_type=MESH,
            )
            copy.start()
            parts.append(copy)

    row = lax.broadcasted_iota(jnp.int32, (32, 256), 0)
    chosen = lax.broadcasted_iota(jnp.int32, (32, 256), 1) == (
        (row & 15) * 16 + jnp.where(row >= 16, 15, 0)
    )
    edge_s[...] = dot(
        jnp.where(chosen, 1.0, 0.0),
        jnp.concatenate([sums, span, jnp.zeros((62, 256), jnp.float32)], axis=0),
        turned,
    )
    ups, downs = [], []
    for dz, dx in OFFSETS + ((0, 0),):
        slot = dz * 4 + dx
        for rows, cell_to, target, out, into, kept in (
            (16, up, prev_s, up_out, up_in, ups),
            (0, down, next_s, down_out, down_in, downs),
        ):
            kept.append(
                pltpu.make_async_remote_copy(
                    src_ref=edge_s.at[pl.ds(rows, 16)],
                    dst_ref=target.at[slot],
                    send_sem=out.at[slot],
                    recv_sem=into.at[slot],
                    device_id=(partner(dz, dx), cell_to),
                    device_id_type=MESH,
                )
            )
    pl.semaphore_wait(ready, 7)

    @pl.when(has_up)
    def _():
        for copy in ups:
            copy.start()

    @pl.when(has_down)
    def _():
        for copy in downs:
            copy.start()

    for i in range(6, 9):
        loads[i].wait()
    hp = hp_s[...]
    stacked = jnp.concatenate([hp[:, k * 64 : (k + 1) * 64] for k in range(9)], axis=0)
    stencil = dot(stacked, value_s[...])
    part0, part1, _ = split3(stencil)
    stencil_parts = jnp.concatenate([part0, part1, part0], axis=1).astype(jnp.bfloat16)
    near = near_s[...] - c * 256
    near_edge = ((near >> 4) & 15) + jnp.where(near < 0, 16, 0)
    near_side = (near < 0) | (near >= 256)

    own = send_s[s]
    for copy in parts:
        copy.wait_recv()
    blocks = [own] + [part_s[k] for k in range(1, 8)]
    spans = [span] + [spans_s[k] for k in range(1, 8)]
    peaks = jnp.concatenate([one[0:1] for one in spans], axis=0)
    totals = jnp.concatenate([one[1:2] for one in spans], axis=0)
    factor = jnp.exp(peaks - jnp.max(peaks, axis=0, keepdims=True))
    below = jnp.sum(totals * factor, axis=0, keepdims=True)
    above = sum(blocks[k] * factor[k : k + 1] for k in range(8))
    pool_s[s] = above / below

    pools = []
    for dz, dx in OFFSETS:
        slot = dz * 4 + dx
        copy = pltpu.make_async_remote_copy(
            src_ref=pool_s.at[s],
            dst_ref=pool_s.at[s],
            send_sem=pool_out.at[slot],
            recv_sem=pool_in.at[slot],
            device_id=(partner(dz, dx), c),
            device_id_type=MESH,
        )
        copy.start()
        pools.append(copy)

    @pl.when(has_down)
    def _():
        for copy in ups:
            copy.wait_recv()

    @pl.when(has_up)
    def _():
        for copy in downs:
            copy.wait_recv()

    edges = []
    for side in (next_s, prev_s):
        blocks = [side[k] for k in range(8)]
        joint = functools.reduce(jnp.maximum, blocks)[:, 64:65]
        whole = sum(block * jnp.exp(block[:, 64:65] - joint) for block in blocks)
        edges.append(whole[:, 0:64] / whole[:, 65:66])
    edges = jnp.concatenate(edges + [jnp.zeros((96, 64), jnp.float32)], axis=0)
    outer = dot(stencil[8:72], edges, turned, HIGH)

    for copy in pools:
        copy.wait_recv()
    part0, part1, _ = split3(pool_s[...].reshape(64, 256))
    inner = dot(
        stencil_parts,
        jnp.concatenate([part0, part0, part1], axis=0).astype(jnp.bfloat16),
        precision=None,
    )
    joined = inner[0:8]
    picked = []
    for k in range(8):
        index = jnp.broadcast_to(near[k : k + 1], (8, 256))
        row = inner[8 + k * 8 : 16 + k * 8]
        halves = []
        for h in range(2):
            part = index[:, h * 128 : (h + 1) * 128]
            halves.append(
                jnp.where(
                    (part & 128) > 0,
                    lanes(row[:, 128:], part & 127),
                    lanes(row[:, :128], part & 127),
                )
            )
        picked.append(halves)

    for h in range(2):
        total = joined[:, h * 128 : (h + 1) * 128]
        for k in range(8):
            cut = slice(h * 128, (h + 1) * 128)
            index = jnp.broadcast_to(near_edge[k : k + 1, cut], (8, 128))
            side = jnp.broadcast_to(near_side[k : k + 1, cut], (8, 128))
            total = total + jnp.where(
                side, lanes(outer[k * 8 : (k + 1) * 8], index), picked[k][h]
            )
        out_ref[:, h * 128 : (h + 1) * 128] = total

    @pl.when(has_up)
    def _():
        for copy in [tail] + ups:
            copy.wait_send()

    @pl.when(has_down)
    def _():
        for copy in downs:
            copy.wait_send()

    for copy in parts + pools:
        copy.wait_send()


def on_device(*operands):
    f32, i32 = jnp.float32, jnp.int32
    dma = pltpu.SemaphoreType.DMA
    return pl.pallas_call(
        kernel,
        out_shape=pltpu.VMEM((8, 256), f32),
        in_specs=[
            pl.BlockSpec(memory_space=pltpu.SMEM if i == 7 else pltpu.HBM)
            for i in range(10)
        ],
        out_specs=pl.BlockSpec(memory_space=pltpu.VMEM),
        scratch_shapes=[
            pltpu.VMEM((64, 512), f32),
            pltpu.VMEM((64, 192), f32),
            pltpu.VMEM((64, 64), f32),
            pltpu.VMEM((64, 64), f32),
            pltpu.VMEM((64, 256), f32),
            pltpu.VMEM((1, 512), f32),
            pltpu.VMEM((1, 512), i32),
            pltpu.VMEM((8, 256), i32),
            pltpu.VMEM((8, 576), f32),
            pltpu.VMEM((192, 512), f32),
            pltpu.VMEM((256, 512), jnp.bfloat16),
            pltpu.VMEM((64, 512), f32),
            pltpu.VMEM((1, 256), f32),
            pltpu.VMEM((8, 128), f32),
            pltpu.VMEM((8, 128), f32),
            pltpu.VMEM((8, 8, 256), f32),
            pltpu.VMEM((2, 256), f32),
            pltpu.VMEM((32, 128), f32),
            pltpu.VMEM((8, 8, 256), f32),
            pltpu.VMEM((8, 2, 256), f32),
            pltpu.VMEM((8, 8, 256), f32),
            pltpu.VMEM((8, 16, 128), f32),
            pltpu.VMEM((8, 16, 128), f32),
            dma((9,)),
            dma((2,)),
        ]
        + [dma((8,))] * 10
        + [pltpu.SemaphoreType.REGULAR],
        compiler_params=pltpu.CompilerParams(collective_id=0, has_side_effects=True),
    )(*operands)


def solution(mesh):
    in_specs = (
        P("sensor", None, "cell"),
        P("sensor", None, None),
        P(),
        P(),
        P(None, "cell"),
        P("sensor", "cell"),
        P("sensor", "cell"),
        P("sensor", "cell"),
        P(None, "cell"),
        P(),
    )
    return jax.shard_map(
        on_device,
        mesh=mesh,
        in_specs=in_specs,
        out_specs=P("sensor", "cell"),
        check_vma=False,
    )
```

```python
import functools

import jax
import jax.numpy as jnp
from jax import lax
from jax.experimental import pallas as pl
from jax.experimental.pallas import tpu as pltpu
from jax.sharding import PartitionSpec as P

MESH = pl.DeviceIdType.MESH
FLOOR = -1e30
HIGH, HIGHEST = lax.Precision.HIGH, lax.Precision.HIGHEST
OFFSETS = ((1, 2), (0, 2), (1, 1), (1, 3), (0, 1), (0, 3), (1, 0))


def dot(a, b, dims=((1,), (0,)), precision=HIGHEST):
    return lax.dot_general(
        a, b, (dims, ((), ())), precision=precision, preferred_element_type=jnp.float32
    )


def lanes(values, index):
    return jnp.take_along_axis(values, index, axis=1, mode="promise_in_bounds")


def split3(x):
    high = x.astype(jnp.bfloat16).astype(jnp.float32)
    mid = (x - high).astype(jnp.bfloat16).astype(jnp.float32)
    return high, mid, x - high - mid


def full_dot(a, b):
    a0, a1, a2 = split3(a)
    b0, b1, b2 = split3(b)
    left = jnp.concatenate([a0, a0, a1, a1, a0, a2], axis=1).astype(jnp.bfloat16)
    right = jnp.concatenate([b0, b1, b0, b1, b2, b0], axis=0).astype(jnp.bfloat16)
    return dot(left, right, precision=None)


def gelu(x):
    return 0.5 * x * (1.0 + lax.erf(x * 0.7071067811865476))


def kernel(
    swath_ref,
    enc_ref,
    key_ref,
    value_ref,
    query_ref,
    quality_ref,
    cell_ref,
    live_ref,
    near_ref,
    hp_ref,
    out_ref,
    x_s,
    enc_s,
    key_s,
    value_s,
    query_s,
    quality_s,
    cell_s,
    near_s,
    hp_s,
    mixed_s,
    hot_s,
    asked_s,
    prior_s,
    tail_s,
    head_s,
    send_s,
    span_s,
    edge_s,
    early_s,
    pack_s,
    packed_s,
    token_s,
    tokens_s,
    side_s,
    part_s,
    spans_s,
    pool_s,
    prev_s,
    next_s,
    in_sem,
    tail_sem,
    part_out,
    part_in,
    span_out,
    span_in,
    pool_out,
    pool_in,
    up_out,
    up_in,
    down_out,
    down_in,
    packet_sem,
    token_out,
    token_in,
    ready,
):
    s = lax.axis_index("sensor")
    c = lax.axis_index("cell")
    z, x = s // 4, s % 4
    up, down = c + 1, c - 1
    has_up, has_down = c < 63, c > 0
    far_up, far_down = has_up & (c % 16 == 15), has_down & (c % 16 == 0)

    def partner(dz, dx):
        return ((z + dz) % 2) * 4 + (x + dx) % 4

    loads = [
        pltpu.make_async_copy(source, target, in_sem.at[i])
        for i, (source, target) in enumerate(
            (
                (swath_ref.at[0], x_s),
                (cell_ref, cell_s),
                (query_ref, query_s),
                (key_ref, key_s),
                (enc_ref.at[0], enc_s),
                (quality_ref, quality_s),
                (hp_ref.at[pl.ds(pl.multiple_of(s * 8, 8), 8)], hp_s),
                (value_ref, value_s),
                (near_ref, near_s),
            )
        )
    ]
    for load in loads:
        load.start()

    barrier = pltpu.get_barrier_semaphore()
    for target, there in ((up, has_up), (down, has_down)):

        @pl.when(there)
        def _():
            pl.semaphore_signal(
                barrier, inc=1, device_id=(s, target), device_id_type=MESH
            )

    for dz, dx in OFFSETS:
        pl.semaphore_signal(
            barrier, inc=1, device_id=(partner(dz, dx), c), device_id_type=MESH
        )
    for i in range(6):
        loads[i].wait()
    last = jnp.transpose(x_s[:, 384:512])
    row = lax.broadcasted_iota(jnp.int32, (8, 64), 0)
    head_s[...] = jnp.where(
        lax.broadcasted_iota(jnp.int32, (8, 128), 0) < 2,
        jnp.concatenate(
            [
                jnp.where(row == 0, last[126:127], last[127:128]),
                jnp.where(row == 0, last[127:128], 0.0),
            ],
            axis=1,
        ),
        0.0,
    )

    query = query_s[...]
    bilinear = full_dot(jnp.transpose(key_s[...]) * 0.125, query)
    cell = cell_s[...]
    hot_s[...] = jnp.where(
        lax.broadcasted_iota(jnp.int32, (256, 512), 0) == cell, 1.0, 0.0
    ).astype(jnp.bfloat16)
    enc = enc_s[...]
    taps = jnp.concatenate([enc[:, 0:64], enc[:, 64:128], enc[:, 128:192]], axis=0)
    mixed_s[...] = full_dot(taps, x_s[...])
    for b in range(4):
        index = jnp.broadcast_to(cell[:, b * 128 : (b + 1) * 128], (64, 128))
        asked_s[:, b * 128 : (b + 1) * 128] = jnp.where(
            index >= 128,
            lanes(bilinear[:, 128:], index & 127),
            lanes(bilinear[:, :128], index & 127),
        )
    prior_s[...] = jnp.sum(query * bilinear, axis=0, keepdims=True)

    pl.semaphore_wait(
        barrier, 7 + has_up.astype(jnp.int32) + has_down.astype(jnp.int32)
    )
    tail = pltpu.make_async_remote_copy(
        src_ref=head_s,
        dst_ref=tail_s,
        send_sem=tail_sem.at[0],
        recv_sem=tail_sem.at[1],
        device_id=(s, up),
        device_id_type=MESH,
    )

    @pl.when(has_up)
    def _():
        tail.start()

    for dz, dx in OFFSETS:
        pl.semaphore_signal(
            ready, inc=1, device_id=(partner(dz, dx), c), device_id_type=MESH
        )

    @pl.when(jnp.logical_not(has_down))
    def _():
        tail_s[...] = jnp.zeros((8, 128), jnp.float32)
        prev_s[...] = jnp.ones((8, 16, 128), jnp.float32)

    @pl.when(jnp.logical_not(has_up))
    def _():
        next_s[...] = jnp.ones((8, 16, 128), jnp.float32)

    mixed = mixed_s[...]
    two, one, zero = mixed[0:64], mixed[64:128], mixed[128:192]
    slot = lax.broadcasted_iota(jnp.int32, (1, 512), 1)
    drawn = (
        zero
        + jnp.where(slot < 1, 0.0, pltpu.roll(one, 1, 1))
        + jnp.where(slot < 2, 0.0, pltpu.roll(two, 2, 1))
    )
    cell = cell_s[...]
    quality = quality_s[...]
    live = live_ref[0, 0]
    packet = pltpu.make_async_remote_copy(
        src_ref=pack_s,
        dst_ref=packed_s,
        send_sem=packet_sem.at[0],
        recv_sem=packet_sem.at[1],
        device_id=(s, down),
        device_id_type=MESH,
    )

    @pl.when(far_down)
    def _():
        lane = lax.broadcasted_iota(jnp.int32, (64, 128), 1)
        lane8 = lax.broadcasted_iota(jnp.int32, (8, 128), 1)
        row8 = lax.broadcasted_iota(jnp.int32, (8, 128), 0)
        pack_s[0:64] = jnp.where(
            lane < 2, drawn[:, 0:128], pltpu.roll(asked_s[:, 0:128], 2, 1)
        )
        pack_s[64:72] = jnp.where(
            row8 == 0,
            quality[:, 0:128],
            jnp.where(
                row8 == 1,
                cell[:, 0:128].astype(jnp.float32),
                jnp.where(lane8 < live, 1.0, 0.0),
            ),
        )
        packet.start()

    encoded = gelu(drawn)
    score = jnp.sum(encoded * asked_s[...], axis=0, keepdims=True)
    score = score + quality
    valid = (slot < live) & (slot >= 2)

    hot = lax.broadcasted_iota(jnp.int32, (256, 512), 0) == cell
    masked = jnp.where(valid, score, FLOOR)
    peak = jnp.max(jnp.where(hot, masked, FLOOR), axis=1, keepdims=True)
    eye = lax.broadcasted_iota(jnp.int32, (128, 128), 0) == lax.broadcasted_iota(
        jnp.int32, (128, 128), 1
    )
    halves = [
        jnp.max(
            jnp.where(eye, peak[h * 128 : (h + 1) * 128], FLOOR), axis=0, keepdims=True
        )
        for h in range(2)
    ]
    slot_peak = []
    for b in range(4):
        index = jnp.broadcast_to(cell[:, b * 128 : (b + 1) * 128], (8, 128))
        low, high = (lanes(jnp.broadcast_to(half, (8, 128)), index & 127) for half in halves)
        slot_peak.append(jnp.where(index >= 128, high, low)[0:1])
    slot_peak = jnp.concatenate(slot_peak, axis=1)
    peak = jnp.concatenate(halves, axis=1)
    weight = jnp.where(valid, jnp.exp(score - slot_peak), 0.0)
    weighted = jnp.concatenate(
        [encoded * weight, jnp.broadcast_to(weight, (8, 512))], axis=0
    )
    one_hot = hot_s[...]
    turned = ((1,), (1,))
    high = weighted.astype(jnp.bfloat16)
    low = (weighted - high.astype(jnp.float32)).astype(jnp.bfloat16)
    sums = dot(high, one_hot, turned, None) + dot(low, one_hot, turned, None)
    query = query_s[...]
    prior = prior_s[...]
    prior = jnp.where(s == 0, prior, FLOOR)
    joint = jnp.maximum(peak, prior)
    factor = jnp.exp(peak - joint)
    prior_factor = jnp.exp(prior - joint)
    total = sums[64:65] * factor + prior_factor
    sums = sums[0:64] * factor + query * prior_factor
    peak = joint

    row = lax.broadcasted_iota(jnp.int32, (32, 256), 0)
    chosen = lax.broadcasted_iota(jnp.int32, (32, 256), 1) == (
        (row & 15) * 16 + jnp.where(row >= 16, 15, 0)
    )
    chosen = jnp.where(chosen, 1.0, 0.0)
    chosen = jnp.concatenate([chosen] * 3, axis=1).astype(jnp.bfloat16)

    def edge_rows(peak, total, sums):
        rows = jnp.concatenate(
            [sums, peak, total, jnp.zeros((62, 256), jnp.float32)], axis=0
        )
        rows = jnp.concatenate(split3(rows), axis=1).astype(jnp.bfloat16)
        return dot(chosen, rows, turned, None)

    def edge_copy(source, k, cell_to, target, out, into):
        dz, dx = (OFFSETS + ((0, 0),))[k]
        slot = dz * 4 + dx
        return pltpu.make_async_remote_copy(
            src_ref=source,
            dst_ref=target.at[slot],
            send_sem=out.at[slot],
            recv_sem=into.at[slot],
            device_id=(partner(dz, dx), cell_to),
            device_id_type=MESH,
        )

    ups = [
        edge_copy(edge_s.at[pl.ds(16, 16)], k, up, prev_s, up_out, up_in)
        for k in range(8)
    ]
    downs, far_downs = (
        [edge_copy(source, k, down, next_s, down_out, down_in) for k in range(8)]
        for source in (edge_s.at[pl.ds(0, 16)], early_s)
    )

    @pl.when(far_down)
    def _():
        early_s[...] = edge_rows(peak, total, sums)[0:16]
        pl.semaphore_wait(ready, 7)
        for copy in far_downs:
            copy.start()

    @pl.when(has_down)
    def _():
        tail.wait_recv()

    parity = (lax.broadcasted_iota(jnp.int32, (64, 128), 1) & 1) == 0

    def late_tokens(rows, drawn, asked):
        made = [
            jnp.sum(enc_s[:, 0:128] * rows[t : t + 1], axis=1, keepdims=True)
            + drawn[:, t : t + 1]
            for t in range(2)
        ]
        made = gelu(jnp.where(parity, made[0], made[1]))
        asked = jnp.where(parity, asked[:, 0:1], asked[:, 1:2])
        return made, jnp.sum(made * asked, axis=0, keepdims=True)

    late, late_score = late_tokens(tail_s[...], drawn[:, 0:128], asked_s[:, 0:2])
    cells = lax.broadcasted_iota(jnp.int32, (1, 256), 1)
    there = [(cells == cell[:, t : t + 1]) & (t < live) for t in range(2)]
    scores = [
        jnp.where(there[t], late_score[:, t : t + 1] + quality[:, t : t + 1], FLOOR)
        for t in range(2)
    ]
    joint = jnp.maximum(peak, jnp.maximum(scores[0], scores[1]))
    factor = jnp.exp(peak - joint)
    total, sums = total * factor, sums * factor
    for t in range(2):
        weight = jnp.where(there[t], jnp.exp(scores[t] - joint), 0.0)
        total = total + weight
        sums = sums + late[:, t : t + 1] * weight
    span = jnp.concatenate([joint, total], axis=0)
    span_s[...] = span
    send_s[...] = sums.reshape(8, 8, 256)

    parts = []
    for dz, dx in OFFSETS:
        slot = dz * 4 + dx
        to = partner(dz, dx)
        for source, target, out, into in (
            (send_s.at[to], part_s.at[slot], part_out, part_in),
            (span_s, spans_s.at[slot], span_out, span_in),
        ):
            copy = pltpu.make_async_remote_copy(
                src_ref=source,
                dst_ref=target,
                send_sem=out.at[slot],
                recv_sem=into.at[slot],
                device_id=(to, c),
                device_id_type=MESH,
            )
            copy.start()
            parts.append(copy)

    edge_s[...] = edge_rows(joint, total, sums)

    @pl.when(jnp.logical_not(far_down))
    def _():
        pl.semaphore_wait(ready, 7)

    @pl.when(has_up)
    def _():
        for copy in ups:
            copy.start()

    @pl.when(has_down & jnp.logical_not(far_down))
    def _():
        for copy in downs:
            copy.start()

    for i in range(6, 9):
        loads[i].wait()
    hp = hp_s[...]
    stacked = jnp.concatenate([hp[:, k * 64 : (k + 1) * 64] for k in range(9)], axis=0)
    stencil = dot(stacked, value_s[...])
    part0, part1, _ = split3(stencil)
    stencil_parts = jnp.concatenate([part0, part1, part0], axis=1).astype(jnp.bfloat16)
    near = near_s[...] - c * 256
    near_edge = ((near >> 4) & 15) + jnp.where(near < 0, 16, 0)
    near_side = (near < 0) | (near >= 256)

    shared = []
    for dz, dx in OFFSETS:
        slot = dz * 4 + dx
        shared.append(
            pltpu.make_async_remote_copy(
                src_ref=token_s,
                dst_ref=tokens_s.at[slot],
                send_sem=token_out.at[slot],
                recv_sem=token_in.at[slot],
                device_id=(partner(dz, dx), c),
                device_id_type=MESH,
            )
        )

    @pl.when(far_up)
    def _():
        packet.wait_recv()
        made, made_score = late_tokens(
            head_s[...], packed_s[0:64, 0:2], packed_s[0:64, 2:4]
        )
        made_score = jnp.where(
            packed_s[66:67] > 0.0, made_score + packed_s[64:65], FLOOR
        )
        rows = jnp.transpose(made)[0:8]
        row8 = lax.broadcasted_iota(jnp.int32, (8, 64), 0)
        lane8 = lax.broadcasted_iota(jnp.int32, (8, 64), 1)
        others = [
            jnp.where(row8 == 0, one[:, 0:1], one[:, 1:2])
            for one in (made_score, packed_s[65:66])
        ]
        token_s[...] = jnp.concatenate(
            [
                rows,
                jnp.where(
                    lane8 == 0, others[0], jnp.where(lane8 == 1, 1.0, others[1])
                ),
            ],
            axis=1,
        )
        for copy in shared:
            copy.start()

    own = send_s[s]
    for copy in parts:
        copy.wait_recv()
    blocks = [own] + [part_s[k] for k in range(1, 8)]
    spans = [span] + [spans_s[k] for k in range(1, 8)]
    peaks = jnp.concatenate([one[0:1] for one in spans], axis=0)
    totals = jnp.concatenate([one[1:2] for one in spans], axis=0)
    factor = jnp.exp(peaks - jnp.max(peaks, axis=0, keepdims=True))
    below = jnp.sum(totals * factor, axis=0, keepdims=True)
    above = sum(blocks[k] * factor[k : k + 1] for k in range(8))
    pool_s[s] = above / below

    pools = []
    for dz, dx in OFFSETS:
        slot = dz * 4 + dx
        copy = pltpu.make_async_remote_copy(
            src_ref=pool_s.at[s],
            dst_ref=pool_s.at[s],
            send_sem=pool_out.at[slot],
            recv_sem=pool_in.at[slot],
            device_id=(partner(dz, dx), c),
            device_id_type=MESH,
        )
        copy.start()
        pools.append(copy)

    @pl.when(has_down)
    def _():
        for copy in ups:
            copy.wait_recv()

    @pl.when(has_up)
    def _():
        for copy in downs:
            copy.wait_recv()

    def mean(blocks):
        joint = functools.reduce(jnp.maximum, blocks)[:, 64:65]
        whole = sum(block * jnp.exp(block[:, 64:65] - joint) for block in blocks)
        return whole[:, 0:64] / whole[:, 65:66]

    below_blocks = [next_s[k] for k in range(8)]

    @pl.when(jnp.logical_not(far_up))
    def _():
        side_s[...] = mean(below_blocks)

    @pl.when(far_up)
    def _():
        for copy in shared:
            copy.wait_recv()
        first_cell = lax.broadcasted_iota(jnp.int32, (16, 128), 0).astype(jnp.float32) * 16.0
        more = []
        for tokens in [token_s[...]] + [tokens_s[k] for k in range(1, 8)]:
            for t in range(2):
                more.append(
                    jnp.where(
                        first_cell == tokens[t : t + 1, 66:67], tokens[t : t + 1], FLOOR
                    )
                )
        side_s[...] = mean(below_blocks + more)

    edges = jnp.concatenate(
        [
            side_s[...],
            mean([prev_s[k] for k in range(8)]),
            jnp.zeros((96, 64), jnp.float32),
        ],
        axis=0,
    )
    outer = dot(stencil[8:72], edges, turned, HIGH)

    for copy in pools:
        copy.wait_recv()
    part0, part1, _ = split3(pool_s[...].reshape(64, 256))
    inner = dot(
        stencil_parts,
        jnp.concatenate([part0, part0, part1], axis=0).astype(jnp.bfloat16),
        precision=None,
    )
    joined = inner[0:8]
    picked = []
    for k in range(8):
        index = jnp.broadcast_to(near[k : k + 1], (8, 256))
        row = inner[8 + k * 8 : 16 + k * 8]
        halves = []
        for h in range(2):
            part = index[:, h * 128 : (h + 1) * 128]
            halves.append(
                jnp.where(
                    (part & 128) > 0,
                    lanes(row[:, 128:], part & 127),
                    lanes(row[:, :128], part & 127),
                )
            )
        picked.append(halves)

    for h in range(2):
        total = joined[:, h * 128 : (h + 1) * 128]
        for k in range(8):
            cut = slice(h * 128, (h + 1) * 128)
            index = jnp.broadcast_to(near_edge[k : k + 1, cut], (8, 128))
            side = jnp.broadcast_to(near_side[k : k + 1, cut], (8, 128))
            total = total + jnp.where(
                side, lanes(outer[k * 8 : (k + 1) * 8], index), picked[k][h]
            )
        out_ref[:, h * 128 : (h + 1) * 128] = total

    @pl.when(has_up)
    def _():
        for copy in [tail] + ups:
            copy.wait_send()

    @pl.when(has_down)
    def _():
        for copy in downs:
            copy.wait_send()

    @pl.when(far_down)
    def _():
        packet.wait_send()

    @pl.when(far_up)
    def _():
        for copy in shared:
            copy.wait_send()

    for copy in parts + pools:
        copy.wait_send()


def on_device(*operands):
    f32, i32 = jnp.float32, jnp.int32
    dma = pltpu.SemaphoreType.DMA
    return pl.pallas_call(
        kernel,
        out_shape=pltpu.VMEM((8, 256), f32),
        in_specs=[
            pl.BlockSpec(memory_space=pltpu.SMEM if i == 7 else pltpu.HBM)
            for i in range(10)
        ],
        out_specs=pl.BlockSpec(memory_space=pltpu.VMEM),
        scratch_shapes=[
            pltpu.VMEM((64, 512), f32),
            pltpu.VMEM((64, 192), f32),
            pltpu.VMEM((64, 64), f32),
            pltpu.VMEM((64, 64), f32),
            pltpu.VMEM((64, 256), f32),
            pltpu.VMEM((1, 512), f32),
            pltpu.VMEM((1, 512), i32),
            pltpu.VMEM((8, 256), i32),
            pltpu.VMEM((8, 576), f32),
            pltpu.VMEM((192, 512), f32),
            pltpu.VMEM((256, 512), jnp.bfloat16),
            pltpu.VMEM((64, 512), f32),
            pltpu.VMEM((1, 256), f32),
            pltpu.VMEM((8, 128), f32),
            pltpu.VMEM((8, 128), f32),
            pltpu.VMEM((8, 8, 256), f32),
            pltpu.VMEM((2, 256), f32),
            pltpu.VMEM((32, 128), f32),
            pltpu.VMEM((16, 128), f32),
            pltpu.VMEM((72, 128), f32),
            pltpu.VMEM((72, 128), f32),
            pltpu.VMEM((8, 128), f32),
            pltpu.VMEM((8, 8, 128), f32),
            pltpu.VMEM((16, 64), f32),
            pltpu.VMEM((8, 8, 256), f32),
            pltpu.VMEM((8, 2, 256), f32),
            pltpu.VMEM((8, 8, 256), f32),
            pltpu.VMEM((8, 16, 128), f32),
            pltpu.VMEM((8, 16, 128), f32),
            dma((9,)),
            dma((2,)),
        ]
        + [dma((8,))] * 10
        + [dma((2,)), dma((8,)), dma((8,)), pltpu.SemaphoreType.REGULAR],
        compiler_params=pltpu.CompilerParams(collective_id=0, has_side_effects=True),
    )(*operands)


def solution(mesh):
    in_specs = (
        P("sensor", None, "cell"),
        P("sensor", None, None),
        P(),
        P(),
        P(None, "cell"),
        P("sensor", "cell"),
        P("sensor", "cell"),
        P("sensor", "cell"),
        P(None, "cell"),
        P(),
    )
    return jax.shard_map(
        on_device,
        mesh=mesh,
        in_specs=in_specs,
        out_specs=P("sensor", "cell"),
        check_vma=False,
    )
```

```python
import functools

import jax
import jax.numpy as jnp
from jax import lax
from jax.experimental import pallas as pl
from jax.experimental.pallas import tpu as pltpu
from jax.sharding import PartitionSpec as P

MESH = pl.DeviceIdType.MESH
FLOOR = -1e30
HIGH, HIGHEST = lax.Precision.HIGH, lax.Precision.HIGHEST
OFFSETS = ((1, 2), (0, 2), (1, 1), (1, 3), (0, 1), (0, 3), (1, 0))


def dot(a, b, dims=((1,), (0,)), precision=HIGHEST):
    return lax.dot_general(
        a, b, (dims, ((), ())), precision=precision, preferred_element_type=jnp.float32
    )


def lanes(values, index):
    return jnp.take_along_axis(values, index, axis=1, mode="promise_in_bounds")


def split3(x):
    high = x.astype(jnp.bfloat16).astype(jnp.float32)
    mid = (x - high).astype(jnp.bfloat16).astype(jnp.float32)
    return high, mid, x - high - mid


def full_dot(a, b):
    a0, a1, a2 = split3(a)
    b0, b1, b2 = split3(b)
    left = jnp.concatenate([a0, a0, a1, a1, a0, a2], axis=1).astype(jnp.bfloat16)
    right = jnp.concatenate([b0, b1, b0, b1, b2, b0], axis=0).astype(jnp.bfloat16)
    return dot(left, right, precision=None)


def gelu(x):
    return 0.5 * x * (1.0 + lax.erf(x * 0.7071067811865476))


def kernel(
    swath_ref,
    enc_ref,
    key_ref,
    value_ref,
    query_ref,
    quality_ref,
    cell_ref,
    live_ref,
    near_ref,
    hp_ref,
    out_ref,
    x_s,
    enc_s,
    key_s,
    value_s,
    query_s,
    quality_s,
    cell_s,
    near_s,
    hp_s,
    hot_s,
    asked_s,
    prior_s,
    tail_s,
    head_s,
    send_s,
    span_s,
    edge_s,
    early_s,
    pack_s,
    packed_s,
    token_s,
    tokens_s,
    late_s,
    lates_s,
    side_s,
    part_s,
    spans_s,
    pool_s,
    prev_s,
    next_s,
    in_sem,
    tail_sem,
    part_out,
    part_in,
    span_out,
    span_in,
    pool_out,
    pool_in,
    up_out,
    up_in,
    down_out,
    down_in,
    packet_sem,
    token_out,
    token_in,
    late_out,
    late_in,
    ready,
):
    s = lax.axis_index("sensor")
    c = lax.axis_index("cell")
    z, x = s // 4, s % 4
    up, down = c + 1, c - 1
    has_up, has_down = c < 63, c > 0
    far_up, far_down = has_up & (c % 16 == 15), has_down & (c % 16 == 0)

    def partner(dz, dx):
        return ((z + dz) % 2) * 4 + (x + dx) % 4

    loads = [
        pltpu.make_async_copy(source, target, in_sem.at[i])
        for i, (source, target) in enumerate(
            (
                (swath_ref.at[0], x_s),
                (cell_ref, cell_s),
                (query_ref, query_s),
                (key_ref, key_s),
                (enc_ref.at[0], enc_s),
                (quality_ref, quality_s),
                (hp_ref.at[pl.ds(pl.multiple_of(s * 8, 8), 8)], hp_s),
                (value_ref, value_s),
                (near_ref, near_s),
            )
        )
    ]
    for load in loads:
        load.start()

    barrier = pltpu.get_barrier_semaphore()
    for target, there in ((up, has_up), (down, has_down)):

        @pl.when(there)
        def _():
            pl.semaphore_signal(
                barrier, inc=1, device_id=(s, target), device_id_type=MESH
            )

    for dz, dx in OFFSETS:
        pl.semaphore_signal(
            barrier, inc=1, device_id=(partner(dz, dx), c), device_id_type=MESH
        )
    loads[0].wait()
    last = jnp.transpose(x_s[:, 384:512])
    row = lax.broadcasted_iota(jnp.int32, (8, 64), 0)
    head_s[...] = jnp.where(
        lax.broadcasted_iota(jnp.int32, (8, 128), 0) < 2,
        jnp.concatenate(
            [
                jnp.where(row == 0, last[126:127], last[127:128]),
                jnp.where(row == 0, last[127:128], 0.0),
            ],
            axis=1,
        ),
        0.0,
    )

    pl.semaphore_wait(
        barrier, 7 + has_up.astype(jnp.int32) + has_down.astype(jnp.int32)
    )
    tail = pltpu.make_async_remote_copy(
        src_ref=head_s,
        dst_ref=tail_s,
        send_sem=tail_sem.at[0],
        recv_sem=tail_sem.at[1],
        device_id=(s, up),
        device_id_type=MESH,
    )

    @pl.when(has_up)
    def _():
        tail.start()

    for dz, dx in OFFSETS:
        pl.semaphore_signal(
            ready, inc=1, device_id=(partner(dz, dx), c), device_id_type=MESH
        )

    @pl.when(jnp.logical_not(has_down))
    def _():
        tail_s[...] = jnp.zeros((8, 128), jnp.float32)
        prev_s[...] = jnp.ones((8, 16, 128), jnp.float32)

    @pl.when(jnp.logical_not(has_up))
    def _():
        next_s[...] = jnp.ones((8, 16, 128), jnp.float32)

    for i in range(1, 6):
        loads[i].wait()
    query = query_s[...]
    bilinear = full_dot(jnp.transpose(key_s[...]) * 0.125, query)
    cell = cell_s[...]
    hot_s[...] = jnp.where(
        lax.broadcasted_iota(jnp.int32, (256, 512), 0) == cell, 1.0, 0.0
    ).astype(jnp.bfloat16)
    enc = enc_s[...]
    taps = jnp.concatenate([enc[:, 0:64], enc[:, 64:128], enc[:, 128:192]], axis=0)
    mixed = full_dot(taps, x_s[...])
    for b in range(4):
        index = jnp.broadcast_to(cell[:, b * 128 : (b + 1) * 128], (64, 128))
        asked_s[:, b * 128 : (b + 1) * 128] = jnp.where(
            index >= 128,
            lanes(bilinear[:, 128:], index & 127),
            lanes(bilinear[:, :128], index & 127),
        )
    prior_s[...] = jnp.sum(query * bilinear, axis=0, keepdims=True)

    two, one, zero = mixed[0:64], mixed[64:128], mixed[128:192]
    slot = lax.broadcasted_iota(jnp.int32, (1, 512), 1)
    drawn = (
        zero
        + jnp.where(slot < 1, 0.0, pltpu.roll(one, 1, 1))
        + jnp.where(slot < 2, 0.0, pltpu.roll(two, 2, 1))
    )
    cell = cell_s[...]
    quality = quality_s[...]
    live = live_ref[0, 0]
    packet = pltpu.make_async_remote_copy(
        src_ref=pack_s,
        dst_ref=packed_s,
        send_sem=packet_sem.at[0],
        recv_sem=packet_sem.at[1],
        device_id=(s, down),
        device_id_type=MESH,
    )

    @pl.when(far_down)
    def _():
        lane = lax.broadcasted_iota(jnp.int32, (64, 128), 1)
        lane8 = lax.broadcasted_iota(jnp.int32, (8, 128), 1)
        row8 = lax.broadcasted_iota(jnp.int32, (8, 128), 0)
        pack_s[0:64] = jnp.where(
            lane < 2, drawn[:, 0:128], pltpu.roll(asked_s[:, 0:128], 2, 1)
        )
        pack_s[64:72] = jnp.where(
            row8 == 0,
            quality[:, 0:128],
            jnp.where(
                row8 == 1,
                cell[:, 0:128].astype(jnp.float32),
                jnp.where(lane8 < live, 1.0, 0.0),
            ),
        )
        packet.start()

    encoded = gelu(drawn)
    score = jnp.sum(encoded * asked_s[...], axis=0, keepdims=True)
    score = score + quality
    valid = (slot < live) & (slot >= 2)

    hot = lax.broadcasted_iota(jnp.int32, (256, 512), 0) == cell
    masked = jnp.where(valid, score, FLOOR)
    peak = jnp.max(jnp.where(hot, masked, FLOOR), axis=1, keepdims=True)
    eye = lax.broadcasted_iota(jnp.int32, (128, 128), 0) == lax.broadcasted_iota(
        jnp.int32, (128, 128), 1
    )
    halves = [
        jnp.max(
            jnp.where(eye, peak[h * 128 : (h + 1) * 128], FLOOR), axis=0, keepdims=True
        )
        for h in range(2)
    ]
    slot_peak = []
    for b in range(4):
        index = jnp.broadcast_to(cell[:, b * 128 : (b + 1) * 128], (8, 128))
        low, high = (lanes(jnp.broadcast_to(half, (8, 128)), index & 127) for half in halves)
        slot_peak.append(jnp.where(index >= 128, high, low)[0:1])
    slot_peak = jnp.concatenate(slot_peak, axis=1)
    peak = jnp.concatenate(halves, axis=1)
    weight = jnp.where(valid, jnp.exp(score - slot_peak), 0.0)
    weighted = jnp.concatenate(
        [encoded * weight, jnp.broadcast_to(weight, (8, 512))], axis=0
    )
    one_hot = hot_s[...]
    turned = ((1,), (1,))
    high = weighted.astype(jnp.bfloat16)
    low = (weighted - high.astype(jnp.float32)).astype(jnp.bfloat16)
    sums = dot(high, one_hot, turned, None) + dot(low, one_hot, turned, None)
    query = query_s[...]
    prior = prior_s[...]
    prior = jnp.where(s == 0, prior, FLOOR)
    joint = jnp.maximum(peak, prior)
    factor = jnp.exp(peak - joint)
    prior_factor = jnp.exp(prior - joint)
    total = sums[64:65] * factor + prior_factor
    sums = sums[0:64] * factor + query * prior_factor
    peak = joint

    row = lax.broadcasted_iota(jnp.int32, (32, 256), 0)
    chosen = lax.broadcasted_iota(jnp.int32, (32, 256), 1) == (
        (row & 15) * 16 + jnp.where(row >= 16, 15, 0)
    )
    chosen = jnp.where(chosen, 1.0, 0.0)
    chosen = jnp.concatenate([chosen] * 3, axis=1).astype(jnp.bfloat16)

    def edge_rows(peak, total, sums):
        rows = jnp.concatenate(
            [sums, peak, total, jnp.zeros((62, 256), jnp.float32)], axis=0
        )
        rows = jnp.concatenate(split3(rows), axis=1).astype(jnp.bfloat16)
        return dot(chosen, rows, turned, None)

    def edge_copy(source, k, cell_to, target, out, into):
        dz, dx = (OFFSETS + ((0, 0),))[k]
        slot = dz * 4 + dx
        return pltpu.make_async_remote_copy(
            src_ref=source,
            dst_ref=target.at[slot],
            send_sem=out.at[slot],
            recv_sem=into.at[slot],
            device_id=(partner(dz, dx), cell_to),
            device_id_type=MESH,
        )

    ups = [
        edge_copy(edge_s.at[pl.ds(16, 16)], k, up, prev_s, up_out, up_in)
        for k in range(8)
    ]
    downs, far_downs = (
        [edge_copy(source, k, down, next_s, down_out, down_in) for k in range(8)]
        for source in (edge_s.at[pl.ds(0, 16)], early_s)
    )

    parts, lates = [], []
    for dz, dx in OFFSETS:
        slot = dz * 4 + dx
        to = partner(dz, dx)
        for source, target, out, into in (
            (send_s.at[to], part_s.at[slot], part_out, part_in),
            (span_s, spans_s.at[slot], span_out, span_in),
        ):
            parts.append(
                pltpu.make_async_remote_copy(
                    src_ref=source,
                    dst_ref=target,
                    send_sem=out.at[slot],
                    recv_sem=into.at[slot],
                    device_id=(to, c),
                    device_id_type=MESH,
                )
            )
        lates.append(
            pltpu.make_async_remote_copy(
                src_ref=late_s.at[to],
                dst_ref=lates_s.at[slot],
                send_sem=late_out.at[slot],
                recv_sem=late_in.at[slot],
                device_id=(to, c),
                device_id_type=MESH,
            )
        )

    @pl.when(far_down)
    def _():
        span_s[...] = jnp.concatenate([peak, total], axis=0)
        send_s[...] = sums.reshape(8, 8, 256)
        for copy in parts:
            copy.start()
        early_s[...] = edge_rows(peak, total, sums)[0:16]
        pl.semaphore_wait(ready, 7)
        for copy in far_downs:
            copy.start()

    @pl.when(has_down)
    def _():
        tail.wait_recv()

    parity = (lax.broadcasted_iota(jnp.int32, (64, 128), 1) & 1) == 0

    def late_tokens(rows, drawn, asked):
        made = [
            jnp.sum(enc_s[:, 0:128] * rows[t : t + 1], axis=1, keepdims=True)
            + drawn[:, t : t + 1]
            for t in range(2)
        ]
        made = gelu(jnp.where(parity, made[0], made[1]))
        asked = jnp.where(parity, asked[:, 0:1], asked[:, 1:2])
        return made, jnp.sum(made * asked, axis=0, keepdims=True)

    late, late_score = late_tokens(tail_s[...], drawn[:, 0:128], asked_s[:, 0:2])

    @pl.when(far_down)
    def _():
        lane = lax.broadcasted_iota(jnp.int32, (1, 128), 1)
        where_t = (lane & 1) == 0
        marks = [
            jnp.where(where_t, one[:, 0:1], one[:, 1:2])
            for one in (
                jnp.where(lane < live, late_score + quality[:, 0:128], FLOOR),
                cell[:, 0:128].astype(jnp.float32),
            )
        ]
        late_s[...] = jnp.where(
            lane < 64, late, jnp.where(lane < 96, marks[0], marks[1])
        ).reshape(8, 8, 128)
        for copy in lates:
            copy.start()

    cells = lax.broadcasted_iota(jnp.int32, (1, 256), 1)
    there = [(cells == cell[:, t : t + 1]) & (t < live) for t in range(2)]
    scores = [
        jnp.where(there[t], late_score[:, t : t + 1] + quality[:, t : t + 1], FLOOR)
        for t in range(2)
    ]
    joint = jnp.maximum(peak, jnp.maximum(scores[0], scores[1]))
    factor = jnp.exp(peak - joint)
    total, sums = total * factor, sums * factor
    for t in range(2):
        weight = jnp.where(there[t], jnp.exp(scores[t] - joint), 0.0)
        total = total + weight
        sums = sums + late[:, t : t + 1] * weight
    @pl.when(jnp.logical_not(far_down))
    def _():
        span_s[...] = jnp.concatenate([joint, total], axis=0)
        send_s[...] = sums.reshape(8, 8, 256)
        for copy in parts:
            copy.start()

    edge_s[...] = edge_rows(joint, total, sums)

    @pl.when(jnp.logical_not(far_down))
    def _():
        pl.semaphore_wait(ready, 7)

    @pl.when(has_up)
    def _():
        for copy in ups:
            copy.start()

    @pl.when(has_down & jnp.logical_not(far_down))
    def _():
        for copy in downs:
            copy.start()

    for i in range(6, 9):
        loads[i].wait()
    hp = hp_s[...]
    stacked = jnp.concatenate([hp[:, k * 64 : (k + 1) * 64] for k in range(9)], axis=0)
    stencil = dot(stacked, value_s[...])
    part0, part1, _ = split3(stencil)
    stencil_parts = jnp.concatenate([part0, part1, part0], axis=1).astype(jnp.bfloat16)
    near = near_s[...] - c * 256
    near_edge = ((near >> 4) & 15) + jnp.where(near < 0, 16, 0)
    near_side = (near < 0) | (near >= 256)

    shared = []
    for dz, dx in OFFSETS:
        slot = dz * 4 + dx
        shared.append(
            pltpu.make_async_remote_copy(
                src_ref=token_s,
                dst_ref=tokens_s.at[slot],
                send_sem=token_out.at[slot],
                recv_sem=token_in.at[slot],
                device_id=(partner(dz, dx), c),
                device_id_type=MESH,
            )
        )

    @pl.when(far_up)
    def _():
        packet.wait_recv()
        made, made_score = late_tokens(
            head_s[...], packed_s[0:64, 0:2], packed_s[0:64, 2:4]
        )
        made_score = jnp.where(
            packed_s[66:67] > 0.0, made_score + packed_s[64:65], FLOOR
        )
        rows = jnp.transpose(made)[0:8]
        row8 = lax.broadcasted_iota(jnp.int32, (8, 64), 0)
        lane8 = lax.broadcasted_iota(jnp.int32, (8, 64), 1)
        others = [
            jnp.where(row8 == 0, one[:, 0:1], one[:, 1:2])
            for one in (made_score, packed_s[65:66])
        ]
        token_s[...] = jnp.concatenate(
            [
                rows,
                jnp.where(
                    lane8 == 0, others[0], jnp.where(lane8 == 1, 1.0, others[1])
                ),
            ],
            axis=1,
        )
        for copy in shared:
            copy.start()

    for copy in parts:
        copy.wait_recv()
    blocks = [send_s[s]] + [part_s[k] for k in range(1, 8)]
    spans = [span_s[...]] + [spans_s[k] for k in range(1, 8)]
    peaks = jnp.concatenate([one[0:1] for one in spans], axis=0)
    totals = jnp.concatenate([one[1:2] for one in spans], axis=0)
    joint = jnp.max(peaks, axis=0, keepdims=True)

    @pl.when(jnp.logical_not(far_down))
    def _():
        factor = jnp.exp(peaks - joint)
        below = jnp.sum(totals * factor, axis=0, keepdims=True)
        pool_s[s] = sum(blocks[k] * factor[k : k + 1] for k in range(8)) / below

    @pl.when(far_down)
    def _():
        for copy in lates:
            copy.wait_recv()
        cells = lax.broadcasted_iota(jnp.int32, (8, 256), 1).astype(jnp.float32)
        tiles = [late_s[s]] + [lates_s[k] for k in range(1, 8)]
        entries = []
        for t in range(2):
            scores = jnp.concatenate([one[0:1, 64 + t : 65 + t] for one in tiles], axis=0)
            places = jnp.concatenate([one[0:1, 96 + t : 97 + t] for one in tiles], axis=0)
            entries.append(jnp.where(cells == places, scores, FLOOR))
        all_joint = jnp.maximum(
            joint, jnp.max(jnp.maximum(entries[0], entries[1]), axis=0, keepdims=True)
        )
        factor = jnp.exp(peaks - all_joint)
        below = jnp.sum(totals * factor, axis=0, keepdims=True)
        above = sum(blocks[k] * factor[k : k + 1] for k in range(8))
        for t in range(2):
            weight = jnp.exp(entries[t] - all_joint)
            below = below + jnp.sum(weight, axis=0, keepdims=True)
            above = above + sum(
                tiles[k][:, t : t + 1] * weight[k : k + 1] for k in range(8)
            )
        pool_s[s] = above / below

    pools = []
    for dz, dx in OFFSETS:
        slot = dz * 4 + dx
        copy = pltpu.make_async_remote_copy(
            src_ref=pool_s.at[s],
            dst_ref=pool_s.at[s],
            send_sem=pool_out.at[slot],
            recv_sem=pool_in.at[slot],
            device_id=(partner(dz, dx), c),
            device_id_type=MESH,
        )
        copy.start()
        pools.append(copy)

    @pl.when(has_down)
    def _():
        for copy in ups:
            copy.wait_recv()

    @pl.when(has_up)
    def _():
        for copy in downs:
            copy.wait_recv()

    def mean(blocks):
        joint = functools.reduce(jnp.maximum, blocks)[:, 64:65]
        whole = sum(block * jnp.exp(block[:, 64:65] - joint) for block in blocks)
        return whole[:, 0:64] / whole[:, 65:66]

    below_blocks = [next_s[k] for k in range(8)]

    @pl.when(jnp.logical_not(far_up))
    def _():
        side_s[...] = mean(below_blocks)

    @pl.when(far_up)
    def _():
        for copy in shared:
            copy.wait_recv()
        first_cell = lax.broadcasted_iota(jnp.int32, (16, 128), 0).astype(jnp.float32) * 16.0
        more = []
        for tokens in [token_s[...]] + [tokens_s[k] for k in range(1, 8)]:
            for t in range(2):
                more.append(
                    jnp.where(
                        first_cell == tokens[t : t + 1, 66:67], tokens[t : t + 1], FLOOR
                    )
                )
        side_s[...] = mean(below_blocks + more)

    edges = jnp.concatenate(
        [
            side_s[...],
            mean([prev_s[k] for k in range(8)]),
            jnp.zeros((96, 64), jnp.float32),
        ],
        axis=0,
    )
    outer = dot(stencil[8:72], edges, turned, HIGH)

    for copy in pools:
        copy.wait_recv()
    part0, part1, _ = split3(pool_s[...].reshape(64, 256))
    inner = dot(
        stencil_parts,
        jnp.concatenate([part0, part0, part1], axis=0).astype(jnp.bfloat16),
        precision=None,
    )
    joined = inner[0:8]
    picked = []
    for k in range(8):
        index = jnp.broadcast_to(near[k : k + 1], (8, 256))
        row = inner[8 + k * 8 : 16 + k * 8]
        halves = []
        for h in range(2):
            part = index[:, h * 128 : (h + 1) * 128]
            halves.append(
                jnp.where(
                    (part & 128) > 0,
                    lanes(row[:, 128:], part & 127),
                    lanes(row[:, :128], part & 127),
                )
            )
        picked.append(halves)

    for h in range(2):
        total = joined[:, h * 128 : (h + 1) * 128]
        for k in range(8):
            cut = slice(h * 128, (h + 1) * 128)
            index = jnp.broadcast_to(near_edge[k : k + 1, cut], (8, 128))
            side = jnp.broadcast_to(near_side[k : k + 1, cut], (8, 128))
            total = total + jnp.where(
                side, lanes(outer[k * 8 : (k + 1) * 8], index), picked[k][h]
            )
        out_ref[:, h * 128 : (h + 1) * 128] = total

    @pl.when(has_up)
    def _():
        for copy in [tail] + ups:
            copy.wait_send()

    @pl.when(has_down)
    def _():
        for copy in downs:
            copy.wait_send()

    @pl.when(far_down)
    def _():
        for copy in [packet] + lates:
            copy.wait_send()

    @pl.when(far_up)
    def _():
        for copy in shared:
            copy.wait_send()

    for copy in parts + pools:
        copy.wait_send()


def on_device(*operands):
    f32, i32 = jnp.float32, jnp.int32
    dma = pltpu.SemaphoreType.DMA
    return pl.pallas_call(
        kernel,
        out_shape=pltpu.VMEM((8, 256), f32),
        in_specs=[
            pl.BlockSpec(memory_space=pltpu.SMEM if i == 7 else pltpu.HBM)
            for i in range(10)
        ],
        out_specs=pl.BlockSpec(memory_space=pltpu.VMEM),
        scratch_shapes=[
            pltpu.VMEM((64, 512), f32),
            pltpu.VMEM((64, 192), f32),
            pltpu.VMEM((64, 64), f32),
            pltpu.VMEM((64, 64), f32),
            pltpu.VMEM((64, 256), f32),
            pltpu.VMEM((1, 512), f32),
            pltpu.VMEM((1, 512), i32),
            pltpu.VMEM((8, 256), i32),
            pltpu.VMEM((8, 576), f32),
            pltpu.VMEM((256, 512), jnp.bfloat16),
            pltpu.VMEM((64, 512), f32),
            pltpu.VMEM((1, 256), f32),
            pltpu.VMEM((8, 128), f32),
            pltpu.VMEM((8, 128), f32),
            pltpu.VMEM((8, 8, 256), f32),
            pltpu.VMEM((2, 256), f32),
            pltpu.VMEM((32, 128), f32),
            pltpu.VMEM((16, 128), f32),
            pltpu.VMEM((72, 128), f32),
            pltpu.VMEM((72, 128), f32),
            pltpu.VMEM((8, 128), f32),
            pltpu.VMEM((8, 8, 128), f32),
            pltpu.VMEM((8, 8, 128), f32),
            pltpu.VMEM((8, 8, 128), f32),
            pltpu.VMEM((16, 64), f32),
            pltpu.VMEM((8, 8, 256), f32),
            pltpu.VMEM((8, 2, 256), f32),
            pltpu.VMEM((8, 8, 256), f32),
            pltpu.VMEM((8, 16, 128), f32),
            pltpu.VMEM((8, 16, 128), f32),
            dma((9,)),
            dma((2,)),
        ]
        + [dma((8,))] * 10
        + [dma((2,))]
        + [dma((8,))] * 4
        + [pltpu.SemaphoreType.REGULAR],
        compiler_params=pltpu.CompilerParams(collective_id=0, has_side_effects=True),
    )(*operands)


def solution(mesh):
    in_specs = (
        P("sensor", None, "cell"),
        P("sensor", None, None),
        P(),
        P(),
        P(None, "cell"),
        P("sensor", "cell"),
        P("sensor", "cell"),
        P("sensor", "cell"),
        P(None, "cell"),
        P(),
    )
    return jax.shard_map(
        on_device,
        mesh=mesh,
        in_specs=in_specs,
        out_specs=P("sensor", "cell"),
        check_vma=False,
    )
```

```python
import functools

import jax
import jax.numpy as jnp
from jax import lax
from jax.experimental import pallas as pl
from jax.experimental.pallas import tpu as pltpu
from jax.sharding import PartitionSpec as P

MESH = pl.DeviceIdType.MESH
FLOOR = -1e30
HIGH, HIGHEST = lax.Precision.HIGH, lax.Precision.HIGHEST
OFFSETS = ((1, 2), (0, 2), (1, 1), (1, 3), (0, 1), (0, 3), (1, 0))


def dot(a, b, dims=((1,), (0,)), precision=HIGHEST):
    return lax.dot_general(
        a, b, (dims, ((), ())), precision=precision, preferred_element_type=jnp.float32
    )


def lanes(values, index):
    return jnp.take_along_axis(values, index, axis=1, mode="promise_in_bounds")


def split3(x):
    high = x.astype(jnp.bfloat16).astype(jnp.float32)
    mid = (x - high).astype(jnp.bfloat16).astype(jnp.float32)
    return high, mid, x - high - mid


def full_dot(a, b):
    a0, a1, a2 = split3(a)
    b0, b1, b2 = split3(b)
    left = jnp.concatenate([a0, a0, a1, a1, a0, a2], axis=1).astype(jnp.bfloat16)
    right = jnp.concatenate([b0, b1, b0, b1, b2, b0], axis=0).astype(jnp.bfloat16)
    return dot(left, right, precision=None)


def gelu(x):
    return 0.5 * x * (1.0 + lax.erf(x * 0.7071067811865476))


def kernel(
    swath_ref,
    enc_ref,
    key_ref,
    value_ref,
    query_ref,
    quality_ref,
    cell_ref,
    live_ref,
    near_ref,
    hp_ref,
    out_ref,
    x_s,
    enc_s,
    key_s,
    value_s,
    query_s,
    quality_s,
    cell_s,
    near_s,
    hp_s,
    hot_s,
    asked_s,
    prior_s,
    tail_s,
    head_s,
    send_s,
    span_s,
    edge_s,
    early_s,
    pack_s,
    packed_s,
    token_s,
    tokens_s,
    pooled_s,
    side_s,
    part_s,
    spans_s,
    pool_s,
    prev_s,
    next_s,
    in_sem,
    tail_sem,
    part_out,
    part_in,
    span_out,
    span_in,
    pool_out,
    pool_in,
    up_out,
    up_in,
    down_out,
    down_in,
    packet_sem,
    token_out,
    token_in,
    ready,
):
    s = lax.axis_index("sensor")
    c = lax.axis_index("cell")
    z, x = s // 4, s % 4
    up, down = c + 1, c - 1
    has_up, has_down = c < 63, c > 0
    far_up, far_down = has_up & (c % 16 == 15), has_down & (c % 16 == 0)
    ahead = c % 16 == 0

    def partner(dz, dx):
        return ((z + dz) % 2) * 4 + (x + dx) % 4

    loads = [
        pltpu.make_async_copy(source, target, in_sem.at[i])
        for i, (source, target) in enumerate(
            (
                (swath_ref.at[0], x_s),
                (cell_ref, cell_s),
                (query_ref, query_s),
                (key_ref, key_s),
                (enc_ref.at[0], enc_s),
                (quality_ref, quality_s),
                (hp_ref.at[pl.ds(pl.multiple_of(s * 8, 8), 8)], hp_s),
                (value_ref, value_s),
                (near_ref, near_s),
            )
        )
    ]
    for load in loads:
        load.start()

    barrier = pltpu.get_barrier_semaphore()
    for target, there in ((up, has_up), (down, has_down)):

        @pl.when(there)
        def _():
            pl.semaphore_signal(
                barrier, inc=1, device_id=(s, target), device_id_type=MESH
            )

    for dz, dx in OFFSETS:
        pl.semaphore_signal(
            barrier, inc=1, device_id=(partner(dz, dx), c), device_id_type=MESH
        )
    loads[0].wait()
    last = jnp.transpose(x_s[:, 384:512])
    row = lax.broadcasted_iota(jnp.int32, (8, 64), 0)
    head_s[...] = jnp.where(
        lax.broadcasted_iota(jnp.int32, (8, 128), 0) < 2,
        jnp.concatenate(
            [
                jnp.where(row == 0, last[126:127], last[127:128]),
                jnp.where(row == 0, last[127:128], 0.0),
            ],
            axis=1,
        ),
        0.0,
    )

    pl.semaphore_wait(
        barrier, 7 + has_up.astype(jnp.int32) + has_down.astype(jnp.int32)
    )
    tail = pltpu.make_async_remote_copy(
        src_ref=head_s,
        dst_ref=tail_s,
        send_sem=tail_sem.at[0],
        recv_sem=tail_sem.at[1],
        device_id=(s, up),
        device_id_type=MESH,
    )

    @pl.when(has_up)
    def _():
        tail.start()

    for dz, dx in OFFSETS:
        pl.semaphore_signal(
            ready, inc=1, device_id=(partner(dz, dx), c), device_id_type=MESH
        )

    @pl.when(jnp.logical_not(has_down))
    def _():
        tail_s[...] = jnp.zeros((8, 128), jnp.float32)
        prev_s[...] = jnp.ones((8, 16, 128), jnp.float32)

    @pl.when(jnp.logical_not(has_up))
    def _():
        next_s[...] = jnp.ones((8, 16, 128), jnp.float32)

    for i in range(1, 6):
        loads[i].wait()
    query = query_s[...]
    bilinear = full_dot(jnp.transpose(key_s[...]) * 0.125, query)
    cell = cell_s[...]
    hot_s[...] = jnp.where(
        lax.broadcasted_iota(jnp.int32, (256, 512), 0) == cell, 1.0, 0.0
    ).astype(jnp.bfloat16)
    enc = enc_s[...]
    taps = jnp.concatenate([enc[:, 0:64], enc[:, 64:128], enc[:, 128:192]], axis=0)
    mixed = full_dot(taps, x_s[...])
    for b in range(4):
        index = jnp.broadcast_to(cell[:, b * 128 : (b + 1) * 128], (64, 128))
        asked_s[:, b * 128 : (b + 1) * 128] = jnp.where(
            index >= 128,
            lanes(bilinear[:, 128:], index & 127),
            lanes(bilinear[:, :128], index & 127),
        )
    prior_s[...] = jnp.sum(query * bilinear, axis=0, keepdims=True)

    two, one, zero = mixed[0:64], mixed[64:128], mixed[128:192]
    slot = lax.broadcasted_iota(jnp.int32, (1, 512), 1)
    one, two = pltpu.roll(one, 1, 1), pltpu.roll(two, 2, 1)
    begin = slot[:, 0:128]
    drawn = zero + jnp.concatenate(
        [
            jnp.where(begin < 1, 0.0, one[:, 0:128])
            + jnp.where(begin < 2, 0.0, two[:, 0:128]),
            one[:, 128:] + two[:, 128:],
        ],
        axis=1,
    )
    cell = cell_s[...]
    quality = quality_s[...]
    live = live_ref[0, 0]
    packet = pltpu.make_async_remote_copy(
        src_ref=pack_s,
        dst_ref=packed_s,
        send_sem=packet_sem.at[0],
        recv_sem=packet_sem.at[1],
        device_id=(s, down),
        device_id_type=MESH,
    )

    @pl.when(far_down)
    def _():
        lane = lax.broadcasted_iota(jnp.int32, (64, 128), 1)
        lane8 = lax.broadcasted_iota(jnp.int32, (8, 128), 1)
        row8 = lax.broadcasted_iota(jnp.int32, (8, 128), 0)
        pack_s[0:64] = jnp.where(
            lane < 2, drawn[:, 0:128], pltpu.roll(asked_s[:, 0:128], 2, 1)
        )
        pack_s[64:72] = jnp.where(
            row8 == 0,
            quality[:, 0:128],
            jnp.where(
                row8 == 1,
                cell[:, 0:128].astype(jnp.float32),
                jnp.where(lane8 < live, 1.0, 0.0),
            ),
        )
        packet.start()

    encoded = gelu(drawn)
    score = jnp.sum(encoded * asked_s[...], axis=0, keepdims=True)
    score = score + quality
    valid = (slot < live) & (slot >= jnp.where(has_down, 2, 0))

    hot = lax.broadcasted_iota(jnp.int32, (256, 512), 0) == cell
    masked = jnp.where(valid, score, FLOOR)
    peak = jnp.max(jnp.where(hot, masked, FLOOR), axis=1, keepdims=True)
    eye = lax.broadcasted_iota(jnp.int32, (128, 128), 0) == lax.broadcasted_iota(
        jnp.int32, (128, 128), 1
    )
    halves = [
        jnp.max(
            jnp.where(eye, peak[h * 128 : (h + 1) * 128], FLOOR), axis=0, keepdims=True
        )
        for h in range(2)
    ]
    slot_peak = []
    for b in range(4):
        index = jnp.broadcast_to(cell[:, b * 128 : (b + 1) * 128], (8, 128))
        low, high = (lanes(jnp.broadcast_to(half, (8, 128)), index & 127) for half in halves)
        slot_peak.append(jnp.where(index >= 128, high, low)[0:1])
    slot_peak = jnp.concatenate(slot_peak, axis=1)
    peak = jnp.concatenate(halves, axis=1)
    weight = jnp.where(valid, jnp.exp(score - slot_peak), 0.0)
    weighted = jnp.concatenate(
        [encoded * weight, jnp.broadcast_to(weight, (8, 512))], axis=0
    )
    one_hot = hot_s[...]
    turned = ((1,), (1,))
    high = weighted.astype(jnp.bfloat16)
    low = (weighted - high.astype(jnp.float32)).astype(jnp.bfloat16)
    sums = dot(high, one_hot, turned, None) + dot(low, one_hot, turned, None)
    query = query_s[...]
    prior = prior_s[...]
    prior = jnp.where(s == 0, prior, FLOOR)
    joint = jnp.maximum(peak, prior)
    factor = jnp.exp(peak - joint)
    prior_factor = jnp.exp(prior - joint)
    total = sums[64:65] * factor + prior_factor
    sums = sums[0:64] * factor + query * prior_factor
    peak = joint

    row = lax.broadcasted_iota(jnp.int32, (32, 256), 0)
    chosen = lax.broadcasted_iota(jnp.int32, (32, 256), 1) == (
        (row & 15) * 16 + jnp.where(row >= 16, 15, 0)
    )
    chosen = jnp.where(chosen, 1.0, 0.0)
    chosen = jnp.concatenate([chosen] * 3, axis=1).astype(jnp.bfloat16)

    def edge_rows(peak, total, sums):
        rows = jnp.concatenate(
            [sums, peak, total, jnp.zeros((62, 256), jnp.float32)], axis=0
        )
        rows = jnp.concatenate(split3(rows), axis=1).astype(jnp.bfloat16)
        return dot(chosen, rows, turned, None)

    def edge_copy(source, k, cell_to, target, out, into):
        dz, dx = (OFFSETS + ((0, 0),))[k]
        slot = dz * 4 + dx
        return pltpu.make_async_remote_copy(
            src_ref=source,
            dst_ref=target.at[slot],
            send_sem=out.at[slot],
            recv_sem=into.at[slot],
            device_id=(partner(dz, dx), cell_to),
            device_id_type=MESH,
        )

    ups = [
        edge_copy(edge_s.at[pl.ds(16, 16)], k, up, prev_s, up_out, up_in)
        for k in range(8)
    ]
    downs, far_downs = (
        [edge_copy(source, k, down, next_s, down_out, down_in) for k in range(8)]
        for source in (edge_s.at[pl.ds(0, 16)], early_s)
    )

    parts = []
    for dz, dx in OFFSETS:
        slot = dz * 4 + dx
        to = partner(dz, dx)
        for source, target, out, into in (
            (send_s.at[to], part_s.at[slot], part_out, part_in),
            (span_s, spans_s.at[slot], span_out, span_in),
        ):
            parts.append(
                pltpu.make_async_remote_copy(
                    src_ref=source,
                    dst_ref=target,
                    send_sem=out.at[slot],
                    recv_sem=into.at[slot],
                    device_id=(to, c),
                    device_id_type=MESH,
                )
            )

    shared = []
    for dz, dx in OFFSETS:
        slot = dz * 4 + dx
        shared.append(
            pltpu.make_async_remote_copy(
                src_ref=token_s,
                dst_ref=tokens_s.at[slot],
                send_sem=token_out.at[slot],
                recv_sem=token_in.at[slot],
                device_id=(partner(dz, dx), c),
                device_id_type=MESH,
            )
        )

    def share(made, made_score, cells):
        row = lax.broadcasted_iota(jnp.int32, (8, 64), 0)
        column = lax.broadcasted_iota(jnp.int32, (8, 64), 1)
        marks = [
            jnp.where(row == 0, one[:, 0:1], one[:, 1:2]) for one in (made_score, cells)
        ]
        token_s[...] = jnp.concatenate(
            [
                jnp.transpose(made)[0:8],
                jnp.where(column == 0, marks[0], jnp.where(column == 1, 1.0, marks[1])),
            ],
            axis=1,
        )
        for copy in shared:
            copy.start()

    @pl.when(ahead)
    def _():
        span_s[...] = jnp.concatenate([peak, total], axis=0)
        send_s[...] = sums.reshape(8, 8, 256)
        for copy in parts:
            copy.start()

    @pl.when(far_down)
    def _():
        early_s[...] = edge_rows(peak, total, sums)[0:16]
        pl.semaphore_wait(ready, 7)
        for copy in far_downs:
            copy.start()

    @pl.when(has_down)
    def _():
        tail.wait_recv()

    parity = (lax.broadcasted_iota(jnp.int32, (64, 128), 1) & 1) == 0

    def late_tokens(rows, drawn, asked):
        made = [
            jnp.sum(enc_s[:, 0:128] * rows[t : t + 1], axis=1, keepdims=True)
            + drawn[:, t : t + 1]
            for t in range(2)
        ]
        made = gelu(jnp.where(parity, made[0], made[1]))
        asked = jnp.where(parity, asked[:, 0:1], asked[:, 1:2])
        return made, jnp.sum(made * asked, axis=0, keepdims=True)

    late, late_score = late_tokens(tail_s[...], drawn[:, 0:128], asked_s[:, 0:2])

    @pl.when(far_down)
    def _():
        column = lax.broadcasted_iota(jnp.int32, (1, 128), 1)
        share(
            late,
            jnp.where(column < live, late_score + quality[:, 0:128], FLOOR),
            cell[:, 0:128].astype(jnp.float32),
        )

    cells = lax.broadcasted_iota(jnp.int32, (1, 256), 1)
    there = [
        (cells == cell[:, t : t + 1]) & (t < live) & has_down for t in range(2)
    ]
    scores = [
        jnp.where(there[t], late_score[:, t : t + 1] + quality[:, t : t + 1], FLOOR)
        for t in range(2)
    ]
    joint = jnp.maximum(peak, jnp.maximum(scores[0], scores[1]))
    factor = jnp.exp(peak - joint)
    total, sums = total * factor, sums * factor
    for t in range(2):
        weight = jnp.where(there[t], jnp.exp(scores[t] - joint), 0.0)
        total = total + weight
        sums = sums + late[:, t : t + 1] * weight
    @pl.when(jnp.logical_not(ahead))
    def _():
        span_s[...] = jnp.concatenate([joint, total], axis=0)
        send_s[...] = sums.reshape(8, 8, 256)
        for copy in parts:
            copy.start()

    edge_s[...] = edge_rows(joint, total, sums)

    @pl.when(jnp.logical_not(far_down))
    def _():
        pl.semaphore_wait(ready, 7)

    @pl.when(has_up)
    def _():
        for copy in ups:
            copy.start()

    @pl.when(has_down & jnp.logical_not(far_down))
    def _():
        for copy in downs:
            copy.start()

    for i in range(6, 9):
        loads[i].wait()
    hp = hp_s[...]
    stacked = jnp.concatenate([hp[:, k * 64 : (k + 1) * 64] for k in range(9)], axis=0)
    stencil = dot(stacked, value_s[...])
    part0, part1, _ = split3(stencil)
    stencil_parts = jnp.concatenate([part0, part1, part0], axis=1).astype(jnp.bfloat16)
    near = near_s[...] - c * 256
    near_edge = ((near >> 4) & 15) + jnp.where(near < 0, 16, 0)
    near_side = (near < 0) | (near >= 256)

    @pl.when(far_up)
    def _():
        packet.wait_recv()
        made, made_score = late_tokens(
            head_s[...], packed_s[0:64, 0:2], packed_s[0:64, 2:4]
        )
        share(
            made,
            jnp.where(packed_s[66:67] > 0.0, made_score + packed_s[64:65], FLOOR),
            packed_s[65:66],
        )

    for copy in parts:
        copy.wait_recv()
    blocks = [send_s[s]] + [part_s[k] for k in range(1, 8)]
    spans = [span_s[...]] + [spans_s[k] for k in range(1, 8)]
    peaks = jnp.concatenate([one[0:1] for one in spans], axis=0)
    totals = jnp.concatenate([one[1:2] for one in spans], axis=0)
    joint = jnp.max(peaks, axis=0, keepdims=True)
    factor = jnp.exp(peaks - joint)
    below = jnp.sum(totals * factor, axis=0, keepdims=True)
    pool_s[s] = sum(blocks[k] * factor[k : k + 1] for k in range(8)) / below

    pools = []
    for dz, dx in OFFSETS:
        slot = dz * 4 + dx
        copy = pltpu.make_async_remote_copy(
            src_ref=pool_s.at[s],
            dst_ref=pool_s.at[s],
            send_sem=pool_out.at[slot],
            recv_sem=pool_in.at[slot],
            device_id=(partner(dz, dx), c),
            device_id_type=MESH,
        )
        copy.start()
        pools.append(copy)

    @pl.when(has_down)
    def _():
        for copy in ups:
            copy.wait_recv()

    @pl.when(has_up)
    def _():
        for copy in downs:
            copy.wait_recv()

    def mean(blocks):
        joint = functools.reduce(jnp.maximum, blocks)[:, 64:65]
        whole = sum(block * jnp.exp(block[:, 64:65] - joint) for block in blocks)
        return whole[:, 0:64] / whole[:, 65:66]

    below_blocks = [next_s[k] for k in range(8)]

    @pl.when(jnp.logical_not(far_up))
    def _():
        side_s[...] = mean(below_blocks)

    @pl.when(far_up)
    def _():
        for copy in shared:
            copy.wait_recv()
        first_cell = lax.broadcasted_iota(jnp.int32, (16, 128), 0).astype(jnp.float32) * 16.0
        more = []
        for tokens in [token_s[...]] + [tokens_s[k] for k in range(1, 8)]:
            for t in range(2):
                more.append(
                    jnp.where(
                        first_cell == tokens[t : t + 1, 66:67], tokens[t : t + 1], FLOOR
                    )
                )
        side_s[...] = mean(below_blocks + more)

    edges = jnp.concatenate(
        [
            side_s[...],
            mean([prev_s[k] for k in range(8)]),
            jnp.zeros((96, 64), jnp.float32),
        ],
        axis=0,
    )
    outer = dot(stencil[8:72], edges, turned, HIGH)
    outside = []
    for h in range(2):
        cut = slice(h * 128, (h + 1) * 128)
        part = jnp.zeros((8, 128), jnp.float32)
        for k in range(8):
            index = jnp.broadcast_to(near_edge[k : k + 1, cut], (8, 128))
            side = jnp.broadcast_to(near_side[k : k + 1, cut], (8, 128))
            part = part + jnp.where(
                side, lanes(outer[k * 8 : (k + 1) * 8], index), 0.0
            )
        outside.append(part)

    for copy in pools:
        copy.wait_recv()

    @pl.when(jnp.logical_not(far_down))
    def _():
        pooled_s[...] = pool_s[...].reshape(64, 256)

    @pl.when(far_down)
    def _():
        for copy in shared:
            copy.wait_recv()
        rows = jnp.concatenate(
            [token_s[0:2]] + [tokens_s[k, 0:2] for k in range(1, 8)], axis=0
        )
        cells = lax.broadcasted_iota(jnp.int32, (16, 256), 1).astype(jnp.float32)
        entries = jnp.where(cells == rows[:, 66:67], rows[:, 64:65], FLOOR)
        all_joint = jnp.maximum(joint, jnp.max(entries, axis=0, keepdims=True))
        weight = jnp.exp(entries - all_joint)
        old = below * jnp.exp(joint - all_joint)
        pooled_s[...] = (
            pool_s[...].reshape(64, 256) * old + dot(rows[:, 0:64], weight, ((0,), (0,)))
        ) / (old + jnp.sum(weight, axis=0, keepdims=True))

    part0, part1, _ = split3(pooled_s[...])
    inner = dot(
        stencil_parts,
        jnp.concatenate([part0, part0, part1], axis=0).astype(jnp.bfloat16),
        precision=None,
    )
    for h in range(2):
        cut = slice(h * 128, (h + 1) * 128)
        joined = inner[0:8, cut] + outside[h]
        for k in range(8):
            row = inner[8 + k * 8 : 16 + k * 8]
            index = jnp.broadcast_to(near[k : k + 1, cut], (8, 128))
            side = jnp.broadcast_to(near_side[k : k + 1, cut], (8, 128))
            picked = jnp.where(
                (index & 128) > 0,
                lanes(row[:, 128:], index & 127),
                lanes(row[:, :128], index & 127),
            )
            joined = joined + jnp.where(side, 0.0, picked)
        out_ref[:, cut] = joined

    @pl.when(has_up)
    def _():
        for copy in [tail] + ups:
            copy.wait_send()

    @pl.when(has_down)
    def _():
        for copy in downs:
            copy.wait_send()

    @pl.when(far_down)
    def _():
        packet.wait_send()

    @pl.when(far_up | far_down)
    def _():
        for copy in shared:
            copy.wait_send()

    for copy in parts + pools:
        copy.wait_send()


def on_device(*operands):
    f32, i32 = jnp.float32, jnp.int32
    dma = pltpu.SemaphoreType.DMA
    return pl.pallas_call(
        kernel,
        out_shape=pltpu.VMEM((8, 256), f32),
        in_specs=[
            pl.BlockSpec(memory_space=pltpu.SMEM if i == 7 else pltpu.HBM)
            for i in range(10)
        ],
        out_specs=pl.BlockSpec(memory_space=pltpu.VMEM),
        scratch_shapes=[
            pltpu.VMEM((64, 512), f32),
            pltpu.VMEM((64, 192), f32),
            pltpu.VMEM((64, 64), f32),
            pltpu.VMEM((64, 64), f32),
            pltpu.VMEM((64, 256), f32),
            pltpu.VMEM((1, 512), f32),
            pltpu.VMEM((1, 512), i32),
            pltpu.VMEM((8, 256), i32),
            pltpu.VMEM((8, 576), f32),
            pltpu.VMEM((256, 512), jnp.bfloat16),
            pltpu.VMEM((64, 512), f32),
            pltpu.VMEM((1, 256), f32),
            pltpu.VMEM((8, 128), f32),
            pltpu.VMEM((8, 128), f32),
            pltpu.VMEM((8, 8, 256), f32),
            pltpu.VMEM((2, 256), f32),
            pltpu.VMEM((32, 128), f32),
            pltpu.VMEM((16, 128), f32),
            pltpu.VMEM((72, 128), f32),
            pltpu.VMEM((72, 128), f32),
            pltpu.VMEM((8, 128), f32),
            pltpu.VMEM((8, 8, 128), f32),
            pltpu.VMEM((64, 256), f32),
            pltpu.VMEM((16, 64), f32),
            pltpu.VMEM((8, 8, 256), f32),
            pltpu.VMEM((8, 2, 256), f32),
            pltpu.VMEM((8, 8, 256), f32),
            pltpu.VMEM((8, 16, 128), f32),
            pltpu.VMEM((8, 16, 128), f32),
            dma((9,)),
            dma((2,)),
        ]
        + [dma((8,))] * 10
        + [dma((2,))]
        + [dma((8,))] * 2
        + [pltpu.SemaphoreType.REGULAR],
        compiler_params=pltpu.CompilerParams(collective_id=0, has_side_effects=True),
    )(*operands)


def solution(mesh):
    in_specs = (
        P("sensor", None, "cell"),
        P("sensor", None, None),
        P(),
        P(),
        P(None, "cell"),
        P("sensor", "cell"),
        P("sensor", "cell"),
        P("sensor", "cell"),
        P(None, "cell"),
        P(),
    )
    return jax.shard_map(
        on_device,
        mesh=mesh,
        in_specs=in_specs,
        out_specs=P("sensor", "cell"),
        check_vma=False,
    )
```

```python
import functools

import jax
import jax.numpy as jnp
from jax import lax
from jax.experimental import pallas as pl
from jax.experimental.pallas import tpu as pltpu
from jax.sharding import PartitionSpec as P

MESH = pl.DeviceIdType.MESH
FLOOR = -1e30
HIGH, HIGHEST = lax.Precision.HIGH, lax.Precision.HIGHEST
OFFSETS = ((1, 2), (0, 2), (1, 1), (1, 3), (0, 1), (0, 3), (1, 0))


def dot(a, b, dims=((1,), (0,)), precision=HIGHEST):
    return lax.dot_general(
        a, b, (dims, ((), ())), precision=precision, preferred_element_type=jnp.float32
    )


def lanes(values, index):
    return jnp.take_along_axis(values, index, axis=1, mode="promise_in_bounds")


def split3(x):
    high = x.astype(jnp.bfloat16).astype(jnp.float32)
    mid = (x - high).astype(jnp.bfloat16).astype(jnp.float32)
    return high, mid, x - high - mid


def full_dot(a, b):
    a0, a1, a2 = split3(a)
    b0, b1, b2 = split3(b)
    left = jnp.concatenate([a0, a0, a1, a1, a0, a2], axis=1).astype(jnp.bfloat16)
    right = jnp.concatenate([b0, b1, b0, b1, b2, b0], axis=0).astype(jnp.bfloat16)
    return dot(left, right, precision=None)


def gelu(x):
    return 0.5 * x * (1.0 + lax.erf(x * 0.7071067811865476))


def kernel(
    swath_ref,
    enc_ref,
    key_ref,
    value_ref,
    query_ref,
    quality_ref,
    cell_ref,
    live_ref,
    near_ref,
    hp_ref,
    out_ref,
    x_s,
    enc_s,
    key_s,
    value_s,
    query_s,
    quality_s,
    cell_s,
    near_s,
    hp_s,
    hot_s,
    asked_s,
    prior_s,
    tail_s,
    head_s,
    send_s,
    span_s,
    edge_s,
    early_s,
    pack_s,
    packed_s,
    token_s,
    tokens_s,
    far_s,
    fars_s,
    scale_s,
    shift_s,
    side_s,
    part_s,
    spans_s,
    pool_s,
    prev_s,
    next_s,
    in_sem,
    tail_sem,
    part_out,
    part_in,
    span_out,
    span_in,
    pool_out,
    pool_in,
    up_out,
    up_in,
    down_out,
    down_in,
    packet_sem,
    token_out,
    token_in,
    far_out,
    far_in,
    ready,
):
    s = lax.axis_index("sensor")
    c = lax.axis_index("cell")
    z, x = s // 4, s % 4
    up, down = c + 1, c - 1
    has_up, has_down = c < 63, c > 0
    far_up, far_down = has_up & (c % 16 == 15), has_down & (c % 16 == 0)

    def partner(dz, dx):
        return ((z + dz) % 2) * 4 + (x + dx) % 4

    loads = [
        pltpu.make_async_copy(source, target, in_sem.at[i])
        for i, (source, target) in enumerate(
            (
                (swath_ref.at[0], x_s),
                (cell_ref, cell_s),
                (query_ref, query_s),
                (key_ref, key_s),
                (enc_ref.at[0], enc_s),
                (quality_ref, quality_s),
                (hp_ref.at[pl.ds(pl.multiple_of(s * 8, 8), 8)], hp_s),
                (value_ref, value_s),
                (near_ref, near_s),
            )
        )
    ]
    for load in loads:
        load.start()

    barrier = pltpu.get_barrier_semaphore()
    for target, there in ((up, has_up), (down, has_down)):

        @pl.when(there)
        def _():
            pl.semaphore_signal(
                barrier, inc=1, device_id=(s, target), device_id_type=MESH
            )

    for dz, dx in OFFSETS:
        pl.semaphore_signal(
            barrier, inc=1, device_id=(partner(dz, dx), c), device_id_type=MESH
        )
    for i in range(6):
        loads[i].wait()
    last = jnp.transpose(x_s[:, 384:512])
    row = lax.broadcasted_iota(jnp.int32, (8, 64), 0)
    head_s[...] = jnp.where(
        lax.broadcasted_iota(jnp.int32, (8, 128), 0) < 2,
        jnp.concatenate(
            [
                jnp.where(row == 0, last[126:127], last[127:128]),
                jnp.where(row == 0, last[127:128], 0.0),
            ],
            axis=1,
        ),
        0.0,
    )

    query = query_s[...]
    bilinear = full_dot(jnp.transpose(key_s[...]) * 0.125, query)
    cell = cell_s[...]
    hot_s[...] = jnp.where(
        lax.broadcasted_iota(jnp.int32, (256, 512), 0) == cell, 1.0, 0.0
    ).astype(jnp.bfloat16)
    enc = enc_s[...]
    taps = jnp.concatenate([enc[:, 0:64], enc[:, 64:128], enc[:, 128:192]], axis=0)
    mixed = full_dot(taps, x_s[...])
    for b in range(4):
        index = jnp.broadcast_to(cell[:, b * 128 : (b + 1) * 128], (64, 128))
        asked_s[:, b * 128 : (b + 1) * 128] = jnp.where(
            index >= 128,
            lanes(bilinear[:, 128:], index & 127),
            lanes(bilinear[:, :128], index & 127),
        )
    prior_s[...] = jnp.sum(query * bilinear, axis=0, keepdims=True)

    two, one, zero = mixed[0:64], mixed[64:128], mixed[128:192]
    slot = lax.broadcasted_iota(jnp.int32, (1, 512), 1)
    one, two = pltpu.roll(one, 1, 1), pltpu.roll(two, 2, 1)
    begin = slot[:, 0:128]
    drawn = zero + jnp.concatenate(
        [
            jnp.where(begin < 1, 0.0, one[:, 0:128])
            + jnp.where(begin < 2, 0.0, two[:, 0:128]),
            one[:, 128:] + two[:, 128:],
        ],
        axis=1,
    )

    pl.semaphore_wait(
        barrier, 7 + has_up.astype(jnp.int32) + has_down.astype(jnp.int32)
    )
    tail = pltpu.make_async_remote_copy(
        src_ref=head_s,
        dst_ref=tail_s,
        send_sem=tail_sem.at[0],
        recv_sem=tail_sem.at[1],
        device_id=(s, up),
        device_id_type=MESH,
    )

    @pl.when(has_up)
    def _():
        tail.start()

    for dz, dx in OFFSETS:
        pl.semaphore_signal(
            ready, inc=1, device_id=(partner(dz, dx), c), device_id_type=MESH
        )

    @pl.when(jnp.logical_not(has_down))
    def _():
        tail_s[...] = jnp.zeros((8, 128), jnp.float32)
        prev_s[...] = jnp.ones((8, 16, 128), jnp.float32)

    @pl.when(jnp.logical_not(has_up))
    def _():
        next_s[...] = jnp.ones((8, 16, 128), jnp.float32)

    cell = cell_s[...]
    quality = quality_s[...]
    live = live_ref[0, 0]
    packet = pltpu.make_async_remote_copy(
        src_ref=pack_s,
        dst_ref=packed_s,
        send_sem=packet_sem.at[0],
        recv_sem=packet_sem.at[1],
        device_id=(s, down),
        device_id_type=MESH,
    )

    @pl.when(far_down)
    def _():
        lane = lax.broadcasted_iota(jnp.int32, (64, 128), 1)
        lane8 = lax.broadcasted_iota(jnp.int32, (8, 128), 1)
        row8 = lax.broadcasted_iota(jnp.int32, (8, 128), 0)
        pack_s[0:64] = jnp.where(
            lane < 2, drawn[:, 0:128], pltpu.roll(asked_s[:, 0:128], 2, 1)
        )
        pack_s[64:72] = jnp.where(
            row8 == 0,
            quality[:, 0:128],
            jnp.where(
                row8 == 1,
                cell[:, 0:128].astype(jnp.float32),
                jnp.where(lane8 < live, 1.0, 0.0),
            ),
        )
        packet.start()

    encoded = gelu(drawn)
    score = jnp.sum(encoded * asked_s[...], axis=0, keepdims=True)
    score = score + quality
    valid = (slot < live) & (slot >= jnp.where(has_down, 2, 0))

    hot = lax.broadcasted_iota(jnp.int32, (256, 512), 0) == cell
    masked = jnp.where(valid, score, FLOOR)
    peak = jnp.max(jnp.where(hot, masked, FLOOR), axis=1, keepdims=True)
    eye = lax.broadcasted_iota(jnp.int32, (128, 128), 0) == lax.broadcasted_iota(
        jnp.int32, (128, 128), 1
    )
    halves = [
        jnp.max(
            jnp.where(eye, peak[h * 128 : (h + 1) * 128], FLOOR), axis=0, keepdims=True
        )
        for h in range(2)
    ]
    slot_peak = []
    for b in range(4):
        index = jnp.broadcast_to(cell[:, b * 128 : (b + 1) * 128], (8, 128))
        low, high = (lanes(jnp.broadcast_to(half, (8, 128)), index & 127) for half in halves)
        slot_peak.append(jnp.where(index >= 128, high, low)[0:1])
    slot_peak = jnp.concatenate(slot_peak, axis=1)
    peak = jnp.concatenate(halves, axis=1)
    weight = jnp.where(valid, jnp.exp(score - slot_peak), 0.0)
    weighted = jnp.concatenate(
        [encoded * weight, jnp.broadcast_to(weight, (8, 512))], axis=0
    )
    one_hot = hot_s[...]
    turned = ((1,), (1,))
    high = weighted.astype(jnp.bfloat16)
    low = (weighted - high.astype(jnp.float32)).astype(jnp.bfloat16)
    sums = dot(high, one_hot, turned, None) + dot(low, one_hot, turned, None)
    query = query_s[...]
    prior = prior_s[...]
    prior = jnp.where(s == 0, prior, FLOOR)
    joint = jnp.maximum(peak, prior)
    factor = jnp.exp(peak - joint)
    prior_factor = jnp.exp(prior - joint)
    total = sums[64:65] * factor + prior_factor
    sums = sums[0:64] * factor + query * prior_factor
    peak = joint

    row = lax.broadcasted_iota(jnp.int32, (32, 256), 0)
    chosen = lax.broadcasted_iota(jnp.int32, (32, 256), 1) == (
        (row & 15) * 16 + jnp.where(row >= 16, 15, 0)
    )
    chosen = jnp.where(chosen, 1.0, 0.0)
    chosen = jnp.concatenate([chosen] * 3, axis=1).astype(jnp.bfloat16)

    def edge_rows(peak, total, sums):
        rows = jnp.concatenate(
            [sums, peak, total, jnp.zeros((62, 256), jnp.float32)], axis=0
        )
        rows = jnp.concatenate(split3(rows), axis=1).astype(jnp.bfloat16)
        return dot(chosen, rows, turned, None)

    def edge_copy(source, k, cell_to, target, out, into):
        dz, dx = (OFFSETS + ((0, 0),))[k]
        slot = dz * 4 + dx
        return pltpu.make_async_remote_copy(
            src_ref=source,
            dst_ref=target.at[slot],
            send_sem=out.at[slot],
            recv_sem=into.at[slot],
            device_id=(partner(dz, dx), cell_to),
            device_id_type=MESH,
        )

    ups = [
        edge_copy(edge_s.at[pl.ds(16, 16)], k, up, prev_s, up_out, up_in)
        for k in range(8)
    ]
    downs, far_downs = (
        [edge_copy(source, k, down, next_s, down_out, down_in) for k in range(8)]
        for source in (edge_s.at[pl.ds(0, 16)], early_s)
    )

    parts = []
    for dz, dx in OFFSETS:
        slot = dz * 4 + dx
        to = partner(dz, dx)
        for source, target, out, into in (
            (send_s.at[to], part_s.at[slot], part_out, part_in),
            (span_s, spans_s.at[slot], span_out, span_in),
        ):
            parts.append(
                pltpu.make_async_remote_copy(
                    src_ref=source,
                    dst_ref=target,
                    send_sem=out.at[slot],
                    recv_sem=into.at[slot],
                    device_id=(to, c),
                    device_id_type=MESH,
                )
            )

    shared, far_shared = (
        [
            pltpu.make_async_remote_copy(
                src_ref=source,
                dst_ref=target.at[dz * 4 + dx],
                send_sem=out.at[dz * 4 + dx],
                recv_sem=into.at[dz * 4 + dx],
                device_id=(partner(dz, dx), c),
                device_id_type=MESH,
            )
            for dz, dx in OFFSETS
        ]
        for source, target, out, into in (
            (token_s, tokens_s, token_out, token_in),
            (far_s, fars_s, far_out, far_in),
        )
    )

    def share(target, copies, made, made_score, cells):
        row = lax.broadcasted_iota(jnp.int32, (8, 64), 0)
        column = lax.broadcasted_iota(jnp.int32, (8, 64), 1)
        marks = [
            jnp.where(row == 0, one[:, 0:1], one[:, 1:2]) for one in (made_score, cells)
        ]
        target[...] = jnp.concatenate(
            [
                jnp.transpose(made)[0:8],
                jnp.where(column == 0, marks[0], jnp.where(column == 1, 1.0, marks[1])),
            ],
            axis=1,
        )
        for copy in copies:
            copy.start()

    span_s[...] = jnp.concatenate([peak, total], axis=0)
    send_s[...] = sums.reshape(8, 8, 256)
    for copy in parts:
        copy.start()

    @pl.when(far_down)
    def _():
        early_s[...] = edge_rows(peak, total, sums)[0:16]
        pl.semaphore_wait(ready, 7)
        for copy in far_downs:
            copy.start()

    @pl.when(has_down)
    def _():
        tail.wait_recv()

    parity = (lax.broadcasted_iota(jnp.int32, (64, 128), 1) & 1) == 0

    def late_tokens(rows, drawn, asked):
        made = [
            jnp.sum(enc_s[:, 0:128] * rows[t : t + 1], axis=1, keepdims=True)
            + drawn[:, t : t + 1]
            for t in range(2)
        ]
        made = gelu(jnp.where(parity, made[0], made[1]))
        asked = jnp.where(parity, asked[:, 0:1], asked[:, 1:2])
        return made, jnp.sum(made * asked, axis=0, keepdims=True)

    late, late_score = late_tokens(tail_s[...], drawn[:, 0:128], asked_s[:, 0:2])

    def share_own():
        column = lax.broadcasted_iota(jnp.int32, (1, 128), 1)
        share(
            token_s,
            shared,
            late,
            jnp.where(column < live, late_score + quality[:, 0:128], FLOOR),
            cell[:, 0:128].astype(jnp.float32),
        )

    pl.when(far_down)(share_own)
    cells = lax.broadcasted_iota(jnp.int32, (1, 256), 1)
    there = [
        (cells == cell[:, t : t + 1]) & (t < live) & has_down for t in range(2)
    ]
    scores = [
        jnp.where(there[t], late_score[:, t : t + 1] + quality[:, t : t + 1], FLOOR)
        for t in range(2)
    ]
    joint = jnp.maximum(peak, jnp.maximum(scores[0], scores[1]))
    factor = jnp.exp(peak - joint)
    total, sums = total * factor, sums * factor
    for t in range(2):
        weight = jnp.where(there[t], jnp.exp(scores[t] - joint), 0.0)
        total = total + weight
        sums = sums + late[:, t : t + 1] * weight

    edge_s[...] = edge_rows(joint, total, sums)

    @pl.when(jnp.logical_not(far_down))
    def _():
        pl.semaphore_wait(ready, 7)

    @pl.when(has_up)
    def _():
        for copy in ups:
            copy.start()

    @pl.when(has_down & jnp.logical_not(far_down))
    def _():
        for copy in downs:
            copy.start()

    pl.when(has_down & jnp.logical_not(far_down))(share_own)

    for i in range(6, 9):
        loads[i].wait()
    hp = hp_s[...]
    stacked = jnp.concatenate([hp[:, k * 64 : (k + 1) * 64] for k in range(9)], axis=0)
    stencil = dot(stacked, value_s[...])
    part0, part1, _ = split3(stencil)
    stencil_parts = jnp.concatenate([part0, part1, part0], axis=1).astype(jnp.bfloat16)
    near = near_s[...] - c * 256
    near_edge = ((near >> 4) & 15) + jnp.where(near < 0, 16, 0)
    near_side = (near < 0) | (near >= 256)

    @pl.when(far_up)
    def _():
        packet.wait_recv()
        made, made_score = late_tokens(
            head_s[...], packed_s[0:64, 0:2], packed_s[0:64, 2:4]
        )
        share(
            far_s,
            far_shared,
            made,
            jnp.where(packed_s[66:67] > 0.0, made_score + packed_s[64:65], FLOOR),
            packed_s[65:66],
        )

    for copy in parts:
        copy.wait_recv()
    blocks = [send_s[s]] + [part_s[k] for k in range(1, 8)]
    spans = [span_s[...]] + [spans_s[k] for k in range(1, 8)]
    peaks = jnp.concatenate([one[0:1] for one in spans], axis=0)
    totals = jnp.concatenate([one[1:2] for one in spans], axis=0)
    joint = jnp.max(peaks, axis=0, keepdims=True)
    factor = jnp.exp(peaks - joint)
    below = jnp.sum(totals * factor, axis=0, keepdims=True)
    pool_s[s] = sum(blocks[k] * factor[k : k + 1] for k in range(8)) / below

    pools = []
    for dz, dx in OFFSETS:
        slot = dz * 4 + dx
        copy = pltpu.make_async_remote_copy(
            src_ref=pool_s.at[s],
            dst_ref=pool_s.at[s],
            send_sem=pool_out.at[slot],
            recv_sem=pool_in.at[slot],
            device_id=(partner(dz, dx), c),
            device_id_type=MESH,
        )
        copy.start()
        pools.append(copy)

    @pl.when(has_down)
    def _():
        for copy in ups:
            copy.wait_recv()

    @pl.when(has_up)
    def _():
        for copy in downs:
            copy.wait_recv()

    def mean(blocks):
        joint = functools.reduce(jnp.maximum, blocks)[:, 64:65]
        whole = sum(block * jnp.exp(block[:, 64:65] - joint) for block in blocks)
        return whole[:, 0:64] / whole[:, 65:66]

    below_blocks = [next_s[k] for k in range(8)]

    @pl.when(jnp.logical_not(far_up))
    def _():
        side_s[...] = mean(below_blocks)

    @pl.when(far_up)
    def _():
        for copy in far_shared:
            copy.wait_recv()
        first_cell = lax.broadcasted_iota(jnp.int32, (16, 128), 0).astype(jnp.float32) * 16.0
        more = []
        for tokens in [far_s[...]] + [fars_s[k] for k in range(1, 8)]:
            for t in range(2):
                more.append(
                    jnp.where(
                        first_cell == tokens[t : t + 1, 66:67], tokens[t : t + 1], FLOOR
                    )
                )
        side_s[...] = mean(below_blocks + more)

    edges = jnp.concatenate(
        [
            side_s[...],
            mean([prev_s[k] for k in range(8)]),
            jnp.zeros((96, 64), jnp.float32),
        ],
        axis=0,
    )
    outer = dot(stencil[8:72], edges, turned, HIGH)
    outside = []
    for h in range(2):
        cut = slice(h * 128, (h + 1) * 128)
        part = jnp.zeros((8, 128), jnp.float32)
        for k in range(8):
            index = jnp.broadcast_to(near_edge[k : k + 1, cut], (8, 128))
            side = jnp.broadcast_to(near_side[k : k + 1, cut], (8, 128))
            part = part + jnp.where(
                side, lanes(outer[k * 8 : (k + 1) * 8], index), 0.0
            )
        outside.append(part)

    @pl.when(jnp.logical_not(has_down))
    def _():
        scale_s[...] = jnp.ones((1, 256), jnp.float32)
        shift_s[...] = jnp.zeros((64, 256), jnp.float32)

    @pl.when(has_down)
    def _():
        for copy in shared:
            copy.wait_recv()
        rows = jnp.concatenate(
            [token_s[0:2]] + [tokens_s[k, 0:2] for k in range(1, 8)], axis=0
        )
        cells = lax.broadcasted_iota(jnp.int32, (16, 256), 1).astype(jnp.float32)
        entries = jnp.where(cells == rows[:, 66:67], rows[:, 64:65], FLOOR)
        all_joint = jnp.maximum(joint, jnp.max(entries, axis=0, keepdims=True))
        weight = jnp.exp(entries - all_joint)
        old = below * jnp.exp(joint - all_joint)
        share_of = 1.0 / (old + jnp.sum(weight, axis=0, keepdims=True))
        scale_s[...] = old * share_of
        shift_s[...] = dot(rows[:, 0:64], weight * share_of, ((0,), (0,)))

    for copy in pools:
        copy.wait_recv()
    pooled = pool_s[...].reshape(64, 256) * scale_s[...] + shift_s[...]
    part0, part1, _ = split3(pooled)
    inner = dot(
        stencil_parts,
        jnp.concatenate([part0, part0, part1], axis=0).astype(jnp.bfloat16),
        precision=None,
    )
    for h in range(2):
        cut = slice(h * 128, (h + 1) * 128)
        joined = inner[0:8, cut] + outside[h]
        for k in range(8):
            row = inner[8 + k * 8 : 16 + k * 8]
            index = jnp.broadcast_to(near[k : k + 1, cut], (8, 128))
            side = jnp.broadcast_to(near_side[k : k + 1, cut], (8, 128))
            picked = jnp.where(
                (index & 128) > 0,
                lanes(row[:, 128:], index & 127),
                lanes(row[:, :128], index & 127),
            )
            joined = joined + jnp.where(side, 0.0, picked)
        out_ref[:, cut] = joined

    @pl.when(has_up)
    def _():
        for copy in [tail] + ups:
            copy.wait_send()

    @pl.when(has_down)
    def _():
        for copy in downs:
            copy.wait_send()

    @pl.when(far_down)
    def _():
        packet.wait_send()

    @pl.when(has_down)
    def _():
        for copy in shared:
            copy.wait_send()

    @pl.when(far_up)
    def _():
        for copy in far_shared:
            copy.wait_send()

    for copy in parts + pools:
        copy.wait_send()


def on_device(*operands):
    f32, i32 = jnp.float32, jnp.int32
    dma = pltpu.SemaphoreType.DMA
    return pl.pallas_call(
        kernel,
        out_shape=pltpu.VMEM((8, 256), f32),
        in_specs=[
            pl.BlockSpec(memory_space=pltpu.SMEM if i == 7 else pltpu.HBM)
            for i in range(10)
        ],
        out_specs=pl.BlockSpec(memory_space=pltpu.VMEM),
        scratch_shapes=[
            pltpu.VMEM((64, 512), f32),
            pltpu.VMEM((64, 192), f32),
            pltpu.VMEM((64, 64), f32),
            pltpu.VMEM((64, 64), f32),
            pltpu.VMEM((64, 256), f32),
            pltpu.VMEM((1, 512), f32),
            pltpu.VMEM((1, 512), i32),
            pltpu.VMEM((8, 256), i32),
            pltpu.VMEM((8, 576), f32),
            pltpu.VMEM((256, 512), jnp.bfloat16),
            pltpu.VMEM((64, 512), f32),
            pltpu.VMEM((1, 256), f32),
            pltpu.VMEM((8, 128), f32),
            pltpu.VMEM((8, 128), f32),
            pltpu.VMEM((8, 8, 256), f32),
            pltpu.VMEM((2, 256), f32),
            pltpu.VMEM((32, 128), f32),
            pltpu.VMEM((16, 128), f32),
            pltpu.VMEM((72, 128), f32),
            pltpu.VMEM((72, 128), f32),
            pltpu.VMEM((8, 128), f32),
            pltpu.VMEM((8, 8, 128), f32),
            pltpu.VMEM((8, 128), f32),
            pltpu.VMEM((8, 8, 128), f32),
            pltpu.VMEM((1, 256), f32),
            pltpu.VMEM((64, 256), f32),
            pltpu.VMEM((16, 64), f32),
            pltpu.VMEM((8, 8, 256), f32),
            pltpu.VMEM((8, 2, 256), f32),
            pltpu.VMEM((8, 8, 256), f32),
            pltpu.VMEM((8, 16, 128), f32),
            pltpu.VMEM((8, 16, 128), f32),
            dma((9,)),
            dma((2,)),
        ]
        + [dma((8,))] * 10
        + [dma((2,))]
        + [dma((8,))] * 4
        + [pltpu.SemaphoreType.REGULAR],
        compiler_params=pltpu.CompilerParams(collective_id=0, has_side_effects=True),
    )(*operands)


def solution(mesh):
    in_specs = (
        P("sensor", None, "cell"),
        P("sensor", None, None),
        P(),
        P(),
        P(None, "cell"),
        P("sensor", "cell"),
        P("sensor", "cell"),
        P("sensor", "cell"),
        P(None, "cell"),
        P(),
    )
    return jax.shard_map(
        on_device,
        mesh=mesh,
        in_specs=in_specs,
        out_specs=P("sensor", "cell"),
        check_vma=False,
    )
```

```python
import functools

import jax
import jax.numpy as jnp
from jax import lax
from jax.experimental import pallas as pl
from jax.experimental.pallas import tpu as pltpu
from jax.sharding import PartitionSpec as P

MESH = pl.DeviceIdType.MESH
FLOOR = -1e30
HIGH, HIGHEST = lax.Precision.HIGH, lax.Precision.HIGHEST
OFFSETS = ((1, 2), (0, 2), (1, 1), (1, 3), (0, 1), (0, 3), (1, 0))


def dot(a, b, dims=((1,), (0,)), precision=HIGHEST):
    return lax.dot_general(
        a, b, (dims, ((), ())), precision=precision, preferred_element_type=jnp.float32
    )


def lanes(values, index):
    return jnp.take_along_axis(values, index, axis=1, mode="promise_in_bounds")


def split3(x):
    high = x.astype(jnp.bfloat16).astype(jnp.float32)
    mid = (x - high).astype(jnp.bfloat16).astype(jnp.float32)
    return high, mid, x - high - mid


def full_dot(a, b):
    a0, a1, a2 = split3(a)
    b0, b1, b2 = split3(b)
    left = jnp.concatenate([a0, a0, a1, a1, a0, a2], axis=1).astype(jnp.bfloat16)
    right = jnp.concatenate([b0, b1, b0, b1, b2, b0], axis=0).astype(jnp.bfloat16)
    return dot(left, right, precision=None)


def gelu(x):
    return 0.5 * x * (1.0 + lax.erf(x * 0.7071067811865476))


def kernel(
    swath_ref,
    enc_ref,
    key_ref,
    value_ref,
    query_ref,
    quality_ref,
    cell_ref,
    live_ref,
    near_ref,
    hp_ref,
    out_ref,
    x_s,
    enc_s,
    key_s,
    value_s,
    query_s,
    quality_s,
    cell_s,
    near_s,
    hp_s,
    hot_s,
    asked_s,
    prior_s,
    tail_s,
    head_s,
    send_s,
    span_s,
    edge_s,
    early_s,
    pack_s,
    packed_s,
    token_s,
    tokens_s,
    far_s,
    fars_s,
    scale_s,
    shift_s,
    side_s,
    part_s,
    spans_s,
    pool_s,
    prev_s,
    next_s,
    in_sem,
    tail_sem,
    part_out,
    part_in,
    span_out,
    span_in,
    pool_out,
    pool_in,
    up_out,
    up_in,
    down_out,
    down_in,
    packet_sem,
    token_out,
    token_in,
    far_out,
    far_in,
    ready,
):
    s = lax.axis_index("sensor")
    c = lax.axis_index("cell")
    z, x = s // 4, s % 4
    up, down = c + 1, c - 1
    has_up, has_down = c < 63, c > 0
    far_up, far_down = has_up & (c % 16 == 15), has_down & (c % 16 == 0)

    def partner(dz, dx):
        return ((z + dz) % 2) * 4 + (x + dx) % 4

    loads = [
        pltpu.make_async_copy(source, target, in_sem.at[i])
        for i, (source, target) in enumerate(
            (
                (cell_ref, cell_s),
                (swath_ref.at[0], x_s),
                (query_ref, query_s),
                (key_ref, key_s),
                (enc_ref.at[0], enc_s),
                (quality_ref, quality_s),
                (hp_ref.at[pl.ds(pl.multiple_of(s * 8, 8), 8)], hp_s),
                (value_ref, value_s),
                (near_ref, near_s),
            )
        )
    ]
    for load in loads:
        load.start()

    barrier = pltpu.get_barrier_semaphore()
    for target, there in ((up, has_up), (down, has_down)):

        @pl.when(there)
        def _():
            pl.semaphore_signal(
                barrier, inc=1, device_id=(s, target), device_id_type=MESH
            )

    for dz, dx in OFFSETS:
        pl.semaphore_signal(
            barrier, inc=1, device_id=(partner(dz, dx), c), device_id_type=MESH
        )
    loads[0].wait()
    cell = cell_s[...]
    hot_s[...] = jnp.where(
        lax.broadcasted_iota(jnp.int32, (256, 512), 0) == cell, 1.0, 0.0
    ).astype(jnp.bfloat16)

    for i in range(1, 6):
        loads[i].wait()
    last = jnp.transpose(x_s[:, 384:512])
    row = lax.broadcasted_iota(jnp.int32, (8, 64), 0)
    head_s[...] = jnp.where(
        lax.broadcasted_iota(jnp.int32, (8, 128), 0) < 2,
        jnp.concatenate(
            [
                jnp.where(row == 0, last[126:127], last[127:128]),
                jnp.where(row == 0, last[127:128], 0.0),
            ],
            axis=1,
        ),
        0.0,
    )

    query = query_s[...]
    bilinear = full_dot(jnp.transpose(key_s[...]) * 0.125, query)
    enc = enc_s[...]
    taps = jnp.concatenate([enc[:, 0:64], enc[:, 64:128], enc[:, 128:192]], axis=0)
    mixed = full_dot(taps, x_s[...])
    found = dot(
        jnp.concatenate(split3(bilinear), axis=0).astype(jnp.bfloat16),
        hot_s[...],
        precision=None,
    )
    asked_s[...] = found[0:64] + (found[64:128] + found[128:192])
    prior_s[...] = jnp.sum(query * bilinear, axis=0, keepdims=True)

    two, one, zero = mixed[0:64], mixed[64:128], mixed[128:192]
    slot = lax.broadcasted_iota(jnp.int32, (1, 512), 1)
    one, two = pltpu.roll(one, 1, 1), pltpu.roll(two, 2, 1)
    begin = slot[:, 0:128]
    drawn = zero + jnp.concatenate(
        [
            jnp.where(begin < 1, 0.0, one[:, 0:128])
            + jnp.where(begin < 2, 0.0, two[:, 0:128]),
            one[:, 128:] + two[:, 128:],
        ],
        axis=1,
    )

    pl.semaphore_wait(
        barrier, 7 + has_up.astype(jnp.int32) + has_down.astype(jnp.int32)
    )
    tail = pltpu.make_async_remote_copy(
        src_ref=head_s,
        dst_ref=tail_s,
        send_sem=tail_sem.at[0],
        recv_sem=tail_sem.at[1],
        device_id=(s, up),
        device_id_type=MESH,
    )

    @pl.when(has_up)
    def _():
        tail.start()

    for dz, dx in OFFSETS:
        pl.semaphore_signal(
            ready, inc=1, device_id=(partner(dz, dx), c), device_id_type=MESH
        )

    @pl.when(jnp.logical_not(has_down))
    def _():
        tail_s[...] = jnp.zeros((8, 128), jnp.float32)
        prev_s[...] = jnp.ones((8, 16, 128), jnp.float32)

    @pl.when(jnp.logical_not(has_up))
    def _():
        next_s[...] = jnp.ones((8, 16, 128), jnp.float32)

    cell = cell_s[...]
    quality = quality_s[...]
    live = live_ref[0, 0]
    packet = pltpu.make_async_remote_copy(
        src_ref=pack_s,
        dst_ref=packed_s,
        send_sem=packet_sem.at[0],
        recv_sem=packet_sem.at[1],
        device_id=(s, down),
        device_id_type=MESH,
    )

    @pl.when(far_down)
    def _():
        lane = lax.broadcasted_iota(jnp.int32, (64, 128), 1)
        lane8 = lax.broadcasted_iota(jnp.int32, (8, 128), 1)
        row8 = lax.broadcasted_iota(jnp.int32, (8, 128), 0)
        pack_s[0:64] = jnp.where(
            lane < 2, drawn[:, 0:128], pltpu.roll(asked_s[:, 0:128], 2, 1)
        )
        pack_s[64:72] = jnp.where(
            row8 == 0,
            quality[:, 0:128],
            jnp.where(
                row8 == 1,
                cell[:, 0:128].astype(jnp.float32),
                jnp.where(lane8 < live, 1.0, 0.0),
            ),
        )
        packet.start()

    encoded = gelu(drawn)
    score = jnp.sum(encoded * asked_s[...], axis=0, keepdims=True)
    score = score + quality
    valid = (slot < live) & (slot >= jnp.where(has_down, 2, 0))

    hot = lax.broadcasted_iota(jnp.int32, (256, 512), 0) == cell
    masked = jnp.where(valid, score, FLOOR)
    peak = jnp.max(jnp.where(hot, masked, FLOOR), axis=1, keepdims=True)
    eye = lax.broadcasted_iota(jnp.int32, (128, 128), 0) == lax.broadcasted_iota(
        jnp.int32, (128, 128), 1
    )
    halves = [
        jnp.max(
            jnp.where(eye, peak[h * 128 : (h + 1) * 128], FLOOR), axis=0, keepdims=True
        )
        for h in range(2)
    ]
    slot_peak = []
    for b in range(4):
        index = jnp.broadcast_to(cell[:, b * 128 : (b + 1) * 128], (8, 128))
        low, high = (lanes(jnp.broadcast_to(half, (8, 128)), index & 127) for half in halves)
        slot_peak.append(jnp.where(index >= 128, high, low)[0:1])
    slot_peak = jnp.concatenate(slot_peak, axis=1)
    peak = jnp.concatenate(halves, axis=1)
    weight = jnp.where(valid, jnp.exp(score - slot_peak), 0.0)
    weighted = jnp.concatenate(
        [encoded * weight, jnp.broadcast_to(weight, (16, 512))], axis=0
    )
    one_hot = hot_s[...]
    turned = ((1,), (1,))
    high = weighted.astype(jnp.bfloat16)
    low = (weighted - high.astype(jnp.float32)).astype(jnp.bfloat16)
    sums = dot(jnp.concatenate([high, low], axis=0), one_hot, turned, None)
    sums = sums[0:80] + sums[80:160]
    query = query_s[...]
    prior = prior_s[...]
    prior = jnp.where(s == 0, prior, FLOOR)
    joint = jnp.maximum(peak, prior)
    factor = jnp.exp(peak - joint)
    prior_factor = jnp.exp(prior - joint)
    total = sums[64:65] * factor + prior_factor
    sums = sums[0:64] * factor + query * prior_factor
    peak = joint

    row = lax.broadcasted_iota(jnp.int32, (32, 256), 0)
    chosen = lax.broadcasted_iota(jnp.int32, (32, 256), 1) == (
        (row & 15) * 16 + jnp.where(row >= 16, 15, 0)
    )
    chosen = jnp.where(chosen, 1.0, 0.0)
    chosen = jnp.concatenate([chosen] * 3, axis=1).astype(jnp.bfloat16)

    def edge_rows(peak, total, sums):
        rows = jnp.concatenate(
            [sums, peak, total, jnp.zeros((62, 256), jnp.float32)], axis=0
        )
        rows = jnp.concatenate(split3(rows), axis=1).astype(jnp.bfloat16)
        return dot(chosen, rows, turned, None)

    def edge_copy(source, k, cell_to, target, out, into):
        dz, dx = (OFFSETS + ((0, 0),))[k]
        slot = dz * 4 + dx
        return pltpu.make_async_remote_copy(
            src_ref=source,
            dst_ref=target.at[slot],
            send_sem=out.at[slot],
            recv_sem=into.at[slot],
            device_id=(partner(dz, dx), cell_to),
            device_id_type=MESH,
        )

    ups = [
        edge_copy(edge_s.at[pl.ds(16, 16)], k, up, prev_s, up_out, up_in)
        for k in range(8)
    ]
    downs, far_downs = (
        [edge_copy(source, k, down, next_s, down_out, down_in) for k in range(8)]
        for source in (edge_s.at[pl.ds(0, 16)], early_s)
    )

    parts = []
    for dz, dx in OFFSETS:
        slot = dz * 4 + dx
        to = partner(dz, dx)
        for source, target, out, into in (
            (send_s.at[to], part_s.at[slot], part_out, part_in),
            (span_s, spans_s.at[slot], span_out, span_in),
        ):
            parts.append(
                pltpu.make_async_remote_copy(
                    src_ref=source,
                    dst_ref=target,
                    send_sem=out.at[slot],
                    recv_sem=into.at[slot],
                    device_id=(to, c),
                    device_id_type=MESH,
                )
            )

    shared, far_shared = (
        [
            pltpu.make_async_remote_copy(
                src_ref=source,
                dst_ref=target.at[dz * 4 + dx],
                send_sem=out.at[dz * 4 + dx],
                recv_sem=into.at[dz * 4 + dx],
                device_id=(partner(dz, dx), c),
                device_id_type=MESH,
            )
            for dz, dx in OFFSETS
        ]
        for source, target, out, into in (
            (token_s, tokens_s, token_out, token_in),
            (far_s, fars_s, far_out, far_in),
        )
    )

    def share(target, copies, made, made_score, cells):
        row = lax.broadcasted_iota(jnp.int32, (8, 64), 0)
        column = lax.broadcasted_iota(jnp.int32, (8, 64), 1)
        marks = [
            jnp.where(row == 0, one[:, 0:1], one[:, 1:2]) for one in (made_score, cells)
        ]
        target[...] = jnp.concatenate(
            [
                jnp.transpose(made)[0:8],
                jnp.where(column == 0, marks[0], jnp.where(column == 1, 1.0, marks[1])),
            ],
            axis=1,
        )
        for copy in copies:
            copy.start()

    span_s[...] = jnp.concatenate([peak, total], axis=0)
    send_s[...] = sums.reshape(8, 8, 256)
    for copy in parts:
        copy.start()

    @pl.when(far_down)
    def _():
        early_s[...] = edge_rows(peak, total, sums)[0:16]
        pl.semaphore_wait(ready, 7)
        for copy in far_downs:
            copy.start()

    @pl.when(has_down)
    def _():
        tail.wait_recv()

    parity = (lax.broadcasted_iota(jnp.int32, (64, 128), 1) & 1) == 0

    def late_tokens(rows, drawn, asked):
        made = [
            jnp.sum(enc_s[:, 0:128] * rows[t : t + 1], axis=1, keepdims=True)
            + drawn[:, t : t + 1]
            for t in range(2)
        ]
        made = gelu(jnp.where(parity, made[0], made[1]))
        asked = jnp.where(parity, asked[:, 0:1], asked[:, 1:2])
        return made, jnp.sum(made * asked, axis=0, keepdims=True)

    late, late_score = late_tokens(tail_s[...], drawn[:, 0:128], asked_s[:, 0:2])

    def share_own():
        column = lax.broadcasted_iota(jnp.int32, (1, 128), 1)
        share(
            token_s,
            shared,
            late,
            jnp.where(column < live, late_score + quality[:, 0:128], FLOOR),
            cell[:, 0:128].astype(jnp.float32),
        )

    pl.when(far_down)(share_own)
    cells = lax.broadcasted_iota(jnp.int32, (1, 256), 1)
    there = [
        (cells == cell[:, t : t + 1]) & (t < live) & has_down for t in range(2)
    ]
    scores = [
        jnp.where(there[t], late_score[:, t : t + 1] + quality[:, t : t + 1], FLOOR)
        for t in range(2)
    ]
    joint = jnp.maximum(peak, jnp.maximum(scores[0], scores[1]))
    factor = jnp.exp(peak - joint)
    total, sums = total * factor, sums * factor
    for t in range(2):
        weight = jnp.where(there[t], jnp.exp(scores[t] - joint), 0.0)
        total = total + weight
        sums = sums + late[:, t : t + 1] * weight

    edge_s[...] = edge_rows(joint, total, sums)

    @pl.when(jnp.logical_not(far_down))
    def _():
        pl.semaphore_wait(ready, 7)

    @pl.when(has_up)
    def _():
        for copy in ups:
            copy.start()

    @pl.when(has_down & jnp.logical_not(far_down))
    def _():
        for copy in downs:
            copy.start()

    pl.when(has_down & jnp.logical_not(far_down))(share_own)

    for i in range(6, 9):
        loads[i].wait()
    hp = hp_s[...]
    stacked = jnp.concatenate([hp[:, k * 64 : (k + 1) * 64] for k in range(9)], axis=0)
    stencil = dot(stacked, value_s[...])
    part0, part1, _ = split3(stencil)
    stencil_parts = jnp.concatenate([part0, part1, part0], axis=1).astype(jnp.bfloat16)
    near = near_s[...] - c * 256
    near_edge = ((near >> 4) & 15) + jnp.where(near < 0, 16, 0)
    near_side = (near < 0) | (near >= 256)

    @pl.when(far_up)
    def _():
        packet.wait_recv()
        made, made_score = late_tokens(
            head_s[...], packed_s[0:64, 0:2], packed_s[0:64, 2:4]
        )
        share(
            far_s,
            far_shared,
            made,
            jnp.where(packed_s[66:67] > 0.0, made_score + packed_s[64:65], FLOOR),
            packed_s[65:66],
        )

    for copy in parts:
        copy.wait_recv()
    blocks = [send_s[s]] + [part_s[k] for k in range(1, 8)]
    spans = [span_s[...]] + [spans_s[k] for k in range(1, 8)]
    peaks = jnp.concatenate([one[0:1] for one in spans], axis=0)
    totals = jnp.concatenate([one[1:2] for one in spans], axis=0)
    joint = jnp.max(peaks, axis=0, keepdims=True)
    factor = jnp.exp(peaks - joint)
    below = jnp.sum(totals * factor, axis=0, keepdims=True)
    pool_s[s] = sum(blocks[k] * factor[k : k + 1] for k in range(8)) / below

    pools = []
    for dz, dx in OFFSETS:
        slot = dz * 4 + dx
        copy = pltpu.make_async_remote_copy(
            src_ref=pool_s.at[s],
            dst_ref=pool_s.at[s],
            send_sem=pool_out.at[slot],
            recv_sem=pool_in.at[slot],
            device_id=(partner(dz, dx), c),
            device_id_type=MESH,
        )
        copy.start()
        pools.append(copy)

    @pl.when(has_down)
    def _():
        for copy in ups:
            copy.wait_recv()

    @pl.when(has_up)
    def _():
        for copy in downs:
            copy.wait_recv()

    def mean(blocks):
        joint = functools.reduce(jnp.maximum, blocks)[:, 64:65]
        whole = sum(block * jnp.exp(block[:, 64:65] - joint) for block in blocks)
        return whole[:, 0:64] / whole[:, 65:66]

    below_blocks = [next_s[k] for k in range(8)]

    @pl.when(jnp.logical_not(far_up))
    def _():
        side_s[...] = mean(below_blocks)

    @pl.when(far_up)
    def _():
        for copy in far_shared:
            copy.wait_recv()
        first_cell = lax.broadcasted_iota(jnp.int32, (16, 128), 0).astype(jnp.float32) * 16.0
        more = []
        for tokens in [far_s[...]] + [fars_s[k] for k in range(1, 8)]:
            for t in range(2):
                more.append(
                    jnp.where(
                        first_cell == tokens[t : t + 1, 66:67], tokens[t : t + 1], FLOOR
                    )
                )
        side_s[...] = mean(below_blocks + more)

    edges = jnp.concatenate(
        [
            side_s[...],
            mean([prev_s[k] for k in range(8)]),
            jnp.zeros((96, 64), jnp.float32),
        ],
        axis=0,
    )
    outer = dot(stencil[8:72], edges, turned, HIGH)
    outside = []
    for h in range(2):
        cut = slice(h * 128, (h + 1) * 128)
        part = jnp.zeros((8, 128), jnp.float32)
        for k in range(8):
            index = jnp.broadcast_to(near_edge[k : k + 1, cut], (8, 128))
            side = jnp.broadcast_to(near_side[k : k + 1, cut], (8, 128))
            part = part + jnp.where(
                side, lanes(outer[k * 8 : (k + 1) * 8], index), 0.0
            )
        outside.append(part)

    @pl.when(jnp.logical_not(has_down))
    def _():
        scale_s[...] = jnp.ones((1, 256), jnp.float32)
        shift_s[...] = jnp.zeros((64, 256), jnp.float32)

    @pl.when(has_down)
    def _():
        for copy in shared:
            copy.wait_recv()
        rows = jnp.concatenate(
            [token_s[0:2]] + [tokens_s[k, 0:2] for k in range(1, 8)], axis=0
        )
        cells = lax.broadcasted_iota(jnp.int32, (16, 256), 1).astype(jnp.float32)
        entries = jnp.where(cells == rows[:, 66:67], rows[:, 64:65], FLOOR)
        all_joint = jnp.maximum(joint, jnp.max(entries, axis=0, keepdims=True))
        weight = jnp.exp(entries - all_joint)
        old = below * jnp.exp(joint - all_joint)
        share_of = 1.0 / (old + jnp.sum(weight, axis=0, keepdims=True))
        scale_s[...] = old * share_of
        shift_s[...] = dot(rows[:, 0:64], weight * share_of, ((0,), (0,)))

    for copy in pools:
        copy.wait_recv()
    pooled = pool_s[...].reshape(64, 256) * scale_s[...] + shift_s[...]
    part0, part1, _ = split3(pooled)
    inner = dot(
        stencil_parts,
        jnp.concatenate([part0, part0, part1], axis=0).astype(jnp.bfloat16),
        precision=None,
    )
    for h in range(2):
        cut = slice(h * 128, (h + 1) * 128)
        joined = inner[0:8, cut] + outside[h]
        for k in range(8):
            row = inner[8 + k * 8 : 16 + k * 8]
            index = jnp.broadcast_to(near[k : k + 1, cut], (8, 128))
            side = jnp.broadcast_to(near_side[k : k + 1, cut], (8, 128))
            picked = jnp.where(
                (index & 128) > 0,
                lanes(row[:, 128:], index & 127),
                lanes(row[:, :128], index & 127),
            )
            joined = joined + jnp.where(side, 0.0, picked)
        out_ref[:, cut] = joined

    @pl.when(has_up)
    def _():
        for copy in [tail] + ups:
            copy.wait_send()

    @pl.when(has_down)
    def _():
        for copy in downs:
            copy.wait_send()

    @pl.when(far_down)
    def _():
        packet.wait_send()

    @pl.when(has_down)
    def _():
        for copy in shared:
            copy.wait_send()

    @pl.when(far_up)
    def _():
        for copy in far_shared:
            copy.wait_send()

    for copy in parts + pools:
        copy.wait_send()


def on_device(*operands):
    f32, i32 = jnp.float32, jnp.int32
    dma = pltpu.SemaphoreType.DMA
    return pl.pallas_call(
        kernel,
        out_shape=pltpu.VMEM((8, 256), f32),
        in_specs=[
            pl.BlockSpec(memory_space=pltpu.SMEM if i == 7 else pltpu.HBM)
            for i in range(10)
        ],
        out_specs=pl.BlockSpec(memory_space=pltpu.VMEM),
        scratch_shapes=[
            pltpu.VMEM((64, 512), f32),
            pltpu.VMEM((64, 192), f32),
            pltpu.VMEM((64, 64), f32),
            pltpu.VMEM((64, 64), f32),
            pltpu.VMEM((64, 256), f32),
            pltpu.VMEM((1, 512), f32),
            pltpu.VMEM((1, 512), i32),
            pltpu.VMEM((8, 256), i32),
            pltpu.VMEM((8, 576), f32),
            pltpu.VMEM((256, 512), jnp.bfloat16),
            pltpu.VMEM((64, 512), f32),
            pltpu.VMEM((1, 256), f32),
            pltpu.VMEM((8, 128), f32),
            pltpu.VMEM((8, 128), f32),
            pltpu.VMEM((8, 8, 256), f32),
            pltpu.VMEM((2, 256), f32),
            pltpu.VMEM((32, 128), f32),
            pltpu.VMEM((16, 128), f32),
            pltpu.VMEM((72, 128), f32),
            pltpu.VMEM((72, 128), f32),
            pltpu.VMEM((8, 128), f32),
            pltpu.VMEM((8, 8, 128), f32),
            pltpu.VMEM((8, 128), f32),
            pltpu.VMEM((8, 8, 128), f32),
            pltpu.VMEM((1, 256), f32),
            pltpu.VMEM((64, 256), f32),
            pltpu.VMEM((16, 64), f32),
            pltpu.VMEM((8, 8, 256), f32),
            pltpu.VMEM((8, 2, 256), f32),
            pltpu.VMEM((8, 8, 256), f32),
            pltpu.VMEM((8, 16, 128), f32),
            pltpu.VMEM((8, 16, 128), f32),
            dma((9,)),
            dma((2,)),
        ]
        + [dma((8,))] * 10
        + [dma((2,))]
        + [dma((8,))] * 4
        + [pltpu.SemaphoreType.REGULAR],
        compiler_params=pltpu.CompilerParams(collective_id=0, has_side_effects=True),
    )(*operands)


def solution(mesh):
    in_specs = (
        P("sensor", None, "cell"),
        P("sensor", None, None),
        P(),
        P(),
        P(None, "cell"),
        P("sensor", "cell"),
        P("sensor", "cell"),
        P("sensor", "cell"),
        P(None, "cell"),
        P(),
    )
    return jax.shard_map(
        on_device,
        mesh=mesh,
        in_specs=in_specs,
        out_specs=P("sensor", "cell"),
        check_vma=False,
    )
```

```python
import functools

import jax
import jax.numpy as jnp
from jax import lax
from jax.experimental import pallas as pl
from jax.experimental.pallas import tpu as pltpu
from jax.sharding import PartitionSpec as P

MESH = pl.DeviceIdType.MESH
FLOOR = -1e30
HIGH, HIGHEST = lax.Precision.HIGH, lax.Precision.HIGHEST
OFFSETS = ((1, 2), (0, 2), (1, 1), (1, 3), (0, 1), (0, 3), (1, 0))


def dot(a, b, dims=((1,), (0,)), precision=HIGHEST):
    return lax.dot_general(
        a, b, (dims, ((), ())), precision=precision, preferred_element_type=jnp.float32
    )


def lanes(values, index):
    return jnp.take_along_axis(values, index, axis=1, mode="promise_in_bounds")


def split3(x):
    high = x.astype(jnp.bfloat16).astype(jnp.float32)
    mid = (x - high).astype(jnp.bfloat16).astype(jnp.float32)
    return high, mid, x - high - mid


def full_dot(a, b):
    a0, a1, a2 = split3(a)
    b0, b1, b2 = split3(b)
    left = jnp.concatenate([a0, a0, a1, a1, a0, a2], axis=1).astype(jnp.bfloat16)
    right = jnp.concatenate([b0, b1, b0, b1, b2, b0], axis=0).astype(jnp.bfloat16)
    return dot(left, right, precision=None)


def gelu(x):
    return 0.5 * x * (1.0 + lax.erf(x * 0.7071067811865476))


def kernel(
    swath_ref,
    enc_ref,
    key_ref,
    value_ref,
    query_ref,
    quality_ref,
    cell_ref,
    live_ref,
    near_ref,
    hp_ref,
    out_ref,
    x_s,
    enc_s,
    key_s,
    value_s,
    query_s,
    quality_s,
    cell_s,
    near_s,
    hp_s,
    hot_s,
    asked_s,
    prior_s,
    tail_s,
    head_s,
    send_s,
    span_s,
    edge_s,
    early_s,
    pack_s,
    packed_s,
    token_s,
    tokens_s,
    far_s,
    fars_s,
    scale_s,
    shift_s,
    side_s,
    part_s,
    spans_s,
    pool_s,
    prev_s,
    next_s,
    in_sem,
    tail_sem,
    part_out,
    part_in,
    span_out,
    span_in,
    pool_out,
    pool_in,
    up_out,
    up_in,
    down_out,
    down_in,
    packet_sem,
    token_out,
    token_in,
    far_out,
    far_in,
    ready,
):
    s = lax.axis_index("sensor")
    c = lax.axis_index("cell")
    z, x = s // 4, s % 4
    up, down = c + 1, c - 1
    has_up, has_down = c < 63, c > 0
    far_up, far_down = has_up & (c % 16 == 15), has_down & (c % 16 == 0)

    def partner(dz, dx):
        return ((z + dz) % 2) * 4 + (x + dx) % 4

    loads = [
        pltpu.make_async_copy(source, target, in_sem.at[i])
        for i, (source, target) in enumerate(
            (
                (cell_ref, cell_s),
                (swath_ref.at[0], x_s),
                (query_ref, query_s),
                (key_ref, key_s),
                (enc_ref.at[0], enc_s),
                (quality_ref, quality_s),
                (hp_ref.at[pl.ds(pl.multiple_of(s * 8, 8), 8)], hp_s),
                (value_ref, value_s),
                (near_ref, near_s),
            )
        )
    ]
    for load in loads:
        load.start()

    barrier = pltpu.get_barrier_semaphore()
    for target, there in ((up, has_up), (down, has_down)):

        @pl.when(there)
        def _():
            pl.semaphore_signal(
                barrier, inc=1, device_id=(s, target), device_id_type=MESH
            )

    for dz, dx in OFFSETS:
        pl.semaphore_signal(
            barrier, inc=1, device_id=(partner(dz, dx), c), device_id_type=MESH
        )
    loads[0].wait()
    cell = cell_s[...]
    hot_s[...] = jnp.where(
        lax.broadcasted_iota(jnp.int32, (256, 512), 0) == cell, 1.0, 0.0
    ).astype(jnp.bfloat16)

    for i in range(1, 6):
        loads[i].wait()
    last = jnp.transpose(x_s[:, 384:512])
    row = lax.broadcasted_iota(jnp.int32, (8, 64), 0)
    head_s[...] = jnp.where(
        lax.broadcasted_iota(jnp.int32, (8, 128), 0) < 2,
        jnp.concatenate(
            [
                jnp.where(row == 0, last[126:127], last[127:128]),
                jnp.where(row == 0, last[127:128], 0.0),
            ],
            axis=1,
        ),
        0.0,
    )

    query = query_s[...]
    bilinear = full_dot(jnp.transpose(key_s[...]) * 0.125, query)
    enc = enc_s[...]
    taps = jnp.concatenate([enc[:, 0:64], enc[:, 64:128], enc[:, 128:192]], axis=0)
    mixed = full_dot(taps, x_s[...])
    found = dot(
        jnp.concatenate(split3(bilinear), axis=0).astype(jnp.bfloat16),
        hot_s[...],
        precision=None,
    )
    asked_s[...] = found[0:64] + (found[64:128] + found[128:192])
    prior_s[...] = jnp.sum(query * bilinear, axis=0, keepdims=True)

    two, one, zero = mixed[0:64], mixed[64:128], mixed[128:192]
    slot = lax.broadcasted_iota(jnp.int32, (1, 512), 1)
    one, two = pltpu.roll(one, 1, 1), pltpu.roll(two, 2, 1)
    begin = slot[:, 0:128]
    drawn = zero + jnp.concatenate(
        [
            jnp.where(begin < 1, 0.0, one[:, 0:128])
            + jnp.where(begin < 2, 0.0, two[:, 0:128]),
            one[:, 128:] + two[:, 128:],
        ],
        axis=1,
    )

    cell = cell_s[...]
    quality = quality_s[...]
    live = live_ref[0, 0]
    encoded = gelu(drawn)
    score = jnp.sum(encoded * asked_s[...], axis=0, keepdims=True)
    score = score + quality
    valid = (slot < live) & (slot >= jnp.where(has_down, 2, 0))

    hot = lax.broadcasted_iota(jnp.int32, (256, 512), 0) == cell
    masked = jnp.where(valid, score, FLOOR)
    peak = jnp.max(jnp.where(hot, masked, FLOOR), axis=1, keepdims=True)
    eye = lax.broadcasted_iota(jnp.int32, (128, 128), 0) == lax.broadcasted_iota(
        jnp.int32, (128, 128), 1
    )
    halves = [
        jnp.max(
            jnp.where(eye, peak[h * 128 : (h + 1) * 128], FLOOR), axis=0, keepdims=True
        )
        for h in range(2)
    ]
    slot_peak = []
    for b in range(4):
        index = jnp.broadcast_to(cell[:, b * 128 : (b + 1) * 128], (8, 128))
        low, high = (lanes(jnp.broadcast_to(half, (8, 128)), index & 127) for half in halves)
        slot_peak.append(jnp.where(index >= 128, high, low)[0:1])
    slot_peak = jnp.concatenate(slot_peak, axis=1)
    peak = jnp.concatenate(halves, axis=1)
    weight = jnp.where(valid, jnp.exp(score - slot_peak), 0.0)
    weighted = jnp.concatenate(
        [encoded * weight, jnp.broadcast_to(weight, (16, 512))], axis=0
    )
    one_hot = hot_s[...]
    turned = ((1,), (1,))
    high = weighted.astype(jnp.bfloat16)
    low = (weighted - high.astype(jnp.float32)).astype(jnp.bfloat16)
    sums = dot(jnp.concatenate([high, low], axis=0), one_hot, turned, None)
    sums = sums[0:80] + sums[80:160]
    query = query_s[...]
    prior = prior_s[...]
    prior = jnp.where(s == 0, prior, FLOOR)
    joint = jnp.maximum(peak, prior)
    factor = jnp.exp(peak - joint)
    prior_factor = jnp.exp(prior - joint)
    total = sums[64:65] * factor + prior_factor
    sums = sums[0:64] * factor + query * prior_factor
    peak = joint

    span_s[...] = jnp.concatenate([peak, total], axis=0)
    send_s[...] = sums.reshape(8, 8, 256)

    @pl.when(far_down)
    def _():
        lane = lax.broadcasted_iota(jnp.int32, (64, 128), 1)
        lane8 = lax.broadcasted_iota(jnp.int32, (8, 128), 1)
        row8 = lax.broadcasted_iota(jnp.int32, (8, 128), 0)
        pack_s[0:64] = jnp.where(
            lane < 2, drawn[:, 0:128], pltpu.roll(asked_s[:, 0:128], 2, 1)
        )
        pack_s[64:72] = jnp.where(
            row8 == 0,
            quality[:, 0:128],
            jnp.where(
                row8 == 1,
                cell[:, 0:128].astype(jnp.float32),
                jnp.where(lane8 < live, 1.0, 0.0),
            ),
        )

    pl.semaphore_wait(
        barrier, 7 + has_up.astype(jnp.int32) + has_down.astype(jnp.int32)
    )
    tail = pltpu.make_async_remote_copy(
        src_ref=head_s,
        dst_ref=tail_s,
        send_sem=tail_sem.at[0],
        recv_sem=tail_sem.at[1],
        device_id=(s, up),
        device_id_type=MESH,
    )

    @pl.when(has_up)
    def _():
        tail.start()

    packet = pltpu.make_async_remote_copy(
        src_ref=pack_s,
        dst_ref=packed_s,
        send_sem=packet_sem.at[0],
        recv_sem=packet_sem.at[1],
        device_id=(s, down),
        device_id_type=MESH,
    )

    @pl.when(far_down)
    def _():
        packet.start()

    for dz, dx in OFFSETS:
        pl.semaphore_signal(
            ready, inc=1, device_id=(partner(dz, dx), c), device_id_type=MESH
        )

    @pl.when(jnp.logical_not(has_down))
    def _():
        tail_s[...] = jnp.zeros((8, 128), jnp.float32)
        prev_s[...] = jnp.ones((8, 16, 128), jnp.float32)

    @pl.when(jnp.logical_not(has_up))
    def _():
        next_s[...] = jnp.ones((8, 16, 128), jnp.float32)

    row = lax.broadcasted_iota(jnp.int32, (32, 256), 0)
    chosen = lax.broadcasted_iota(jnp.int32, (32, 256), 1) == (
        (row & 15) * 16 + jnp.where(row >= 16, 15, 0)
    )
    chosen = jnp.where(chosen, 1.0, 0.0)
    chosen = jnp.concatenate([chosen] * 3, axis=1).astype(jnp.bfloat16)

    def edge_rows(peak, total, sums):
        rows = jnp.concatenate(
            [sums, peak, total, jnp.zeros((62, 256), jnp.float32)], axis=0
        )
        rows = jnp.concatenate(split3(rows), axis=1).astype(jnp.bfloat16)
        return dot(chosen, rows, turned, None)

    def edge_copy(source, k, cell_to, target, out, into):
        dz, dx = (OFFSETS + ((0, 0),))[k]
        slot = dz * 4 + dx
        return pltpu.make_async_remote_copy(
            src_ref=source,
            dst_ref=target.at[slot],
            send_sem=out.at[slot],
            recv_sem=into.at[slot],
            device_id=(partner(dz, dx), cell_to),
            device_id_type=MESH,
        )

    ups = [
        edge_copy(edge_s.at[pl.ds(16, 16)], k, up, prev_s, up_out, up_in)
        for k in range(8)
    ]
    downs, far_downs = (
        [edge_copy(source, k, down, next_s, down_out, down_in) for k in range(8)]
        for source in (edge_s.at[pl.ds(0, 16)], early_s)
    )

    parts = []
    for dz, dx in OFFSETS:
        slot = dz * 4 + dx
        to = partner(dz, dx)
        for source, target, out, into in (
            (send_s.at[to], part_s.at[slot], part_out, part_in),
            (span_s, spans_s.at[slot], span_out, span_in),
        ):
            parts.append(
                pltpu.make_async_remote_copy(
                    src_ref=source,
                    dst_ref=target,
                    send_sem=out.at[slot],
                    recv_sem=into.at[slot],
                    device_id=(to, c),
                    device_id_type=MESH,
                )
            )

    shared, far_shared = (
        [
            pltpu.make_async_remote_copy(
                src_ref=source,
                dst_ref=target.at[dz * 4 + dx],
                send_sem=out.at[dz * 4 + dx],
                recv_sem=into.at[dz * 4 + dx],
                device_id=(partner(dz, dx), c),
                device_id_type=MESH,
            )
            for dz, dx in OFFSETS
        ]
        for source, target, out, into in (
            (token_s, tokens_s, token_out, token_in),
            (far_s, fars_s, far_out, far_in),
        )
    )

    def share(target, copies, made, made_score, cells):
        row = lax.broadcasted_iota(jnp.int32, (8, 64), 0)
        column = lax.broadcasted_iota(jnp.int32, (8, 64), 1)
        marks = [
            jnp.where(row == 0, one[:, 0:1], one[:, 1:2]) for one in (made_score, cells)
        ]
        target[...] = jnp.concatenate(
            [
                jnp.transpose(made)[0:8],
                jnp.where(column == 0, marks[0], jnp.where(column == 1, 1.0, marks[1])),
            ],
            axis=1,
        )
        for copy in copies:
            copy.start()

    for copy in parts:
        copy.start()

    @pl.when(far_down)
    def _():
        early_s[...] = edge_rows(peak, total, sums)[0:16]
        pl.semaphore_wait(ready, 7)
        for copy in far_downs:
            copy.start()

    @pl.when(has_down)
    def _():
        tail.wait_recv()

    parity = (lax.broadcasted_iota(jnp.int32, (64, 128), 1) & 1) == 0

    def late_tokens(rows, drawn, asked):
        made = [
            jnp.sum(enc_s[:, 0:128] * rows[t : t + 1], axis=1, keepdims=True)
            + drawn[:, t : t + 1]
            for t in range(2)
        ]
        made = gelu(jnp.where(parity, made[0], made[1]))
        asked = jnp.where(parity, asked[:, 0:1], asked[:, 1:2])
        return made, jnp.sum(made * asked, axis=0, keepdims=True)

    late, late_score = late_tokens(tail_s[...], drawn[:, 0:128], asked_s[:, 0:2])

    def share_own():
        column = lax.broadcasted_iota(jnp.int32, (1, 128), 1)
        share(
            token_s,
            shared,
            late,
            jnp.where(column < live, late_score + quality[:, 0:128], FLOOR),
            cell[:, 0:128].astype(jnp.float32),
        )

    pl.when(far_down)(share_own)
    cells = lax.broadcasted_iota(jnp.int32, (1, 256), 1)
    there = [
        (cells == cell[:, t : t + 1]) & (t < live) & has_down for t in range(2)
    ]
    scores = [
        jnp.where(there[t], late_score[:, t : t + 1] + quality[:, t : t + 1], FLOOR)
        for t in range(2)
    ]
    joint = jnp.maximum(peak, jnp.maximum(scores[0], scores[1]))
    factor = jnp.exp(peak - joint)
    total, sums = total * factor, sums * factor
    for t in range(2):
        weight = jnp.where(there[t], jnp.exp(scores[t] - joint), 0.0)
        total = total + weight
        sums = sums + late[:, t : t + 1] * weight

    edge_s[...] = edge_rows(joint, total, sums)

    @pl.when(jnp.logical_not(far_down))
    def _():
        pl.semaphore_wait(ready, 7)

    @pl.when(has_up)
    def _():
        for copy in ups:
            copy.start()

    @pl.when(has_down & jnp.logical_not(far_down))
    def _():
        for copy in downs:
            copy.start()

    pl.when(has_down & jnp.logical_not(far_down))(share_own)

    for i in range(6, 9):
        loads[i].wait()
    hp = hp_s[...]
    stacked = jnp.concatenate([hp[:, k * 64 : (k + 1) * 64] for k in range(9)], axis=0)
    stencil = dot(stacked, value_s[...])
    part0, part1, _ = split3(stencil)
    stencil_parts = jnp.concatenate([part0, part1, part0], axis=1).astype(jnp.bfloat16)
    near = near_s[...] - c * 256
    near_edge = ((near >> 4) & 15) + jnp.where(near < 0, 16, 0)
    near_side = (near < 0) | (near >= 256)

    @pl.when(far_up)
    def _():
        packet.wait_recv()
        made, made_score = late_tokens(
            head_s[...], packed_s[0:64, 0:2], packed_s[0:64, 2:4]
        )
        share(
            far_s,
            far_shared,
            made,
            jnp.where(packed_s[66:67] > 0.0, made_score + packed_s[64:65], FLOOR),
            packed_s[65:66],
        )

    for copy in parts:
        copy.wait_recv()
    blocks = [send_s[s]] + [part_s[k] for k in range(1, 8)]
    spans = [span_s[...]] + [spans_s[k] for k in range(1, 8)]
    peaks = jnp.concatenate([one[0:1] for one in spans], axis=0)
    totals = jnp.concatenate([one[1:2] for one in spans], axis=0)
    joint = jnp.max(peaks, axis=0, keepdims=True)
    factor = jnp.exp(peaks - joint)
    below = jnp.sum(totals * factor, axis=0, keepdims=True)
    pool_s[s] = sum(blocks[k] * factor[k : k + 1] for k in range(8)) / below

    pools = []
    for dz, dx in OFFSETS:
        slot = dz * 4 + dx
        copy = pltpu.make_async_remote_copy(
            src_ref=pool_s.at[s],
            dst_ref=pool_s.at[s],
            send_sem=pool_out.at[slot],
            recv_sem=pool_in.at[slot],
            device_id=(partner(dz, dx), c),
            device_id_type=MESH,
        )
        copy.start()
        pools.append(copy)

    @pl.when(jnp.logical_not(has_down))
    def _():
        scale_s[...] = jnp.ones((1, 256), jnp.float32)
        shift_s[...] = jnp.zeros((64, 256), jnp.float32)

    @pl.when(has_down)
    def _():
        for copy in shared:
            copy.wait_recv()
        rows = jnp.concatenate(
            [token_s[0:2]] + [tokens_s[k, 0:2] for k in range(1, 8)], axis=0
        )
        cells = lax.broadcasted_iota(jnp.int32, (16, 256), 1).astype(jnp.float32)
        entries = jnp.where(cells == rows[:, 66:67], rows[:, 64:65], FLOOR)
        all_joint = jnp.maximum(joint, jnp.max(entries, axis=0, keepdims=True))
        weight = jnp.exp(entries - all_joint)
        old = below * jnp.exp(joint - all_joint)
        share_of = 1.0 / (old + jnp.sum(weight, axis=0, keepdims=True))
        scale_s[...] = old * share_of
        shift_s[...] = dot(rows[:, 0:64], weight * share_of, ((0,), (0,)))

    @pl.when(has_down)
    def _():
        for copy in ups:
            copy.wait_recv()

    @pl.when(has_up)
    def _():
        for copy in downs:
            copy.wait_recv()

    def mean(blocks):
        joint = functools.reduce(jnp.maximum, blocks)[:, 64:65]
        whole = sum(block * jnp.exp(block[:, 64:65] - joint) for block in blocks)
        return whole[:, 0:64] / whole[:, 65:66]

    below_blocks = [next_s[k] for k in range(8)]

    @pl.when(jnp.logical_not(far_up))
    def _():
        side_s[...] = mean(below_blocks)

    @pl.when(far_up)
    def _():
        for copy in far_shared:
            copy.wait_recv()
        first_cell = lax.broadcasted_iota(jnp.int32, (16, 128), 0).astype(jnp.float32) * 16.0
        more = []
        for tokens in [far_s[...]] + [fars_s[k] for k in range(1, 8)]:
            for t in range(2):
                more.append(
                    jnp.where(
                        first_cell == tokens[t : t + 1, 66:67], tokens[t : t + 1], FLOOR
                    )
                )
        side_s[...] = mean(below_blocks + more)

    edges = jnp.concatenate(
        [
            side_s[...],
            mean([prev_s[k] for k in range(8)]),
            jnp.zeros((96, 64), jnp.float32),
        ],
        axis=0,
    )
    outer = dot(stencil[8:72], edges, turned, HIGH)
    outside = []
    for h in range(2):
        cut = slice(h * 128, (h + 1) * 128)
        part = jnp.zeros((8, 128), jnp.float32)
        for k in range(8):
            index = jnp.broadcast_to(near_edge[k : k + 1, cut], (8, 128))
            side = jnp.broadcast_to(near_side[k : k + 1, cut], (8, 128))
            part = part + jnp.where(
                side, lanes(outer[k * 8 : (k + 1) * 8], index), 0.0
            )
        outside.append(part)

    for copy in pools:
        copy.wait_recv()
    pooled = pool_s[...].reshape(64, 256) * scale_s[...] + shift_s[...]
    part0, part1, _ = split3(pooled)
    inner = dot(
        stencil_parts,
        jnp.concatenate([part0, part0, part1], axis=0).astype(jnp.bfloat16),
        precision=None,
    )
    for h in range(2):
        cut = slice(h * 128, (h + 1) * 128)
        joined = inner[0:8, cut] + outside[h]
        for k in range(8):
            row = inner[8 + k * 8 : 16 + k * 8]
            index = jnp.broadcast_to(near[k : k + 1, cut], (8, 128))
            side = jnp.broadcast_to(near_side[k : k + 1, cut], (8, 128))
            picked = jnp.where(
                (index & 128) > 0,
                lanes(row[:, 128:], index & 127),
                lanes(row[:, :128], index & 127),
            )
            joined = joined + jnp.where(side, 0.0, picked)
        out_ref[:, cut] = joined

    @pl.when(has_up)
    def _():
        for copy in [tail] + ups:
            copy.wait_send()

    @pl.when(has_down)
    def _():
        for copy in downs:
            copy.wait_send()

    @pl.when(far_down)
    def _():
        packet.wait_send()

    @pl.when(has_down)
    def _():
        for copy in shared:
            copy.wait_send()

    @pl.when(far_up)
    def _():
        for copy in far_shared:
            copy.wait_send()

    for copy in parts + pools:
        copy.wait_send()


def on_device(*operands):
    f32, i32 = jnp.float32, jnp.int32
    dma = pltpu.SemaphoreType.DMA
    return pl.pallas_call(
        kernel,
        out_shape=pltpu.VMEM((8, 256), f32),
        in_specs=[
            pl.BlockSpec(memory_space=pltpu.SMEM if i == 7 else pltpu.HBM)
            for i in range(10)
        ],
        out_specs=pl.BlockSpec(memory_space=pltpu.VMEM),
        scratch_shapes=[
            pltpu.VMEM((64, 512), f32),
            pltpu.VMEM((64, 192), f32),
            pltpu.VMEM((64, 64), f32),
            pltpu.VMEM((64, 64), f32),
            pltpu.VMEM((64, 256), f32),
            pltpu.VMEM((1, 512), f32),
            pltpu.VMEM((1, 512), i32),
            pltpu.VMEM((8, 256), i32),
            pltpu.VMEM((8, 576), f32),
            pltpu.VMEM((256, 512), jnp.bfloat16),
            pltpu.VMEM((64, 512), f32),
            pltpu.VMEM((1, 256), f32),
            pltpu.VMEM((8, 128), f32),
            pltpu.VMEM((8, 128), f32),
            pltpu.VMEM((8, 8, 256), f32),
            pltpu.VMEM((2, 256), f32),
            pltpu.VMEM((32, 128), f32),
            pltpu.VMEM((16, 128), f32),
            pltpu.VMEM((72, 128), f32),
            pltpu.VMEM((72, 128), f32),
            pltpu.VMEM((8, 128), f32),
            pltpu.VMEM((8, 8, 128), f32),
            pltpu.VMEM((8, 128), f32),
            pltpu.VMEM((8, 8, 128), f32),
            pltpu.VMEM((1, 256), f32),
            pltpu.VMEM((64, 256), f32),
            pltpu.VMEM((16, 64), f32),
            pltpu.VMEM((8, 8, 256), f32),
            pltpu.VMEM((8, 2, 256), f32),
            pltpu.VMEM((8, 8, 256), f32),
            pltpu.VMEM((8, 16, 128), f32),
            pltpu.VMEM((8, 16, 128), f32),
            dma((9,)),
            dma((2,)),
        ]
        + [dma((8,))] * 10
        + [dma((2,))]
        + [dma((8,))] * 4
        + [pltpu.SemaphoreType.REGULAR],
        compiler_params=pltpu.CompilerParams(collective_id=0, has_side_effects=True),
    )(*operands)


def solution(mesh):
    in_specs = (
        P("sensor", None, "cell"),
        P("sensor", None, None),
        P(),
        P(),
        P(None, "cell"),
        P("sensor", "cell"),
        P("sensor", "cell"),
        P("sensor", "cell"),
        P(None, "cell"),
        P(),
    )
    return jax.shard_map(
        on_device,
        mesh=mesh,
        in_specs=in_specs,
        out_specs=P("sensor", "cell"),
        check_vma=False,
    )
```

```python
import functools

import jax
import jax.numpy as jnp
from jax import lax
from jax.experimental import pallas as pl
from jax.experimental.pallas import tpu as pltpu
from jax.sharding import PartitionSpec as P

MESH = pl.DeviceIdType.MESH
FLOOR = -1e30
HIGH, HIGHEST = lax.Precision.HIGH, lax.Precision.HIGHEST
OFFSETS = ((1, 2), (0, 2), (1, 1), (1, 3), (0, 1), (0, 3), (1, 0))


def dot(a, b, dims=((1,), (0,)), precision=HIGHEST):
    return lax.dot_general(
        a, b, (dims, ((), ())), precision=precision, preferred_element_type=jnp.float32
    )


def lanes(values, index):
    return jnp.take_along_axis(values, index, axis=1, mode="promise_in_bounds")


def split3(x):
    high = x.astype(jnp.bfloat16).astype(jnp.float32)
    mid = (x - high).astype(jnp.bfloat16).astype(jnp.float32)
    return high, mid, x - high - mid


def full_dot(a, b):
    a0, a1, a2 = split3(a)
    b0, b1, b2 = split3(b)
    left = jnp.concatenate([a0, a0, a1, a1, a0, a2], axis=1).astype(jnp.bfloat16)
    right = jnp.concatenate([b0, b1, b0, b1, b2, b0], axis=0).astype(jnp.bfloat16)
    return dot(left, right, precision=None)


def gelu(x):
    return 0.5 * x * (1.0 + lax.erf(x * 0.7071067811865476))


def kernel(
    swath_ref,
    enc_ref,
    key_ref,
    value_ref,
    query_ref,
    quality_ref,
    cell_ref,
    live_ref,
    near_ref,
    hp_ref,
    out_ref,
    x_s,
    enc_s,
    key_s,
    value_s,
    query_s,
    quality_s,
    cell_s,
    near_s,
    hp_s,
    hot_s,
    asked_s,
    prior_s,
    tail_s,
    head_s,
    send_s,
    span_s,
    edge_s,
    early_s,
    pack_s,
    packed_s,
    token_s,
    tokens_s,
    far_s,
    fars_s,
    scale_s,
    shift_s,
    side_s,
    part_s,
    spans_s,
    pool_s,
    prev_s,
    next_s,
    in_sem,
    tail_sem,
    part_out,
    part_in,
    span_out,
    span_in,
    pool_out,
    pool_in,
    up_out,
    up_in,
    down_out,
    down_in,
    packet_sem,
    token_out,
    token_in,
    far_out,
    far_in,
    ready,
):
    s = lax.axis_index("sensor")
    c = lax.axis_index("cell")
    z, x = s // 4, s % 4
    up, down = c + 1, c - 1
    has_up, has_down = c < 63, c > 0
    far_up, far_down = has_up & (c % 16 == 15), has_down & (c % 16 == 0)

    def partner(dz, dx):
        return ((z + dz) % 2) * 4 + (x + dx) % 4

    loads = [
        pltpu.make_async_copy(source, target, in_sem.at[i])
        for i, (source, target) in enumerate(
            (
                (cell_ref, cell_s),
                (swath_ref.at[0], x_s),
                (query_ref, query_s),
                (key_ref, key_s),
                (enc_ref.at[0], enc_s),
                (quality_ref, quality_s),
                (hp_ref.at[pl.ds(pl.multiple_of(s * 8, 8), 8)], hp_s),
                (value_ref, value_s),
                (near_ref, near_s),
            )
        )
    ]
    for load in loads:
        load.start()

    barrier = pltpu.get_barrier_semaphore()
    for dz, dx in OFFSETS:
        pl.semaphore_signal(
            barrier, inc=1, device_id=(partner(dz, dx), c), device_id_type=MESH
        )
    loads[0].wait()
    cell = cell_s[...]
    hot_s[...] = jnp.where(
        lax.broadcasted_iota(jnp.int32, (256, 512), 0) == cell, 1.0, 0.0
    ).astype(jnp.bfloat16)

    for i in range(1, 6):
        loads[i].wait()
    last = jnp.transpose(x_s[:, 384:512])
    row = lax.broadcasted_iota(jnp.int32, (8, 64), 0)
    head_s[...] = jnp.where(
        lax.broadcasted_iota(jnp.int32, (8, 128), 0) < 2,
        jnp.concatenate(
            [
                jnp.where(row == 0, last[126:127], last[127:128]),
                jnp.where(row == 0, last[127:128], 0.0),
            ],
            axis=1,
        ),
        0.0,
    )

    query = query_s[...]
    bilinear = full_dot(jnp.transpose(key_s[...]) * 0.125, query)
    enc = enc_s[...]
    taps = jnp.concatenate([enc[:, 0:64], enc[:, 64:128], enc[:, 128:192]], axis=0)
    mixed = full_dot(taps, x_s[...])
    found = dot(
        jnp.concatenate(split3(bilinear), axis=0).astype(jnp.bfloat16),
        hot_s[...],
        precision=None,
    )
    asked_s[...] = found[0:64] + (found[64:128] + found[128:192])
    prior_s[...] = jnp.sum(query * bilinear, axis=0, keepdims=True)

    two, one, zero = mixed[0:64], mixed[64:128], mixed[128:192]
    slot = lax.broadcasted_iota(jnp.int32, (1, 512), 1)
    one, two = pltpu.roll(one, 1, 1), pltpu.roll(two, 2, 1)
    begin = slot[:, 0:128]
    drawn = zero + jnp.concatenate(
        [
            jnp.where(begin < 1, 0.0, one[:, 0:128])
            + jnp.where(begin < 2, 0.0, two[:, 0:128]),
            one[:, 128:] + two[:, 128:],
        ],
        axis=1,
    )

    cell = cell_s[...]
    quality = quality_s[...]
    live = live_ref[0, 0]
    encoded = gelu(drawn)
    score = jnp.sum(encoded * asked_s[...], axis=0, keepdims=True)
    score = score + quality
    valid = (slot < live) & (slot >= jnp.where(has_down, 2, 0))

    hot = lax.broadcasted_iota(jnp.int32, (256, 512), 0) == cell
    masked = jnp.where(valid, score, FLOOR)
    peak = jnp.max(jnp.where(hot, masked, FLOOR), axis=1, keepdims=True)
    eye = lax.broadcasted_iota(jnp.int32, (128, 128), 0) == lax.broadcasted_iota(
        jnp.int32, (128, 128), 1
    )
    halves = [
        jnp.max(
            jnp.where(eye, peak[h * 128 : (h + 1) * 128], FLOOR), axis=0, keepdims=True
        )
        for h in range(2)
    ]
    slot_peak = []
    for b in range(4):
        index = jnp.broadcast_to(cell[:, b * 128 : (b + 1) * 128], (8, 128))
        low, high = (lanes(jnp.broadcast_to(half, (8, 128)), index & 127) for half in halves)
        slot_peak.append(jnp.where(index >= 128, high, low)[0:1])
    slot_peak = jnp.concatenate(slot_peak, axis=1)
    peak = jnp.concatenate(halves, axis=1)
    weight = jnp.where(valid, jnp.exp(score - slot_peak), 0.0)
    weighted = jnp.concatenate(
        [encoded * weight, jnp.broadcast_to(weight, (16, 512))], axis=0
    )
    one_hot = hot_s[...]
    turned = ((1,), (1,))
    high = weighted.astype(jnp.bfloat16)
    low = (weighted - high.astype(jnp.float32)).astype(jnp.bfloat16)
    sums = dot(jnp.concatenate([high, low], axis=0), one_hot, turned, None)
    sums = sums[0:80] + sums[80:160]
    query = query_s[...]
    prior = prior_s[...]
    prior = jnp.where(s == 0, prior, FLOOR)
    joint = jnp.maximum(peak, prior)
    factor = jnp.exp(peak - joint)
    prior_factor = jnp.exp(prior - joint)
    total = sums[64:65] * factor + prior_factor
    sums = sums[0:64] * factor + query * prior_factor
    peak = joint

    span_s[...] = jnp.concatenate([peak, total], axis=0)
    send_s[...] = sums.reshape(8, 8, 256)

    @pl.when(far_down)
    def _():
        lane = lax.broadcasted_iota(jnp.int32, (64, 128), 1)
        lane8 = lax.broadcasted_iota(jnp.int32, (8, 128), 1)
        row8 = lax.broadcasted_iota(jnp.int32, (8, 128), 0)
        pack_s[0:64] = jnp.where(
            lane < 2, drawn[:, 0:128], pltpu.roll(asked_s[:, 0:128], 2, 1)
        )
        pack_s[64:72] = jnp.where(
            row8 == 0,
            quality[:, 0:128],
            jnp.where(
                row8 == 1,
                cell[:, 0:128].astype(jnp.float32),
                jnp.where(lane8 < live, 1.0, 0.0),
            ),
        )

    beside = has_up.astype(jnp.int32) + has_down.astype(jnp.int32)
    pl.semaphore_wait(barrier, 7 + (1 - c % 2) * beside)
    for target, there in ((up, has_up), (down, has_down)):

        @pl.when(there)
        def _():
            pl.semaphore_signal(
                barrier, inc=1, device_id=(s, target), device_id_type=MESH
            )

    parts = []
    for dz, dx in OFFSETS:
        slot = dz * 4 + dx
        to = partner(dz, dx)
        for source, target, out, into in (
            (send_s.at[to], part_s.at[slot], part_out, part_in),
            (span_s, spans_s.at[slot], span_out, span_in),
        ):
            parts.append(
                pltpu.make_async_remote_copy(
                    src_ref=source,
                    dst_ref=target,
                    send_sem=out.at[slot],
                    recv_sem=into.at[slot],
                    device_id=(to, c),
                    device_id_type=MESH,
                )
            )

    for copy in parts:
        copy.start()

    @pl.when(c % 2 == 1)
    def _():
        pl.semaphore_wait(barrier, beside)

    tail = pltpu.make_async_remote_copy(
        src_ref=head_s,
        dst_ref=tail_s,
        send_sem=tail_sem.at[0],
        recv_sem=tail_sem.at[1],
        device_id=(s, up),
        device_id_type=MESH,
    )

    @pl.when(has_up)
    def _():
        tail.start()

    packet = pltpu.make_async_remote_copy(
        src_ref=pack_s,
        dst_ref=packed_s,
        send_sem=packet_sem.at[0],
        recv_sem=packet_sem.at[1],
        device_id=(s, down),
        device_id_type=MESH,
    )

    @pl.when(far_down)
    def _():
        packet.start()

    for dz, dx in OFFSETS:
        pl.semaphore_signal(
            ready, inc=1, device_id=(partner(dz, dx), c), device_id_type=MESH
        )

    @pl.when(jnp.logical_not(has_down))
    def _():
        tail_s[...] = jnp.zeros((8, 128), jnp.float32)
        prev_s[...] = jnp.ones((8, 16, 128), jnp.float32)

    @pl.when(jnp.logical_not(has_up))
    def _():
        next_s[...] = jnp.ones((8, 16, 128), jnp.float32)

    row = lax.broadcasted_iota(jnp.int32, (32, 256), 0)
    chosen = lax.broadcasted_iota(jnp.int32, (32, 256), 1) == (
        (row & 15) * 16 + jnp.where(row >= 16, 15, 0)
    )
    chosen = jnp.where(chosen, 1.0, 0.0)
    chosen = jnp.concatenate([chosen] * 3, axis=1).astype(jnp.bfloat16)

    def edge_rows(peak, total, sums):
        rows = jnp.concatenate(
            [sums, peak, total, jnp.zeros((62, 256), jnp.float32)], axis=0
        )
        rows = jnp.concatenate(split3(rows), axis=1).astype(jnp.bfloat16)
        return dot(chosen, rows, turned, None)

    def edge_copy(source, k, cell_to, target, out, into):
        dz, dx = (OFFSETS + ((0, 0),))[k]
        slot = dz * 4 + dx
        return pltpu.make_async_remote_copy(
            src_ref=source,
            dst_ref=target.at[slot],
            send_sem=out.at[slot],
            recv_sem=into.at[slot],
            device_id=(partner(dz, dx), cell_to),
            device_id_type=MESH,
        )

    ups = [
        edge_copy(edge_s.at[pl.ds(16, 16)], k, up, prev_s, up_out, up_in)
        for k in range(8)
    ]
    downs, far_downs = (
        [edge_copy(source, k, down, next_s, down_out, down_in) for k in range(8)]
        for source in (edge_s.at[pl.ds(0, 16)], early_s)
    )

    shared, far_shared = (
        [
            pltpu.make_async_remote_copy(
                src_ref=source,
                dst_ref=target.at[dz * 4 + dx],
                send_sem=out.at[dz * 4 + dx],
                recv_sem=into.at[dz * 4 + dx],
                device_id=(partner(dz, dx), c),
                device_id_type=MESH,
            )
            for dz, dx in OFFSETS
        ]
        for source, target, out, into in (
            (token_s, tokens_s, token_out, token_in),
            (far_s, fars_s, far_out, far_in),
        )
    )

    def share(target, copies, made, made_score, cells):
        row = lax.broadcasted_iota(jnp.int32, (8, 64), 0)
        column = lax.broadcasted_iota(jnp.int32, (8, 64), 1)
        marks = [
            jnp.where(row == 0, one[:, 0:1], one[:, 1:2]) for one in (made_score, cells)
        ]
        target[...] = jnp.concatenate(
            [
                jnp.transpose(made)[0:8],
                jnp.where(column == 0, marks[0], jnp.where(column == 1, 1.0, marks[1])),
            ],
            axis=1,
        )
        for copy in copies:
            copy.start()

    @pl.when(far_down)
    def _():
        early_s[...] = edge_rows(peak, total, sums)[0:16]
        pl.semaphore_wait(ready, 7)
        for copy in far_downs:
            copy.start()

    @pl.when(has_down)
    def _():
        tail.wait_recv()

    parity = (lax.broadcasted_iota(jnp.int32, (64, 128), 1) & 1) == 0

    def late_tokens(rows, drawn, asked):
        made = [
            jnp.sum(enc_s[:, 0:128] * rows[t : t + 1], axis=1, keepdims=True)
            + drawn[:, t : t + 1]
            for t in range(2)
        ]
        made = gelu(jnp.where(parity, made[0], made[1]))
        asked = jnp.where(parity, asked[:, 0:1], asked[:, 1:2])
        return made, jnp.sum(made * asked, axis=0, keepdims=True)

    late, late_score = late_tokens(tail_s[...], drawn[:, 0:128], asked_s[:, 0:2])

    def share_own():
        column = lax.broadcasted_iota(jnp.int32, (1, 128), 1)
        share(
            token_s,
            shared,
            late,
            jnp.where(column < live, late_score + quality[:, 0:128], FLOOR),
            cell[:, 0:128].astype(jnp.float32),
        )

    pl.when(far_down)(share_own)
    cells = lax.broadcasted_iota(jnp.int32, (1, 256), 1)
    there = [
        (cells == cell[:, t : t + 1]) & (t < live) & has_down for t in range(2)
    ]
    scores = [
        jnp.where(there[t], late_score[:, t : t + 1] + quality[:, t : t + 1], FLOOR)
        for t in range(2)
    ]
    joint = jnp.maximum(peak, jnp.maximum(scores[0], scores[1]))
    factor = jnp.exp(peak - joint)
    total, sums = total * factor, sums * factor
    for t in range(2):
        weight = jnp.where(there[t], jnp.exp(scores[t] - joint), 0.0)
        total = total + weight
        sums = sums + late[:, t : t + 1] * weight

    edge_s[...] = edge_rows(joint, total, sums)

    @pl.when(jnp.logical_not(far_down))
    def _():
        pl.semaphore_wait(ready, 7)

    @pl.when(has_up)
    def _():
        for copy in ups:
            copy.start()

    @pl.when(has_down & jnp.logical_not(far_down))
    def _():
        for copy in downs:
            copy.start()

    pl.when(has_down & jnp.logical_not(far_down))(share_own)

    for i in range(6, 9):
        loads[i].wait()
    hp = hp_s[...]
    stacked = jnp.concatenate([hp[:, k * 64 : (k + 1) * 64] for k in range(9)], axis=0)
    stencil = dot(stacked, value_s[...])
    part0, part1, _ = split3(stencil)
    stencil_parts = jnp.concatenate([part0, part1, part0], axis=1).astype(jnp.bfloat16)
    near = near_s[...] - c * 256
    near_edge = ((near >> 4) & 15) + jnp.where(near < 0, 16, 0)
    near_side = (near < 0) | (near >= 256)

    @pl.when(far_up)
    def _():
        packet.wait_recv()
        made, made_score = late_tokens(
            head_s[...], packed_s[0:64, 0:2], packed_s[0:64, 2:4]
        )
        share(
            far_s,
            far_shared,
            made,
            jnp.where(packed_s[66:67] > 0.0, made_score + packed_s[64:65], FLOOR),
            packed_s[65:66],
        )

    for copy in parts:
        copy.wait_recv()
    blocks = [send_s[s]] + [part_s[k] for k in range(1, 8)]
    spans = [span_s[...]] + [spans_s[k] for k in range(1, 8)]
    peaks = jnp.concatenate([one[0:1] for one in spans], axis=0)
    totals = jnp.concatenate([one[1:2] for one in spans], axis=0)
    joint = jnp.max(peaks, axis=0, keepdims=True)
    factor = jnp.exp(peaks - joint)
    below = jnp.sum(totals * factor, axis=0, keepdims=True)
    pool_s[s] = sum(blocks[k] * factor[k : k + 1] for k in range(8)) / below

    pools = []
    for dz, dx in OFFSETS:
        slot = dz * 4 + dx
        copy = pltpu.make_async_remote_copy(
            src_ref=pool_s.at[s],
            dst_ref=pool_s.at[s],
            send_sem=pool_out.at[slot],
            recv_sem=pool_in.at[slot],
            device_id=(partner(dz, dx), c),
            device_id_type=MESH,
        )
        copy.start()
        pools.append(copy)

    @pl.when(jnp.logical_not(has_down))
    def _():
        scale_s[...] = jnp.ones((1, 256), jnp.float32)
        shift_s[...] = jnp.zeros((64, 256), jnp.float32)

    @pl.when(has_down)
    def _():
        for copy in shared:
            copy.wait_recv()
        rows = jnp.concatenate(
            [token_s[0:2]] + [tokens_s[k, 0:2] for k in range(1, 8)], axis=0
        )
        cells = lax.broadcasted_iota(jnp.int32, (16, 256), 1).astype(jnp.float32)
        entries = jnp.where(cells == rows[:, 66:67], rows[:, 64:65], FLOOR)
        all_joint = jnp.maximum(joint, jnp.max(entries, axis=0, keepdims=True))
        weight = jnp.exp(entries - all_joint)
        old = below * jnp.exp(joint - all_joint)
        share_of = 1.0 / (old + jnp.sum(weight, axis=0, keepdims=True))
        scale_s[...] = old * share_of
        shift_s[...] = dot(rows[:, 0:64], weight * share_of, ((0,), (0,)))

    @pl.when(has_down)
    def _():
        for copy in ups:
            copy.wait_recv()

    @pl.when(has_up)
    def _():
        for copy in downs:
            copy.wait_recv()

    def mean(blocks):
        joint = functools.reduce(jnp.maximum, blocks)[:, 64:65]
        whole = sum(block * jnp.exp(block[:, 64:65] - joint) for block in blocks)
        return whole[:, 0:64] / whole[:, 65:66]

    below_blocks = [next_s[k] for k in range(8)]

    @pl.when(jnp.logical_not(far_up))
    def _():
        side_s[...] = mean(below_blocks)

    @pl.when(far_up)
    def _():
        for copy in far_shared:
            copy.wait_recv()
        first_cell = lax.broadcasted_iota(jnp.int32, (16, 128), 0).astype(jnp.float32) * 16.0
        more = []
        for tokens in [far_s[...]] + [fars_s[k] for k in range(1, 8)]:
            for t in range(2):
                more.append(
                    jnp.where(
                        first_cell == tokens[t : t + 1, 66:67], tokens[t : t + 1], FLOOR
                    )
                )
        side_s[...] = mean(below_blocks + more)

    edges = jnp.concatenate(
        [
            side_s[...],
            mean([prev_s[k] for k in range(8)]),
            jnp.zeros((96, 64), jnp.float32),
        ],
        axis=0,
    )
    outer = dot(stencil[8:72], edges, turned, HIGH)
    outside = []
    for h in range(2):
        cut = slice(h * 128, (h + 1) * 128)
        part = jnp.zeros((8, 128), jnp.float32)
        for k in range(8):
            index = jnp.broadcast_to(near_edge[k : k + 1, cut], (8, 128))
            side = jnp.broadcast_to(near_side[k : k + 1, cut], (8, 128))
            part = part + jnp.where(
                side, lanes(outer[k * 8 : (k + 1) * 8], index), 0.0
            )
        outside.append(part)

    for copy in pools:
        copy.wait_recv()
    pooled = pool_s[...].reshape(64, 256) * scale_s[...] + shift_s[...]
    part0, part1, _ = split3(pooled)
    inner = dot(
        stencil_parts,
        jnp.concatenate([part0, part0, part1], axis=0).astype(jnp.bfloat16),
        precision=None,
    )
    for h in range(2):
        cut = slice(h * 128, (h + 1) * 128)
        joined = inner[0:8, cut] + outside[h]
        for k in range(8):
            row = inner[8 + k * 8 : 16 + k * 8]
            index = jnp.broadcast_to(near[k : k + 1, cut], (8, 128))
            side = jnp.broadcast_to(near_side[k : k + 1, cut], (8, 128))
            picked = jnp.where(
                (index & 128) > 0,
                lanes(row[:, 128:], index & 127),
                lanes(row[:, :128], index & 127),
            )
            joined = joined + jnp.where(side, 0.0, picked)
        out_ref[:, cut] = joined

    @pl.when(has_up)
    def _():
        for copy in [tail] + ups:
            copy.wait_send()

    @pl.when(has_down)
    def _():
        for copy in downs:
            copy.wait_send()

    @pl.when(far_down)
    def _():
        packet.wait_send()

    @pl.when(has_down)
    def _():
        for copy in shared:
            copy.wait_send()

    @pl.when(far_up)
    def _():
        for copy in far_shared:
            copy.wait_send()

    for copy in parts + pools:
        copy.wait_send()


def on_device(*operands):
    f32, i32 = jnp.float32, jnp.int32
    dma = pltpu.SemaphoreType.DMA
    return pl.pallas_call(
        kernel,
        out_shape=pltpu.VMEM((8, 256), f32),
        in_specs=[
            pl.BlockSpec(memory_space=pltpu.SMEM if i == 7 else pltpu.HBM)
            for i in range(10)
        ],
        out_specs=pl.BlockSpec(memory_space=pltpu.VMEM),
        scratch_shapes=[
            pltpu.VMEM((64, 512), f32),
            pltpu.VMEM((64, 192), f32),
            pltpu.VMEM((64, 64), f32),
            pltpu.VMEM((64, 64), f32),
            pltpu.VMEM((64, 256), f32),
            pltpu.VMEM((1, 512), f32),
            pltpu.VMEM((1, 512), i32),
            pltpu.VMEM((8, 256), i32),
            pltpu.VMEM((8, 576), f32),
            pltpu.VMEM((256, 512), jnp.bfloat16),
            pltpu.VMEM((64, 512), f32),
            pltpu.VMEM((1, 256), f32),
            pltpu.VMEM((8, 128), f32),
            pltpu.VMEM((8, 128), f32),
            pltpu.VMEM((8, 8, 256), f32),
            pltpu.VMEM((2, 256), f32),
            pltpu.VMEM((32, 128), f32),
            pltpu.VMEM((16, 128), f32),
            pltpu.VMEM((72, 128), f32),
            pltpu.VMEM((72, 128), f32),
            pltpu.VMEM((8, 128), f32),
            pltpu.VMEM((8, 8, 128), f32),
            pltpu.VMEM((8, 128), f32),
            pltpu.VMEM((8, 8, 128), f32),
            pltpu.VMEM((1, 256), f32),
            pltpu.VMEM((64, 256), f32),
            pltpu.VMEM((16, 64), f32),
            pltpu.VMEM((8, 8, 256), f32),
            pltpu.VMEM((8, 2, 256), f32),
            pltpu.VMEM((8, 8, 256), f32),
            pltpu.VMEM((8, 16, 128), f32),
            pltpu.VMEM((8, 16, 128), f32),
            dma((9,)),
            dma((2,)),
        ]
        + [dma((8,))] * 10
        + [dma((2,))]
        + [dma((8,))] * 4
        + [pltpu.SemaphoreType.REGULAR],
        compiler_params=pltpu.CompilerParams(collective_id=0, has_side_effects=True),
    )(*operands)


def solution(mesh):
    in_specs = (
        P("sensor", None, "cell"),
        P("sensor", None, None),
        P(),
        P(),
        P(None, "cell"),
        P("sensor", "cell"),
        P("sensor", "cell"),
        P("sensor", "cell"),
        P(None, "cell"),
        P(),
    )
    return jax.shard_map(
        on_device,
        mesh=mesh,
        in_specs=in_specs,
        out_specs=P("sensor", "cell"),
        check_vma=False,
    )
```

```python
import functools

import jax
import jax.numpy as jnp
from jax import lax
from jax.experimental import pallas as pl
from jax.experimental.pallas import tpu as pltpu
from jax.sharding import PartitionSpec as P

MESH = pl.DeviceIdType.MESH
FLOOR = -1e30
HIGH, HIGHEST = lax.Precision.HIGH, lax.Precision.HIGHEST
OFFSETS = ((1, 2), (0, 2), (1, 1), (1, 3), (0, 1), (0, 3), (1, 0))


def dot(a, b, dims=((1,), (0,)), precision=HIGHEST):
    return lax.dot_general(
        a, b, (dims, ((), ())), precision=precision, preferred_element_type=jnp.float32
    )


def lanes(values, index):
    return jnp.take_along_axis(values, index, axis=1, mode="promise_in_bounds")


def split3(x):
    high = x.astype(jnp.bfloat16).astype(jnp.float32)
    mid = (x - high).astype(jnp.bfloat16).astype(jnp.float32)
    return high, mid, x - high - mid


def full_dot(a, b):
    a0, a1, a2 = split3(a)
    b0, b1, b2 = split3(b)
    left = jnp.concatenate([a0, a0, a1, a1, a0, a2], axis=1).astype(jnp.bfloat16)
    right = jnp.concatenate([b0, b1, b0, b1, b2, b0], axis=0).astype(jnp.bfloat16)
    return dot(left, right, precision=None)


def gelu(x):
    return 0.5 * x * (1.0 + lax.erf(x * 0.7071067811865476))


def kernel(
    swath_ref,
    enc_ref,
    key_ref,
    value_ref,
    query_ref,
    quality_ref,
    cell_ref,
    live_ref,
    near_ref,
    hp_ref,
    out_ref,
    x_s,
    enc_s,
    key_s,
    value_s,
    query_s,
    quality_s,
    cell_s,
    near_s,
    hp_s,
    hot_s,
    asked_s,
    prior_s,
    tail_s,
    head_s,
    send_s,
    span_s,
    edge_s,
    early_s,
    pack_s,
    packed_s,
    token_s,
    tokens_s,
    far_s,
    fars_s,
    scale_s,
    shift_s,
    side_s,
    part_s,
    spans_s,
    pool_s,
    prev_s,
    next_s,
    in_sem,
    tail_sem,
    part_out,
    part_in,
    span_out,
    span_in,
    pool_out,
    pool_in,
    up_out,
    up_in,
    down_out,
    down_in,
    packet_sem,
    token_out,
    token_in,
    far_out,
    far_in,
    ready,
):
    s = lax.axis_index("sensor")
    c = lax.axis_index("cell")
    z, x = s // 4, s % 4
    up, down = c + 1, c - 1
    has_up, has_down = c < 63, c > 0
    far_up, far_down = has_up & (c % 16 == 15), has_down & (c % 16 == 0)

    def partner(dz, dx):
        return ((z + dz) % 2) * 4 + (x + dx) % 4

    loads = [
        pltpu.make_async_copy(source, target, in_sem.at[i])
        for i, (source, target) in enumerate(
            (
                (cell_ref, cell_s),
                (swath_ref.at[0], x_s),
                (query_ref, query_s),
                (key_ref, key_s),
                (enc_ref.at[0], enc_s),
                (quality_ref, quality_s),
                (hp_ref.at[pl.ds(pl.multiple_of(s * 8, 8), 8)], hp_s),
                (value_ref, value_s),
                (near_ref, near_s),
            )
        )
    ]
    for load in loads[:6]:
        load.start()

    barrier = pltpu.get_barrier_semaphore()

    def signal_beside(pairs):
        for target, there in pairs:

            @pl.when(there)
            def _():
                pl.semaphore_signal(
                    barrier, inc=1, device_id=(s, target), device_id_type=MESH
                )

    signal_beside([(up, has_up & (c != 0)), (down, c > 1)])
    for dz, dx in OFFSETS:
        pl.semaphore_signal(
            barrier, inc=1, device_id=(partner(dz, dx), c), device_id_type=MESH
        )
    for load in loads[6:]:
        load.start()
    loads[0].wait()
    cell = cell_s[...]
    hot_s[...] = jnp.where(
        lax.broadcasted_iota(jnp.int32, (256, 512), 0) == cell, 1.0, 0.0
    ).astype(jnp.bfloat16)

    for i in range(1, 6):
        loads[i].wait()
    last = jnp.transpose(x_s[:, 384:512])
    row = lax.broadcasted_iota(jnp.int32, (8, 64), 0)
    head_s[...] = jnp.where(
        lax.broadcasted_iota(jnp.int32, (8, 128), 0) < 2,
        jnp.concatenate(
            [
                jnp.where(row == 0, last[126:127], last[127:128]),
                jnp.where(row == 0, last[127:128], 0.0),
            ],
            axis=1,
        ),
        0.0,
    )

    query = query_s[...]
    bilinear = full_dot(jnp.transpose(key_s[...]) * 0.125, query)
    enc = enc_s[...]
    taps = jnp.concatenate([enc[:, 0:64], enc[:, 64:128], enc[:, 128:192]], axis=0)
    mixed = full_dot(taps, x_s[...])
    found = dot(
        jnp.concatenate(split3(bilinear), axis=0).astype(jnp.bfloat16),
        hot_s[...],
        precision=None,
    )
    asked_s[...] = found[0:64] + (found[64:128] + found[128:192])
    prior_s[...] = jnp.sum(query * bilinear, axis=0, keepdims=True)

    two, one, zero = mixed[0:64], mixed[64:128], mixed[128:192]
    slot = lax.broadcasted_iota(jnp.int32, (1, 512), 1)
    one, two = pltpu.roll(one, 1, 1), pltpu.roll(two, 2, 1)
    begin = slot[:, 0:128]
    drawn = zero + jnp.concatenate(
        [
            jnp.where(begin < 1, 0.0, one[:, 0:128])
            + jnp.where(begin < 2, 0.0, two[:, 0:128]),
            one[:, 128:] + two[:, 128:],
        ],
        axis=1,
    )

    cell = cell_s[...]
    quality = quality_s[...]
    live = live_ref[0, 0]
    encoded = gelu(drawn)
    score = jnp.sum(encoded * asked_s[...], axis=0, keepdims=True)
    score = score + quality
    valid = (slot < live) & (slot >= jnp.where(has_down, 2, 0))

    hot = lax.broadcasted_iota(jnp.int32, (256, 512), 0) == cell
    masked = jnp.where(valid, score, FLOOR)
    peak = jnp.max(jnp.where(hot, masked, FLOOR), axis=1, keepdims=True)
    eye = lax.broadcasted_iota(jnp.int32, (128, 128), 0) == lax.broadcasted_iota(
        jnp.int32, (128, 128), 1
    )
    halves = [
        jnp.max(
            jnp.where(eye, peak[h * 128 : (h + 1) * 128], FLOOR), axis=0, keepdims=True
        )
        for h in range(2)
    ]
    slot_peak = []
    for b in range(4):
        index = jnp.broadcast_to(cell[:, b * 128 : (b + 1) * 128], (8, 128))
        low, high = (lanes(jnp.broadcast_to(half, (8, 128)), index & 127) for half in halves)
        slot_peak.append(jnp.where(index >= 128, high, low)[0:1])
    slot_peak = jnp.concatenate(slot_peak, axis=1)
    peak = jnp.concatenate(halves, axis=1)
    weight = jnp.where(valid, jnp.exp(score - slot_peak), 0.0)
    weighted = jnp.concatenate(
        [encoded * weight, jnp.broadcast_to(weight, (16, 512))], axis=0
    )
    one_hot = hot_s[...]
    turned = ((1,), (1,))
    high = weighted.astype(jnp.bfloat16)
    low = (weighted - high.astype(jnp.float32)).astype(jnp.bfloat16)
    sums = dot(jnp.concatenate([high, low], axis=0), one_hot, turned, None)
    sums = sums[0:80] + sums[80:160]
    query = query_s[...]
    prior = prior_s[...]
    prior = jnp.where(s == 0, prior, FLOOR)
    joint = jnp.maximum(peak, prior)
    factor = jnp.exp(peak - joint)
    prior_factor = jnp.exp(prior - joint)
    total = sums[64:65] * factor + prior_factor
    sums = sums[0:64] * factor + query * prior_factor
    peak = joint

    span_s[...] = jnp.concatenate([peak, total], axis=0)
    send_s[...] = sums.reshape(8, 8, 256)

    @pl.when(far_down)
    def _():
        lane = lax.broadcasted_iota(jnp.int32, (64, 128), 1)
        lane8 = lax.broadcasted_iota(jnp.int32, (8, 128), 1)
        row8 = lax.broadcasted_iota(jnp.int32, (8, 128), 0)
        pack_s[0:64] = jnp.where(
            lane < 2, drawn[:, 0:128], pltpu.roll(asked_s[:, 0:128], 2, 1)
        )
        pack_s[64:72] = jnp.where(
            row8 == 0,
            quality[:, 0:128],
            jnp.where(
                row8 == 1,
                cell[:, 0:128].astype(jnp.float32),
                jnp.where(lane8 < live, 1.0, 0.0),
            ),
        )

    first_pair = [(up, c == 0), (down, c == 1)]
    waits = has_up.astype(jnp.int32) + has_down.astype(jnp.int32)
    pl.semaphore_wait(barrier, 7 + jnp.where(c == 1, 1, waits))
    signal_beside(first_pair)
    parts = []
    for dz, dx in OFFSETS:
        slot = dz * 4 + dx
        to = partner(dz, dx)
        for source, target, out, into in (
            (send_s.at[to], part_s.at[slot], part_out, part_in),
            (span_s, spans_s.at[slot], span_out, span_in),
        ):
            parts.append(
                pltpu.make_async_remote_copy(
                    src_ref=source,
                    dst_ref=target,
                    send_sem=out.at[slot],
                    recv_sem=into.at[slot],
                    device_id=(to, c),
                    device_id_type=MESH,
                )
            )

    for copy in parts:
        copy.start()

    @pl.when(c == 1)
    def _():
        pl.semaphore_wait(barrier, 1)

    tail = pltpu.make_async_remote_copy(
        src_ref=head_s,
        dst_ref=tail_s,
        send_sem=tail_sem.at[0],
        recv_sem=tail_sem.at[1],
        device_id=(s, up),
        device_id_type=MESH,
    )

    @pl.when(has_up)
    def _():
        tail.start()

    packet = pltpu.make_async_remote_copy(
        src_ref=pack_s,
        dst_ref=packed_s,
        send_sem=packet_sem.at[0],
        recv_sem=packet_sem.at[1],
        device_id=(s, down),
        device_id_type=MESH,
    )

    @pl.when(far_down)
    def _():
        packet.start()

    for dz, dx in OFFSETS:
        pl.semaphore_signal(
            ready, inc=1, device_id=(partner(dz, dx), c), device_id_type=MESH
        )

    @pl.when(jnp.logical_not(has_down))
    def _():
        tail_s[...] = jnp.zeros((8, 128), jnp.float32)
        prev_s[...] = jnp.ones((8, 16, 128), jnp.float32)

    @pl.when(jnp.logical_not(has_up))
    def _():
        next_s[...] = jnp.ones((8, 16, 128), jnp.float32)

    row = lax.broadcasted_iota(jnp.int32, (32, 256), 0)
    chosen = lax.broadcasted_iota(jnp.int32, (32, 256), 1) == (
        (row & 15) * 16 + jnp.where(row >= 16, 15, 0)
    )
    chosen = jnp.where(chosen, 1.0, 0.0)
    chosen = jnp.concatenate([chosen] * 3, axis=1).astype(jnp.bfloat16)

    def edge_rows(peak, total, sums):
        rows = jnp.concatenate(
            [sums, peak, total, jnp.zeros((62, 256), jnp.float32)], axis=0
        )
        rows = jnp.concatenate(split3(rows), axis=1).astype(jnp.bfloat16)
        return dot(chosen, rows, turned, None)

    def edge_copy(source, k, cell_to, target, out, into):
        dz, dx = (OFFSETS + ((0, 0),))[k]
        slot = dz * 4 + dx
        return pltpu.make_async_remote_copy(
            src_ref=source,
            dst_ref=target.at[slot],
            send_sem=out.at[slot],
            recv_sem=into.at[slot],
            device_id=(partner(dz, dx), cell_to),
            device_id_type=MESH,
        )

    ups = [
        edge_copy(edge_s.at[pl.ds(16, 16)], k, up, prev_s, up_out, up_in)
        for k in range(8)
    ]
    downs, far_downs = (
        [edge_copy(source, k, down, next_s, down_out, down_in) for k in range(8)]
        for source in (edge_s.at[pl.ds(0, 16)], early_s)
    )

    shared, far_shared = (
        [
            pltpu.make_async_remote_copy(
                src_ref=source,
                dst_ref=target.at[dz * 4 + dx],
                send_sem=out.at[dz * 4 + dx],
                recv_sem=into.at[dz * 4 + dx],
                device_id=(partner(dz, dx), c),
                device_id_type=MESH,
            )
            for dz, dx in OFFSETS
        ]
        for source, target, out, into in (
            (token_s, tokens_s, token_out, token_in),
            (far_s, fars_s, far_out, far_in),
        )
    )

    def share(target, copies, made, made_score, cells):
        row = lax.broadcasted_iota(jnp.int32, (8, 64), 0)
        column = lax.broadcasted_iota(jnp.int32, (8, 64), 1)
        marks = [
            jnp.where(row == 0, one[:, 0:1], one[:, 1:2]) for one in (made_score, cells)
        ]
        target[...] = jnp.concatenate(
            [
                jnp.transpose(made)[0:8],
                jnp.where(column == 0, marks[0], jnp.where(column == 1, 1.0, marks[1])),
            ],
            axis=1,
        )
        for copy in copies:
            copy.start()

    @pl.when(far_down)
    def _():
        early_s[...] = edge_rows(peak, total, sums)[0:16]
        pl.semaphore_wait(ready, 7)
        for copy in far_downs:
            copy.start()

    @pl.when(has_down)
    def _():
        tail.wait_recv()

    parity = (lax.broadcasted_iota(jnp.int32, (64, 128), 1) & 1) == 0

    def late_tokens(rows, drawn, asked):
        made = [
            jnp.sum(enc_s[:, 0:128] * rows[t : t + 1], axis=1, keepdims=True)
            + drawn[:, t : t + 1]
            for t in range(2)
        ]
        made = gelu(jnp.where(parity, made[0], made[1]))
        asked = jnp.where(parity, asked[:, 0:1], asked[:, 1:2])
        return made, jnp.sum(made * asked, axis=0, keepdims=True)

    late, late_score = late_tokens(tail_s[...], drawn[:, 0:128], asked_s[:, 0:2])

    def share_own():
        column = lax.broadcasted_iota(jnp.int32, (1, 128), 1)
        share(
            token_s,
            shared,
            late,
            jnp.where(column < live, late_score + quality[:, 0:128], FLOOR),
            cell[:, 0:128].astype(jnp.float32),
        )

    pl.when(far_down)(share_own)
    cells = lax.broadcasted_iota(jnp.int32, (1, 256), 1)
    there = [
        (cells == cell[:, t : t + 1]) & (t < live) & has_down for t in range(2)
    ]
    scores = [
        jnp.where(there[t], late_score[:, t : t + 1] + quality[:, t : t + 1], FLOOR)
        for t in range(2)
    ]
    joint = jnp.maximum(peak, jnp.maximum(scores[0], scores[1]))
    factor = jnp.exp(peak - joint)
    total, sums = total * factor, sums * factor
    for t in range(2):
        weight = jnp.where(there[t], jnp.exp(scores[t] - joint), 0.0)
        total = total + weight
        sums = sums + late[:, t : t + 1] * weight

    edge_s[...] = edge_rows(joint, total, sums)

    @pl.when(jnp.logical_not(far_down))
    def _():
        pl.semaphore_wait(ready, 7)

    @pl.when(has_up)
    def _():
        for copy in ups:
            copy.start()

    @pl.when(has_down & jnp.logical_not(far_down))
    def _():
        for copy in downs:
            copy.start()

    pl.when(has_down & jnp.logical_not(far_down))(share_own)

    for i in range(6, 9):
        loads[i].wait()
    hp = hp_s[...]
    stacked = jnp.concatenate([hp[:, k * 64 : (k + 1) * 64] for k in range(9)], axis=0)
    stencil = dot(stacked, value_s[...])
    part0, part1, _ = split3(stencil)
    stencil_parts = jnp.concatenate([part0, part1, part0], axis=1).astype(jnp.bfloat16)
    near = near_s[...] - c * 256
    near_edge = ((near >> 4) & 15) + jnp.where(near < 0, 16, 0)
    near_side = (near < 0) | (near >= 256)

    @pl.when(far_up)
    def _():
        packet.wait_recv()
        made, made_score = late_tokens(
            head_s[...], packed_s[0:64, 0:2], packed_s[0:64, 2:4]
        )
        share(
            far_s,
            far_shared,
            made,
            jnp.where(packed_s[66:67] > 0.0, made_score + packed_s[64:65], FLOOR),
            packed_s[65:66],
        )

    for copy in parts:
        copy.wait_recv()
    blocks = [send_s[s]] + [part_s[k] for k in range(1, 8)]
    spans = [span_s[...]] + [spans_s[k] for k in range(1, 8)]
    peaks = jnp.concatenate([one[0:1] for one in spans], axis=0)
    totals = jnp.concatenate([one[1:2] for one in spans], axis=0)
    joint = jnp.max(peaks, axis=0, keepdims=True)
    factor = jnp.exp(peaks - joint)
    below = jnp.sum(totals * factor, axis=0, keepdims=True)
    pool_s[s] = sum(blocks[k] * factor[k : k + 1] for k in range(8)) / below

    pools = []
    for dz, dx in OFFSETS:
        slot = dz * 4 + dx
        copy = pltpu.make_async_remote_copy(
            src_ref=pool_s.at[s],
            dst_ref=pool_s.at[s],
            send_sem=pool_out.at[slot],
            recv_sem=pool_in.at[slot],
            device_id=(partner(dz, dx), c),
            device_id_type=MESH,
        )
        copy.start()
        pools.append(copy)

    @pl.when(jnp.logical_not(has_down))
    def _():
        scale_s[...] = jnp.ones((1, 256), jnp.float32)
        shift_s[...] = jnp.zeros((64, 256), jnp.float32)

    @pl.when(has_down)
    def _():
        for copy in shared:
            copy.wait_recv()
        rows = jnp.concatenate(
            [token_s[0:2]] + [tokens_s[k, 0:2] for k in range(1, 8)], axis=0
        )
        cells = lax.broadcasted_iota(jnp.int32, (16, 256), 1).astype(jnp.float32)
        entries = jnp.where(cells == rows[:, 66:67], rows[:, 64:65], FLOOR)
        all_joint = jnp.maximum(joint, jnp.max(entries, axis=0, keepdims=True))
        weight = jnp.exp(entries - all_joint)
        old = below * jnp.exp(joint - all_joint)
        share_of = 1.0 / (old + jnp.sum(weight, axis=0, keepdims=True))
        scale_s[...] = old * share_of
        shift_s[...] = dot(rows[:, 0:64], weight * share_of, ((0,), (0,)))

    @pl.when(has_down)
    def _():
        for copy in ups:
            copy.wait_recv()

    @pl.when(has_up)
    def _():
        for copy in downs:
            copy.wait_recv()

    def mean(blocks):
        joint = functools.reduce(jnp.maximum, blocks)[:, 64:65]
        whole = sum(block * jnp.exp(block[:, 64:65] - joint) for block in blocks)
        return whole[:, 0:64] / whole[:, 65:66]

    below_blocks = [next_s[k] for k in range(8)]

    @pl.when(jnp.logical_not(far_up))
    def _():
        side_s[...] = mean(below_blocks)

    @pl.when(far_up)
    def _():
        for copy in far_shared:
            copy.wait_recv()
        first_cell = lax.broadcasted_iota(jnp.int32, (16, 128), 0).astype(jnp.float32) * 16.0
        more = []
        for tokens in [far_s[...]] + [fars_s[k] for k in range(1, 8)]:
            for t in range(2):
                more.append(
                    jnp.where(
                        first_cell == tokens[t : t + 1, 66:67], tokens[t : t + 1], FLOOR
                    )
                )
        side_s[...] = mean(below_blocks + more)

    edges = jnp.concatenate(
        [
            side_s[...],
            mean([prev_s[k] for k in range(8)]),
            jnp.zeros((96, 64), jnp.float32),
        ],
        axis=0,
    )
    outer = dot(stencil[8:72], edges, turned, HIGH)
    outside = []
    for h in range(2):
        cut = slice(h * 128, (h + 1) * 128)
        part = jnp.zeros((8, 128), jnp.float32)
        for k in range(8):
            index = jnp.broadcast_to(near_edge[k : k + 1, cut], (8, 128))
            side = jnp.broadcast_to(near_side[k : k + 1, cut], (8, 128))
            part = part + jnp.where(
                side, lanes(outer[k * 8 : (k + 1) * 8], index), 0.0
            )
        outside.append(part)

    for copy in pools:
        copy.wait_recv()
    pooled = pool_s[...].reshape(64, 256) * scale_s[...] + shift_s[...]
    part0, part1, _ = split3(pooled)
    inner = dot(
        stencil_parts,
        jnp.concatenate([part0, part0, part1], axis=0).astype(jnp.bfloat16),
        precision=None,
    )
    for h in range(2):
        cut = slice(h * 128, (h + 1) * 128)
        joined = inner[0:8, cut] + outside[h]
        for k in range(8):
            row = inner[8 + k * 8 : 16 + k * 8]
            index = jnp.broadcast_to(near[k : k + 1, cut], (8, 128))
            side = jnp.broadcast_to(near_side[k : k + 1, cut], (8, 128))
            picked = jnp.where(
                (index & 128) > 0,
                lanes(row[:, 128:], index & 127),
                lanes(row[:, :128], index & 127),
            )
            joined = joined + jnp.where(side, 0.0, picked)
        out_ref[:, cut] = joined

    @pl.when(has_up)
    def _():
        for copy in [tail] + ups:
            copy.wait_send()

    @pl.when(has_down)
    def _():
        for copy in downs:
            copy.wait_send()

    @pl.when(far_down)
    def _():
        packet.wait_send()

    @pl.when(has_down)
    def _():
        for copy in shared:
            copy.wait_send()

    @pl.when(far_up)
    def _():
        for copy in far_shared:
            copy.wait_send()

    for copy in parts + pools:
        copy.wait_send()


def on_device(*operands):
    f32, i32 = jnp.float32, jnp.int32
    dma = pltpu.SemaphoreType.DMA
    return pl.pallas_call(
        kernel,
        out_shape=pltpu.VMEM((8, 256), f32),
        in_specs=[
            pl.BlockSpec(memory_space=pltpu.SMEM if i == 7 else pltpu.HBM)
            for i in range(10)
        ],
        out_specs=pl.BlockSpec(memory_space=pltpu.VMEM),
        scratch_shapes=[
            pltpu.VMEM((64, 512), f32),
            pltpu.VMEM((64, 192), f32),
            pltpu.VMEM((64, 64), f32),
            pltpu.VMEM((64, 64), f32),
            pltpu.VMEM((64, 256), f32),
            pltpu.VMEM((1, 512), f32),
            pltpu.VMEM((1, 512), i32),
            pltpu.VMEM((8, 256), i32),
            pltpu.VMEM((8, 576), f32),
            pltpu.VMEM((256, 512), jnp.bfloat16),
            pltpu.VMEM((64, 512), f32),
            pltpu.VMEM((1, 256), f32),
            pltpu.VMEM((8, 128), f32),
            pltpu.VMEM((8, 128), f32),
            pltpu.VMEM((8, 8, 256), f32),
            pltpu.VMEM((2, 256), f32),
            pltpu.VMEM((32, 128), f32),
            pltpu.VMEM((16, 128), f32),
            pltpu.VMEM((72, 128), f32),
            pltpu.VMEM((72, 128), f32),
            pltpu.VMEM((8, 128), f32),
            pltpu.VMEM((8, 8, 128), f32),
            pltpu.VMEM((8, 128), f32),
            pltpu.VMEM((8, 8, 128), f32),
            pltpu.VMEM((1, 256), f32),
            pltpu.VMEM((64, 256), f32),
            pltpu.VMEM((16, 64), f32),
            pltpu.VMEM((8, 8, 256), f32),
            pltpu.VMEM((8, 2, 256), f32),
            pltpu.VMEM((8, 8, 256), f32),
            pltpu.VMEM((8, 16, 128), f32),
            pltpu.VMEM((8, 16, 128), f32),
            dma((9,)),
            dma((2,)),
        ]
        + [dma((8,))] * 10
        + [dma((2,))]
        + [dma((8,))] * 4
        + [pltpu.SemaphoreType.REGULAR],
        compiler_params=pltpu.CompilerParams(collective_id=0, has_side_effects=True),
    )(*operands)


def solution(mesh):
    in_specs = (
        P("sensor", None, "cell"),
        P("sensor", None, None),
        P(),
        P(),
        P(None, "cell"),
        P("sensor", "cell"),
        P("sensor", "cell"),
        P("sensor", "cell"),
        P(None, "cell"),
        P(),
    )
    return jax.shard_map(
        on_device,
        mesh=mesh,
        in_specs=in_specs,
        out_specs=P("sensor", "cell"),
        check_vma=False,
    )
```

```python
import functools

import jax
import jax.numpy as jnp
from jax import lax
from jax.experimental import pallas as pl
from jax.experimental.pallas import tpu as pltpu
from jax.sharding import PartitionSpec as P

MESH = pl.DeviceIdType.MESH
FLOOR = -1e30
HIGH, HIGHEST = lax.Precision.HIGH, lax.Precision.HIGHEST
OFFSETS = ((1, 2), (0, 2), (1, 1), (1, 3), (0, 1), (0, 3), (1, 0))


def dot(a, b, dims=((1,), (0,)), precision=HIGHEST):
    return lax.dot_general(
        a, b, (dims, ((), ())), precision=precision, preferred_element_type=jnp.float32
    )


def lanes(values, index):
    return jnp.take_along_axis(values, index, axis=1, mode="promise_in_bounds")


def split3(x):
    high = x.astype(jnp.bfloat16).astype(jnp.float32)
    mid = (x - high).astype(jnp.bfloat16).astype(jnp.float32)
    return high, mid, x - high - mid


def full_dot(a, b):
    a0, a1, a2 = split3(a)
    b0, b1, b2 = split3(b)
    left = jnp.concatenate([a0, a0, a1, a1, a0, a2], axis=1).astype(jnp.bfloat16)
    right = jnp.concatenate([b0, b1, b0, b1, b2, b0], axis=0).astype(jnp.bfloat16)
    return dot(left, right, precision=None)


def gelu(x):
    return 0.5 * x * (1.0 + lax.erf(x * 0.7071067811865476))


def kernel(
    swath_ref,
    enc_ref,
    key_ref,
    value_ref,
    query_ref,
    quality_ref,
    cell_ref,
    live_ref,
    near_ref,
    hp_ref,
    out_ref,
    x_s,
    enc_s,
    key_s,
    value_s,
    query_s,
    quality_s,
    cell_s,
    near_s,
    hp_s,
    hot_s,
    asked_s,
    prior_s,
    tail_s,
    head_s,
    send_s,
    span_s,
    edge_s,
    early_s,
    pack_s,
    packed_s,
    token_s,
    tokens_s,
    far_s,
    fars_s,
    scale_s,
    shift_s,
    side_s,
    part_s,
    spans_s,
    pool_s,
    prev_s,
    next_s,
    in_sem,
    tail_sem,
    part_out,
    part_in,
    span_out,
    span_in,
    pool_out,
    pool_in,
    up_out,
    up_in,
    down_out,
    down_in,
    packet_sem,
    token_out,
    token_in,
    far_out,
    far_in,
    ready,
):
    s = lax.axis_index("sensor")
    c = lax.axis_index("cell")
    z, x = s // 4, s % 4
    up, down = c + 1, c - 1
    has_up, has_down = c < 63, c > 0
    far_up, far_down = has_up & (c % 16 == 15), has_down & (c % 16 == 0)

    def partner(dz, dx):
        return ((z + dz) % 2) * 4 + (x + dx) % 4

    loads = [
        pltpu.make_async_copy(source, target, in_sem.at[i])
        for i, (source, target) in enumerate(
            (
                (cell_ref, cell_s),
                (swath_ref.at[0], x_s),
                (query_ref, query_s),
                (key_ref, key_s),
                (enc_ref.at[0], enc_s),
                (quality_ref, quality_s),
                (hp_ref.at[pl.ds(pl.multiple_of(s * 8, 8), 8)], hp_s),
                (value_ref, value_s),
                (near_ref, near_s),
            )
        )
    ]
    for load in loads[:6]:
        load.start()

    barrier = pltpu.get_barrier_semaphore()

    def signal_beside(pairs):
        for target, there in pairs:

            @pl.when(there)
            def _():
                pl.semaphore_signal(
                    barrier, inc=1, device_id=(s, target), device_id_type=MESH
                )

    signal_beside([(up, has_up & (c != 0)), (down, c > 1)])
    for dz, dx in OFFSETS:
        pl.semaphore_signal(
            barrier, inc=1, device_id=(partner(dz, dx), c), device_id_type=MESH
        )
    for load in loads[6:]:
        load.start()
    loads[0].wait()
    cell = cell_s[...]
    hot_s[...] = jnp.where(
        lax.broadcasted_iota(jnp.int32, (256, 512), 0) == cell, 1.0, 0.0
    ).astype(jnp.bfloat16)

    for i in range(1, 6):
        loads[i].wait()
    last = jnp.transpose(x_s[:, 384:512])
    row = lax.broadcasted_iota(jnp.int32, (8, 64), 0)
    head_s[...] = jnp.where(
        lax.broadcasted_iota(jnp.int32, (8, 128), 0) < 2,
        jnp.concatenate(
            [
                jnp.where(row == 0, last[126:127], last[127:128]),
                jnp.where(row == 0, last[127:128], 0.0),
            ],
            axis=1,
        ),
        0.0,
    )

    query = query_s[...]
    bilinear = full_dot(jnp.transpose(key_s[...]) * 0.125, query)
    enc = enc_s[...]
    taps = jnp.concatenate([enc[:, 0:64], enc[:, 64:128], enc[:, 128:192]], axis=0)
    mixed = full_dot(taps, x_s[...])
    found = dot(
        jnp.concatenate(split3(bilinear), axis=0).astype(jnp.bfloat16),
        hot_s[...],
        precision=None,
    )
    asked_s[...] = found[0:64] + (found[64:128] + found[128:192])
    prior_s[...] = jnp.sum(query * bilinear, axis=0, keepdims=True)

    two, one, zero = mixed[0:64], mixed[64:128], mixed[128:192]
    slot = lax.broadcasted_iota(jnp.int32, (1, 512), 1)
    one, two = pltpu.roll(one, 1, 1), pltpu.roll(two, 2, 1)
    begin = slot[:, 0:128]
    drawn = zero + jnp.concatenate(
        [
            jnp.where(begin < 1, 0.0, one[:, 0:128])
            + jnp.where(begin < 2, 0.0, two[:, 0:128]),
            one[:, 128:] + two[:, 128:],
        ],
        axis=1,
    )

    cell = cell_s[...]
    quality = quality_s[...]
    live = live_ref[0, 0]
    encoded = gelu(drawn)
    score = jnp.sum(encoded * asked_s[...], axis=0, keepdims=True)
    score = score + quality
    valid = (slot < live) & (slot >= jnp.where(has_down, 2, 0))

    hot = lax.broadcasted_iota(jnp.int32, (256, 512), 0) == cell
    masked = jnp.where(valid, score, FLOOR)
    peak = jnp.max(jnp.where(hot, masked, FLOOR), axis=1, keepdims=True)
    eye = lax.broadcasted_iota(jnp.int32, (128, 128), 0) == lax.broadcasted_iota(
        jnp.int32, (128, 128), 1
    )
    halves = [
        jnp.max(
            jnp.where(eye, peak[h * 128 : (h + 1) * 128], FLOOR), axis=0, keepdims=True
        )
        for h in range(2)
    ]
    slot_peak = []
    for b in range(4):
        index = jnp.broadcast_to(cell[:, b * 128 : (b + 1) * 128], (8, 128))
        low, high = (lanes(jnp.broadcast_to(half, (8, 128)), index & 127) for half in halves)
        slot_peak.append(jnp.where(index >= 128, high, low)[0:1])
    slot_peak = jnp.concatenate(slot_peak, axis=1)
    peak = jnp.concatenate(halves, axis=1)
    weight = jnp.where(valid, jnp.exp(score - slot_peak), 0.0)
    weighted = jnp.concatenate(
        [encoded * weight, jnp.broadcast_to(weight, (16, 512))], axis=0
    )
    one_hot = hot_s[...]
    turned = ((1,), (1,))
    high = weighted.astype(jnp.bfloat16)
    low = (weighted - high.astype(jnp.float32)).astype(jnp.bfloat16)
    sums = dot(jnp.concatenate([high, low], axis=0), one_hot, turned, None)
    sums = sums[0:80] + sums[80:160]
    query = query_s[...]
    prior = prior_s[...]
    prior = jnp.where(s == 0, prior, FLOOR)
    joint = jnp.maximum(peak, prior)
    factor = jnp.exp(peak - joint)
    prior_factor = jnp.exp(prior - joint)
    total = sums[64:65] * factor + prior_factor
    sums = sums[0:64] * factor + query * prior_factor
    peak = joint

    span_s[...] = jnp.concatenate([peak, total], axis=0)
    send_s[...] = sums.reshape(8, 8, 256)

    @pl.when(far_down)
    def _():
        lane = lax.broadcasted_iota(jnp.int32, (64, 128), 1)
        lane8 = lax.broadcasted_iota(jnp.int32, (8, 128), 1)
        row8 = lax.broadcasted_iota(jnp.int32, (8, 128), 0)
        pack_s[0:64] = jnp.where(
            lane < 2, drawn[:, 0:128], pltpu.roll(asked_s[:, 0:128], 2, 1)
        )
        pack_s[64:72] = jnp.where(
            row8 == 0,
            quality[:, 0:128],
            jnp.where(
                row8 == 1,
                cell[:, 0:128].astype(jnp.float32),
                jnp.where(lane8 < live, 1.0, 0.0),
            ),
        )

    first_pair = [(up, c == 0), (down, c == 1)]
    waits = has_up.astype(jnp.int32) + has_down.astype(jnp.int32)
    pl.semaphore_wait(barrier, 7 + jnp.where(c == 1, 1, waits))
    signal_beside(first_pair)
    parts = []
    for dz, dx in OFFSETS:
        slot = dz * 4 + dx
        to = partner(dz, dx)
        for source, target, out, into in (
            (send_s.at[to], part_s.at[slot], part_out, part_in),
            (span_s, spans_s.at[slot], span_out, span_in),
        ):
            parts.append(
                pltpu.make_async_remote_copy(
                    src_ref=source,
                    dst_ref=target,
                    send_sem=out.at[slot],
                    recv_sem=into.at[slot],
                    device_id=(to, c),
                    device_id_type=MESH,
                )
            )

    for copy in parts:
        copy.start()

    tail = pltpu.make_async_remote_copy(
        src_ref=head_s,
        dst_ref=tail_s,
        send_sem=tail_sem.at[0],
        recv_sem=tail_sem.at[1],
        device_id=(s, up),
        device_id_type=MESH,
    )

    @pl.when(has_up)
    def _():
        tail.start()

    packet = pltpu.make_async_remote_copy(
        src_ref=pack_s,
        dst_ref=packed_s,
        send_sem=packet_sem.at[0],
        recv_sem=packet_sem.at[1],
        device_id=(s, down),
        device_id_type=MESH,
    )

    @pl.when(far_down)
    def _():
        packet.start()

    @pl.when(c == 1)
    def _():
        pl.semaphore_wait(barrier, 1)

    for dz, dx in OFFSETS:
        pl.semaphore_signal(
            ready, inc=1, device_id=(partner(dz, dx), c), device_id_type=MESH
        )

    @pl.when(jnp.logical_not(has_down))
    def _():
        tail_s[...] = jnp.zeros((8, 128), jnp.float32)
        prev_s[...] = jnp.ones((8, 16, 128), jnp.float32)

    @pl.when(jnp.logical_not(has_up))
    def _():
        next_s[...] = jnp.ones((8, 16, 128), jnp.float32)

    row = lax.broadcasted_iota(jnp.int32, (32, 256), 0)
    chosen = lax.broadcasted_iota(jnp.int32, (32, 256), 1) == (
        (row & 15) * 16 + jnp.where(row >= 16, 15, 0)
    )
    chosen = jnp.where(chosen, 1.0, 0.0)
    chosen = jnp.concatenate([chosen] * 3, axis=1).astype(jnp.bfloat16)

    def edge_rows(peak, total, sums):
        rows = jnp.concatenate(
            [sums, peak, total, jnp.zeros((62, 256), jnp.float32)], axis=0
        )
        rows = jnp.concatenate(split3(rows), axis=1).astype(jnp.bfloat16)
        return dot(chosen, rows, turned, None)

    def edge_copy(source, k, cell_to, target, out, into):
        dz, dx = (OFFSETS + ((0, 0),))[k]
        slot = dz * 4 + dx
        return pltpu.make_async_remote_copy(
            src_ref=source,
            dst_ref=target.at[slot],
            send_sem=out.at[slot],
            recv_sem=into.at[slot],
            device_id=(partner(dz, dx), cell_to),
            device_id_type=MESH,
        )

    ups = [
        edge_copy(edge_s.at[pl.ds(16, 16)], k, up, prev_s, up_out, up_in)
        for k in range(8)
    ]
    downs, far_downs = (
        [edge_copy(source, k, down, next_s, down_out, down_in) for k in range(8)]
        for source in (edge_s.at[pl.ds(0, 16)], early_s)
    )

    shared, far_shared = (
        [
            pltpu.make_async_remote_copy(
                src_ref=source,
                dst_ref=target.at[dz * 4 + dx],
                send_sem=out.at[dz * 4 + dx],
                recv_sem=into.at[dz * 4 + dx],
                device_id=(partner(dz, dx), c),
                device_id_type=MESH,
            )
            for dz, dx in OFFSETS
        ]
        for source, target, out, into in (
            (token_s, tokens_s, token_out, token_in),
            (far_s, fars_s, far_out, far_in),
        )
    )

    def share(target, copies, made, made_score, cells):
        row = lax.broadcasted_iota(jnp.int32, (8, 64), 0)
        column = lax.broadcasted_iota(jnp.int32, (8, 64), 1)
        marks = [
            jnp.where(row == 0, one[:, 0:1], one[:, 1:2]) for one in (made_score, cells)
        ]
        target[...] = jnp.concatenate(
            [
                jnp.transpose(made)[0:8],
                jnp.where(column == 0, marks[0], jnp.where(column == 1, 1.0, marks[1])),
            ],
            axis=1,
        )
        for copy in copies:
            copy.start()

    @pl.when(far_down)
    def _():
        early_s[...] = edge_rows(peak, total, sums)[0:16]
        pl.semaphore_wait(ready, 7)
        for copy in far_downs:
            copy.start()

    @pl.when(has_down)
    def _():
        tail.wait_recv()

    parity = (lax.broadcasted_iota(jnp.int32, (64, 128), 1) & 1) == 0

    def late_tokens(rows, drawn, asked):
        made = [
            jnp.sum(enc_s[:, 0:128] * rows[t : t + 1], axis=1, keepdims=True)
            + drawn[:, t : t + 1]
            for t in range(2)
        ]
        made = gelu(jnp.where(parity, made[0], made[1]))
        asked = jnp.where(parity, asked[:, 0:1], asked[:, 1:2])
        return made, jnp.sum(made * asked, axis=0, keepdims=True)

    late, late_score = late_tokens(tail_s[...], drawn[:, 0:128], asked_s[:, 0:2])

    def share_own():
        column = lax.broadcasted_iota(jnp.int32, (1, 128), 1)
        share(
            token_s,
            shared,
            late,
            jnp.where(column < live, late_score + quality[:, 0:128], FLOOR),
            cell[:, 0:128].astype(jnp.float32),
        )

    pl.when(far_down)(share_own)
    cells = lax.broadcasted_iota(jnp.int32, (1, 256), 1)
    there = [
        (cells == cell[:, t : t + 1]) & (t < live) & has_down for t in range(2)
    ]
    scores = [
        jnp.where(there[t], late_score[:, t : t + 1] + quality[:, t : t + 1], FLOOR)
        for t in range(2)
    ]
    joint = jnp.maximum(peak, jnp.maximum(scores[0], scores[1]))
    factor = jnp.exp(peak - joint)
    total, sums = total * factor, sums * factor
    for t in range(2):
        weight = jnp.where(there[t], jnp.exp(scores[t] - joint), 0.0)
        total = total + weight
        sums = sums + late[:, t : t + 1] * weight

    edge_s[...] = edge_rows(joint, total, sums)

    pl.when(c == 1)(share_own)

    @pl.when(jnp.logical_not(far_down))
    def _():
        pl.semaphore_wait(ready, 7)

    @pl.when(has_up)
    def _():
        for copy in ups:
            copy.start()

    @pl.when(has_down & jnp.logical_not(far_down))
    def _():
        for copy in downs:
            copy.start()

    pl.when((c > 1) & jnp.logical_not(far_down))(share_own)

    for i in range(6, 9):
        loads[i].wait()
    hp = hp_s[...]
    stacked = jnp.concatenate([hp[:, k * 64 : (k + 1) * 64] for k in range(9)], axis=0)
    stencil = dot(stacked, value_s[...])
    part0, part1, _ = split3(stencil)
    stencil_parts = jnp.concatenate([part0, part1, part0], axis=1).astype(jnp.bfloat16)
    near = near_s[...] - c * 256
    near_edge = ((near >> 4) & 15) + jnp.where(near < 0, 16, 0)
    near_side = (near < 0) | (near >= 256)

    @pl.when(far_up)
    def _():
        packet.wait_recv()
        made, made_score = late_tokens(
            head_s[...], packed_s[0:64, 0:2], packed_s[0:64, 2:4]
        )
        share(
            far_s,
            far_shared,
            made,
            jnp.where(packed_s[66:67] > 0.0, made_score + packed_s[64:65], FLOOR),
            packed_s[65:66],
        )

    for copy in parts:
        copy.wait_recv()
    blocks = [send_s[s]] + [part_s[k] for k in range(1, 8)]
    spans = [span_s[...]] + [spans_s[k] for k in range(1, 8)]
    peaks = jnp.concatenate([one[0:1] for one in spans], axis=0)
    totals = jnp.concatenate([one[1:2] for one in spans], axis=0)
    joint = jnp.max(peaks, axis=0, keepdims=True)
    factor = jnp.exp(peaks - joint)
    below = jnp.sum(totals * factor, axis=0, keepdims=True)
    pool_s[s] = sum(blocks[k] * factor[k : k + 1] for k in range(8)) / below

    pools = []
    for dz, dx in OFFSETS:
        slot = dz * 4 + dx
        copy = pltpu.make_async_remote_copy(
            src_ref=pool_s.at[s],
            dst_ref=pool_s.at[s],
            send_sem=pool_out.at[slot],
            recv_sem=pool_in.at[slot],
            device_id=(partner(dz, dx), c),
            device_id_type=MESH,
        )
        copy.start()
        pools.append(copy)

    @pl.when(jnp.logical_not(has_down))
    def _():
        scale_s[...] = jnp.ones((1, 256), jnp.float32)
        shift_s[...] = jnp.zeros((64, 256), jnp.float32)

    @pl.when(has_down)
    def _():
        for copy in shared:
            copy.wait_recv()
        rows = jnp.concatenate(
            [token_s[0:2]] + [tokens_s[k, 0:2] for k in range(1, 8)], axis=0
        )
        cells = lax.broadcasted_iota(jnp.int32, (16, 256), 1).astype(jnp.float32)
        entries = jnp.where(cells == rows[:, 66:67], rows[:, 64:65], FLOOR)
        all_joint = jnp.maximum(joint, jnp.max(entries, axis=0, keepdims=True))
        weight = jnp.exp(entries - all_joint)
        old = below * jnp.exp(joint - all_joint)
        share_of = 1.0 / (old + jnp.sum(weight, axis=0, keepdims=True))
        scale_s[...] = old * share_of
        shift_s[...] = dot(rows[:, 0:64], weight * share_of, ((0,), (0,)))

    @pl.when(has_down)
    def _():
        for copy in ups:
            copy.wait_recv()

    @pl.when(has_up)
    def _():
        for copy in downs:
            copy.wait_recv()

    def mean(blocks):
        joint = functools.reduce(jnp.maximum, blocks)[:, 64:65]
        whole = sum(block * jnp.exp(block[:, 64:65] - joint) for block in blocks)
        return whole[:, 0:64] / whole[:, 65:66]

    below_blocks = [next_s[k] for k in range(8)]

    @pl.when(jnp.logical_not(far_up))
    def _():
        side_s[...] = mean(below_blocks)

    @pl.when(far_up)
    def _():
        for copy in far_shared:
            copy.wait_recv()
        first_cell = lax.broadcasted_iota(jnp.int32, (16, 128), 0).astype(jnp.float32) * 16.0
        more = []
        for tokens in [far_s[...]] + [fars_s[k] for k in range(1, 8)]:
            for t in range(2):
                more.append(
                    jnp.where(
                        first_cell == tokens[t : t + 1, 66:67], tokens[t : t + 1], FLOOR
                    )
                )
        side_s[...] = mean(below_blocks + more)

    edges = jnp.concatenate(
        [
            side_s[...],
            mean([prev_s[k] for k in range(8)]),
            jnp.zeros((96, 64), jnp.float32),
        ],
        axis=0,
    )
    outer = dot(stencil[8:72], edges, turned, HIGH)
    outside = []
    for h in range(2):
        cut = slice(h * 128, (h + 1) * 128)
        part = jnp.zeros((8, 128), jnp.float32)
        for k in range(8):
            index = jnp.broadcast_to(near_edge[k : k + 1, cut], (8, 128))
            side = jnp.broadcast_to(near_side[k : k + 1, cut], (8, 128))
            part = part + jnp.where(
                side, lanes(outer[k * 8 : (k + 1) * 8], index), 0.0
            )
        outside.append(part)

    for copy in pools:
        copy.wait_recv()
    pooled = pool_s[...].reshape(64, 256) * scale_s[...] + shift_s[...]
    part0, part1, _ = split3(pooled)
    inner = dot(
        stencil_parts,
        jnp.concatenate([part0, part0, part1], axis=0).astype(jnp.bfloat16),
        precision=None,
    )
    for h in range(2):
        cut = slice(h * 128, (h + 1) * 128)
        joined = inner[0:8, cut] + outside[h]
        for k in range(8):
            row = inner[8 + k * 8 : 16 + k * 8]
            index = jnp.broadcast_to(near[k : k + 1, cut], (8, 128))
            side = jnp.broadcast_to(near_side[k : k + 1, cut], (8, 128))
            picked = jnp.where(
                (index & 128) > 0,
                lanes(row[:, 128:], index & 127),
                lanes(row[:, :128], index & 127),
            )
            joined = joined + jnp.where(side, 0.0, picked)
        out_ref[:, cut] = joined

    @pl.when(has_up)
    def _():
        for copy in [tail] + ups:
            copy.wait_send()

    @pl.when(has_down)
    def _():
        for copy in downs:
            copy.wait_send()

    @pl.when(far_down)
    def _():
        packet.wait_send()

    @pl.when(has_down)
    def _():
        for copy in shared:
            copy.wait_send()

    @pl.when(far_up)
    def _():
        for copy in far_shared:
            copy.wait_send()

    for copy in parts + pools:
        copy.wait_send()


def on_device(*operands):
    f32, i32 = jnp.float32, jnp.int32
    dma = pltpu.SemaphoreType.DMA
    return pl.pallas_call(
        kernel,
        out_shape=pltpu.VMEM((8, 256), f32),
        in_specs=[
            pl.BlockSpec(memory_space=pltpu.SMEM if i == 7 else pltpu.HBM)
            for i in range(10)
        ],
        out_specs=pl.BlockSpec(memory_space=pltpu.VMEM),
        scratch_shapes=[
            pltpu.VMEM((64, 512), f32),
            pltpu.VMEM((64, 192), f32),
            pltpu.VMEM((64, 64), f32),
            pltpu.VMEM((64, 64), f32),
            pltpu.VMEM((64, 256), f32),
            pltpu.VMEM((1, 512), f32),
            pltpu.VMEM((1, 512), i32),
            pltpu.VMEM((8, 256), i32),
            pltpu.VMEM((8, 576), f32),
            pltpu.VMEM((256, 512), jnp.bfloat16),
            pltpu.VMEM((64, 512), f32),
            pltpu.VMEM((1, 256), f32),
            pltpu.VMEM((8, 128), f32),
            pltpu.VMEM((8, 128), f32),
            pltpu.VMEM((8, 8, 256), f32),
            pltpu.VMEM((2, 256), f32),
            pltpu.VMEM((32, 128), f32),
            pltpu.VMEM((16, 128), f32),
            pltpu.VMEM((72, 128), f32),
            pltpu.VMEM((72, 128), f32),
            pltpu.VMEM((8, 128), f32),
            pltpu.VMEM((8, 8, 128), f32),
            pltpu.VMEM((8, 128), f32),
            pltpu.VMEM((8, 8, 128), f32),
            pltpu.VMEM((1, 256), f32),
            pltpu.VMEM((64, 256), f32),
            pltpu.VMEM((16, 64), f32),
            pltpu.VMEM((8, 8, 256), f32),
            pltpu.VMEM((8, 2, 256), f32),
            pltpu.VMEM((8, 8, 256), f32),
            pltpu.VMEM((8, 16, 128), f32),
            pltpu.VMEM((8, 16, 128), f32),
            dma((9,)),
            dma((2,)),
        ]
        + [dma((8,))] * 10
        + [dma((2,))]
        + [dma((8,))] * 4
        + [pltpu.SemaphoreType.REGULAR],
        compiler_params=pltpu.CompilerParams(collective_id=0, has_side_effects=True),
    )(*operands)


def solution(mesh):
    in_specs = (
        P("sensor", None, "cell"),
        P("sensor", None, None),
        P(),
        P(),
        P(None, "cell"),
        P("sensor", "cell"),
        P("sensor", "cell"),
        P("sensor", "cell"),
        P(None, "cell"),
        P(),
    )
    return jax.shard_map(
        on_device,
        mesh=mesh,
        in_specs=in_specs,
        out_specs=P("sensor", "cell"),
        check_vma=False,
    )
```

```python
import functools

import jax
import jax.numpy as jnp
from jax import lax
from jax.experimental import pallas as pl
from jax.experimental.pallas import tpu as pltpu
from jax.sharding import PartitionSpec as P

MESH = pl.DeviceIdType.MESH
FLOOR = -1e30
HIGH, HIGHEST = lax.Precision.HIGH, lax.Precision.HIGHEST
OFFSETS = ((1, 2), (0, 2), (1, 1), (1, 3), (0, 1), (0, 3), (1, 0))


def dot(a, b, dims=((1,), (0,)), precision=HIGHEST):
    return lax.dot_general(
        a, b, (dims, ((), ())), precision=precision, preferred_element_type=jnp.float32
    )


def lanes(values, index):
    return jnp.take_along_axis(values, index, axis=1, mode="promise_in_bounds")


def split3(x):
    high = x.astype(jnp.bfloat16).astype(jnp.float32)
    mid = (x - high).astype(jnp.bfloat16).astype(jnp.float32)
    return high, mid, x - high - mid


def full_dot(a, b):
    a0, a1, a2 = split3(a)
    b0, b1, b2 = split3(b)
    left = jnp.concatenate([a0, a0, a1, a1, a0, a2], axis=1).astype(jnp.bfloat16)
    right = jnp.concatenate([b0, b1, b0, b1, b2, b0], axis=0).astype(jnp.bfloat16)
    return dot(left, right, precision=None)


def gelu(x):
    return 0.5 * x * (1.0 + lax.erf(x * 0.7071067811865476))


def kernel(
    swath_ref,
    enc_ref,
    key_ref,
    value_ref,
    query_ref,
    quality_ref,
    cell_ref,
    live_ref,
    near_ref,
    hp_ref,
    out_ref,
    x_s,
    enc_s,
    key_s,
    value_s,
    query_s,
    quality_s,
    cell_s,
    near_s,
    hp_s,
    hot_s,
    asked_s,
    prior_s,
    tail_s,
    head_s,
    send_s,
    span_s,
    edge_s,
    early_s,
    pack_s,
    packed_s,
    token_s,
    tokens_s,
    far_s,
    fars_s,
    scale_s,
    shift_s,
    side_s,
    part_s,
    spans_s,
    pool_s,
    prev_s,
    next_s,
    in_sem,
    tail_sem,
    part_out,
    part_in,
    span_out,
    span_in,
    pool_out,
    pool_in,
    up_out,
    up_in,
    down_out,
    down_in,
    packet_sem,
    token_out,
    token_in,
    far_out,
    far_in,
    ready,
):
    s = lax.axis_index("sensor")
    c = lax.axis_index("cell")
    z, x = s // 4, s % 4
    up, down = c + 1, c - 1
    has_up, has_down = c < 63, c > 0
    far_up, far_down = has_up & (c % 16 == 15), has_down & (c % 16 == 0)

    def partner(dz, dx):
        return ((z + dz) % 2) * 4 + (x + dx) % 4

    loads = [
        pltpu.make_async_copy(source, target, in_sem.at[i])
        for i, (source, target) in enumerate(
            (
                (cell_ref, cell_s),
                (swath_ref.at[0], x_s),
                (query_ref, query_s),
                (key_ref, key_s),
                (enc_ref.at[0], enc_s),
                (quality_ref, quality_s),
                (hp_ref.at[pl.ds(pl.multiple_of(s * 8, 8), 8)], hp_s),
                (value_ref, value_s),
                (near_ref, near_s),
            )
        )
    ]
    for load in loads[:6]:
        load.start()

    barrier = pltpu.get_barrier_semaphore()

    for target, there in ((up, has_up), (down, has_down)):

        @pl.when(there)
        def _():
            pl.semaphore_signal(
                barrier, inc=1, device_id=(s, target), device_id_type=MESH
            )

    for dz, dx in OFFSETS:
        pl.semaphore_signal(
            barrier, inc=1, device_id=(partner(dz, dx), c), device_id_type=MESH
        )
    for load in loads[6:]:
        load.start()
    loads[0].wait()
    cell = cell_s[...]
    hot_s[...] = jnp.where(
        lax.broadcasted_iota(jnp.int32, (256, 512), 0) == cell, 1.0, 0.0
    ).astype(jnp.bfloat16)

    for i in range(1, 6):
        loads[i].wait()
    last = jnp.transpose(x_s[:, 384:512])
    row = lax.broadcasted_iota(jnp.int32, (8, 64), 0)
    head_s[...] = jnp.where(
        lax.broadcasted_iota(jnp.int32, (8, 128), 0) < 2,
        jnp.concatenate(
            [
                jnp.where(row == 0, last[126:127], last[127:128]),
                jnp.where(row == 0, last[127:128], 0.0),
            ],
            axis=1,
        ),
        0.0,
    )

    query = query_s[...]
    bilinear = full_dot(jnp.transpose(key_s[...]) * 0.125, query)
    enc = enc_s[...]
    taps = jnp.concatenate([enc[:, 0:64], enc[:, 64:128], enc[:, 128:192]], axis=0)
    mixed = full_dot(taps, x_s[...])
    found = dot(
        jnp.concatenate(split3(bilinear), axis=0).astype(jnp.bfloat16),
        hot_s[...],
        precision=None,
    )
    asked_s[...] = found[0:64] + (found[64:128] + found[128:192])
    prior_s[...] = jnp.sum(query * bilinear, axis=0, keepdims=True)

    two, one, zero = mixed[0:64], mixed[64:128], mixed[128:192]
    slot = lax.broadcasted_iota(jnp.int32, (1, 512), 1)
    one, two = pltpu.roll(one, 1, 1), pltpu.roll(two, 2, 1)
    begin = slot[:, 0:128]
    drawn = zero + jnp.concatenate(
        [
            jnp.where(begin < 1, 0.0, one[:, 0:128])
            + jnp.where(begin < 2, 0.0, two[:, 0:128]),
            one[:, 128:] + two[:, 128:],
        ],
        axis=1,
    )

    cell = cell_s[...]
    quality = quality_s[...]
    live = live_ref[0, 0]
    encoded = gelu(drawn)
    score = jnp.sum(encoded * asked_s[...], axis=0, keepdims=True)
    score = score + quality
    valid = (slot < live) & (slot >= jnp.where(has_down, 2, 0))

    hot = lax.broadcasted_iota(jnp.int32, (256, 512), 0) == cell
    masked = jnp.where(valid, score, FLOOR)
    peak = jnp.max(jnp.where(hot, masked, FLOOR), axis=1, keepdims=True)
    eye = lax.broadcasted_iota(jnp.int32, (128, 128), 0) == lax.broadcasted_iota(
        jnp.int32, (128, 128), 1
    )
    halves = [
        jnp.max(
            jnp.where(eye, peak[h * 128 : (h + 1) * 128], FLOOR), axis=0, keepdims=True
        )
        for h in range(2)
    ]
    slot_peak = []
    for b in range(4):
        index = jnp.broadcast_to(cell[:, b * 128 : (b + 1) * 128], (8, 128))
        low, high = (lanes(jnp.broadcast_to(half, (8, 128)), index & 127) for half in halves)
        slot_peak.append(jnp.where(index >= 128, high, low)[0:1])
    slot_peak = jnp.concatenate(slot_peak, axis=1)
    peak = jnp.concatenate(halves, axis=1)
    weight = jnp.where(valid, jnp.exp(score - slot_peak), 0.0)
    weighted = jnp.concatenate(
        [encoded * weight, jnp.broadcast_to(weight, (16, 512))], axis=0
    )
    one_hot = hot_s[...]
    turned = ((1,), (1,))
    high = weighted.astype(jnp.bfloat16)
    low = (weighted - high.astype(jnp.float32)).astype(jnp.bfloat16)
    sums = dot(jnp.concatenate([high, low], axis=0), one_hot, turned, None)
    sums = sums[0:80] + sums[80:160]
    query = query_s[...]
    prior = prior_s[...]
    prior = jnp.where(s == 0, prior, FLOOR)
    joint = jnp.maximum(peak, prior)
    factor = jnp.exp(peak - joint)
    prior_factor = jnp.exp(prior - joint)
    total = sums[64:65] * factor + prior_factor
    sums = sums[0:64] * factor + query * prior_factor
    peak = joint

    span_s[...] = jnp.concatenate([peak, total], axis=0)
    send_s[...] = sums.reshape(8, 8, 256)

    @pl.when(far_down)
    def _():
        lane = lax.broadcasted_iota(jnp.int32, (64, 128), 1)
        lane8 = lax.broadcasted_iota(jnp.int32, (8, 128), 1)
        row8 = lax.broadcasted_iota(jnp.int32, (8, 128), 0)
        pack_s[0:64] = jnp.where(
            lane < 2, drawn[:, 0:128], pltpu.roll(asked_s[:, 0:128], 2, 1)
        )
        pack_s[64:72] = jnp.where(
            row8 == 0,
            quality[:, 0:128],
            jnp.where(
                row8 == 1,
                cell[:, 0:128].astype(jnp.float32),
                jnp.where(lane8 < live, 1.0, 0.0),
            ),
        )

    pl.semaphore_wait(
        barrier, 7 + has_up.astype(jnp.int32) + has_down.astype(jnp.int32)
    )
    parts = []
    for dz, dx in OFFSETS:
        slot = dz * 4 + dx
        to = partner(dz, dx)
        for source, target, out, into in (
            (send_s.at[to], part_s.at[slot], part_out, part_in),
            (span_s, spans_s.at[slot], span_out, span_in),
        ):
            parts.append(
                pltpu.make_async_remote_copy(
                    src_ref=source,
                    dst_ref=target,
                    send_sem=out.at[slot],
                    recv_sem=into.at[slot],
                    device_id=(to, c),
                    device_id_type=MESH,
                )
            )

    for copy in parts:
        copy.start()

    tail = pltpu.make_async_remote_copy(
        src_ref=head_s,
        dst_ref=tail_s,
        send_sem=tail_sem.at[0],
        recv_sem=tail_sem.at[1],
        device_id=(s, up),
        device_id_type=MESH,
    )

    @pl.when(has_up)
    def _():
        tail.start()

    packet = pltpu.make_async_remote_copy(
        src_ref=pack_s,
        dst_ref=packed_s,
        send_sem=packet_sem.at[0],
        recv_sem=packet_sem.at[1],
        device_id=(s, down),
        device_id_type=MESH,
    )

    @pl.when(far_down)
    def _():
        packet.start()

    for dz, dx in OFFSETS:
        pl.semaphore_signal(
            ready, inc=1, device_id=(partner(dz, dx), c), device_id_type=MESH
        )

    @pl.when(jnp.logical_not(has_down))
    def _():
        tail_s[...] = jnp.zeros((8, 128), jnp.float32)
        prev_s[...] = jnp.ones((8, 16, 128), jnp.float32)

    @pl.when(jnp.logical_not(has_up))
    def _():
        next_s[...] = jnp.ones((8, 16, 128), jnp.float32)

    row = lax.broadcasted_iota(jnp.int32, (32, 256), 0)
    chosen = lax.broadcasted_iota(jnp.int32, (32, 256), 1) == (
        (row & 15) * 16 + jnp.where(row >= 16, 15, 0)
    )
    chosen = jnp.where(chosen, 1.0, 0.0)
    chosen = jnp.concatenate([chosen] * 3, axis=1).astype(jnp.bfloat16)

    def edge_rows(peak, total, sums):
        rows = jnp.concatenate(
            [sums, peak, total, jnp.zeros((62, 256), jnp.float32)], axis=0
        )
        rows = jnp.concatenate(split3(rows), axis=1).astype(jnp.bfloat16)
        return dot(chosen, rows, turned, None)

    def edge_copy(source, k, cell_to, target, out, into):
        dz, dx = (OFFSETS + ((0, 0),))[k]
        slot = dz * 4 + dx
        return pltpu.make_async_remote_copy(
            src_ref=source,
            dst_ref=target.at[slot],
            send_sem=out.at[slot],
            recv_sem=into.at[slot],
            device_id=(partner(dz, dx), cell_to),
            device_id_type=MESH,
        )

    ups = [
        edge_copy(edge_s.at[pl.ds(16, 16)], k, up, prev_s, up_out, up_in)
        for k in range(8)
    ]
    downs, far_downs = (
        [edge_copy(source, k, down, next_s, down_out, down_in) for k in range(8)]
        for source in (edge_s.at[pl.ds(0, 16)], early_s)
    )

    shared, far_shared = (
        [
            pltpu.make_async_remote_copy(
                src_ref=source,
                dst_ref=target.at[dz * 4 + dx],
                send_sem=out.at[dz * 4 + dx],
                recv_sem=into.at[dz * 4 + dx],
                device_id=(partner(dz, dx), c),
                device_id_type=MESH,
            )
            for dz, dx in OFFSETS
        ]
        for source, target, out, into in (
            (token_s, tokens_s, token_out, token_in),
            (far_s, fars_s, far_out, far_in),
        )
    )

    def share(target, copies, made, made_score, cells):
        row = lax.broadcasted_iota(jnp.int32, (8, 64), 0)
        column = lax.broadcasted_iota(jnp.int32, (8, 64), 1)
        marks = [
            jnp.where(row == 0, one[:, 0:1], one[:, 1:2]) for one in (made_score, cells)
        ]
        target[...] = jnp.concatenate(
            [
                jnp.transpose(made)[0:8],
                jnp.where(column == 0, marks[0], jnp.where(column == 1, 1.0, marks[1])),
            ],
            axis=1,
        )
        for copy in copies:
            copy.start()

    @pl.when(far_down)
    def _():
        early_s[...] = edge_rows(peak, total, sums)[0:16]
        pl.semaphore_wait(ready, 7)
        for copy in far_downs:
            copy.start()

    @pl.when(has_down)
    def _():
        tail.wait_recv()

    parity = (lax.broadcasted_iota(jnp.int32, (64, 128), 1) & 1) == 0

    def late_tokens(rows, drawn, asked):
        made = [
            jnp.sum(enc_s[:, 0:128] * rows[t : t + 1], axis=1, keepdims=True)
            + drawn[:, t : t + 1]
            for t in range(2)
        ]
        made = gelu(jnp.where(parity, made[0], made[1]))
        asked = jnp.where(parity, asked[:, 0:1], asked[:, 1:2])
        return made, jnp.sum(made * asked, axis=0, keepdims=True)

    late, late_score = late_tokens(tail_s[...], drawn[:, 0:128], asked_s[:, 0:2])

    def share_own():
        column = lax.broadcasted_iota(jnp.int32, (1, 128), 1)
        share(
            token_s,
            shared,
            late,
            jnp.where(column < live, late_score + quality[:, 0:128], FLOOR),
            cell[:, 0:128].astype(jnp.float32),
        )

    pl.when(far_down)(share_own)
    cells = lax.broadcasted_iota(jnp.int32, (1, 256), 1)
    there = [
        (cells == cell[:, t : t + 1]) & (t < live) & has_down for t in range(2)
    ]
    scores = [
        jnp.where(there[t], late_score[:, t : t + 1] + quality[:, t : t + 1], FLOOR)
        for t in range(2)
    ]
    joint = jnp.maximum(peak, jnp.maximum(scores[0], scores[1]))
    factor = jnp.exp(peak - joint)
    total, sums = total * factor, sums * factor
    for t in range(2):
        weight = jnp.where(there[t], jnp.exp(scores[t] - joint), 0.0)
        total = total + weight
        sums = sums + late[:, t : t + 1] * weight

    edge_s[...] = edge_rows(joint, total, sums)

    @pl.when(jnp.logical_not(far_down))
    def _():
        pl.semaphore_wait(ready, 7)

    @pl.when(has_up)
    def _():
        for copy in ups:
            copy.start()

    @pl.when(has_down & jnp.logical_not(far_down))
    def _():
        for copy in downs:
            copy.start()

    pl.when(has_down & jnp.logical_not(far_down))(share_own)

    for i in range(6, 9):
        loads[i].wait()
    hp = hp_s[...]
    stacked = jnp.concatenate([hp[:, k * 64 : (k + 1) * 64] for k in range(9)], axis=0)
    stencil = dot(stacked, value_s[...])
    part0, part1, _ = split3(stencil)
    stencil_parts = jnp.concatenate([part0, part1, part0], axis=1).astype(jnp.bfloat16)
    near = near_s[...] - c * 256
    near_edge = ((near >> 4) & 15) + jnp.where(near < 0, 16, 0)
    near_side = (near < 0) | (near >= 256)

    @pl.when(far_up)
    def _():
        packet.wait_recv()
        made, made_score = late_tokens(
            head_s[...], packed_s[0:64, 0:2], packed_s[0:64, 2:4]
        )
        share(
            far_s,
            far_shared,
            made,
            jnp.where(packed_s[66:67] > 0.0, made_score + packed_s[64:65], FLOOR),
            packed_s[65:66],
        )

    for copy in parts:
        copy.wait_recv()
    blocks = [send_s[s]] + [part_s[k] for k in range(1, 8)]
    spans = [span_s[...]] + [spans_s[k] for k in range(1, 8)]
    peaks = jnp.concatenate([one[0:1] for one in spans], axis=0)
    totals = jnp.concatenate([one[1:2] for one in spans], axis=0)
    joint = jnp.max(peaks, axis=0, keepdims=True)
    factor = jnp.exp(peaks - joint)
    below = jnp.sum(totals * factor, axis=0, keepdims=True)
    pool_s[s] = sum(blocks[k] * factor[k : k + 1] for k in range(8)) / below

    pools = []
    for dz, dx in OFFSETS:
        slot = dz * 4 + dx
        copy = pltpu.make_async_remote_copy(
            src_ref=pool_s.at[s],
            dst_ref=pool_s.at[s],
            send_sem=pool_out.at[slot],
            recv_sem=pool_in.at[slot],
            device_id=(partner(dz, dx), c),
            device_id_type=MESH,
        )
        copy.start()
        pools.append(copy)

    @pl.when(jnp.logical_not(has_down))
    def _():
        scale_s[...] = jnp.ones((1, 256), jnp.float32)
        shift_s[...] = jnp.zeros((64, 256), jnp.float32)

    @pl.when(has_down)
    def _():
        for copy in shared:
            copy.wait_recv()
        rows = jnp.concatenate(
            [token_s[0:2]] + [tokens_s[k, 0:2] for k in range(1, 8)], axis=0
        )
        cells = lax.broadcasted_iota(jnp.int32, (16, 256), 1).astype(jnp.float32)
        entries = jnp.where(cells == rows[:, 66:67], rows[:, 64:65], FLOOR)
        all_joint = jnp.maximum(joint, jnp.max(entries, axis=0, keepdims=True))
        weight = jnp.exp(entries - all_joint)
        old = below * jnp.exp(joint - all_joint)
        share_of = 1.0 / (old + jnp.sum(weight, axis=0, keepdims=True))
        scale_s[...] = old * share_of
        shift_s[...] = dot(rows[:, 0:64], weight * share_of, ((0,), (0,)))

    @pl.when(has_down)
    def _():
        for copy in ups:
            copy.wait_recv()

    @pl.when(has_up)
    def _():
        for copy in downs:
            copy.wait_recv()

    def mean(blocks):
        joint = functools.reduce(jnp.maximum, blocks)[:, 64:65]
        whole = sum(block * jnp.exp(block[:, 64:65] - joint) for block in blocks)
        return whole[:, 0:64] / whole[:, 65:66]

    below_blocks = [next_s[k] for k in range(8)]

    @pl.when(jnp.logical_not(far_up))
    def _():
        side_s[...] = mean(below_blocks)

    @pl.when(far_up)
    def _():
        for copy in far_shared:
            copy.wait_recv()
        first_cell = lax.broadcasted_iota(jnp.int32, (16, 128), 0).astype(jnp.float32) * 16.0
        more = []
        for tokens in [far_s[...]] + [fars_s[k] for k in range(1, 8)]:
            for t in range(2):
                more.append(
                    jnp.where(
                        first_cell == tokens[t : t + 1, 66:67], tokens[t : t + 1], FLOOR
                    )
                )
        side_s[...] = mean(below_blocks + more)

    edges = jnp.concatenate(
        [
            side_s[...],
            mean([prev_s[k] for k in range(8)]),
            jnp.zeros((96, 64), jnp.float32),
        ],
        axis=0,
    )
    outer = dot(stencil[8:72], edges, turned, HIGH)
    outside = []
    for h in range(2):
        cut = slice(h * 128, (h + 1) * 128)
        part = jnp.zeros((8, 128), jnp.float32)
        for k in range(8):
            index = jnp.broadcast_to(near_edge[k : k + 1, cut], (8, 128))
            side = jnp.broadcast_to(near_side[k : k + 1, cut], (8, 128))
            part = part + jnp.where(
                side, lanes(outer[k * 8 : (k + 1) * 8], index), 0.0
            )
        outside.append(part)

    for copy in pools:
        copy.wait_recv()
    pooled = pool_s[...].reshape(64, 256) * scale_s[...] + shift_s[...]
    part0, part1, _ = split3(pooled)
    inner = dot(
        stencil_parts,
        jnp.concatenate([part0, part0, part1], axis=0).astype(jnp.bfloat16),
        precision=None,
    )
    for h in range(2):
        cut = slice(h * 128, (h + 1) * 128)
        joined = inner[0:8, cut] + outside[h]
        for k in range(8):
            row = inner[8 + k * 8 : 16 + k * 8]
            index = jnp.broadcast_to(near[k : k + 1, cut], (8, 128))
            side = jnp.broadcast_to(near_side[k : k + 1, cut], (8, 128))
            picked = jnp.where(
                (index & 128) > 0,
                lanes(row[:, 128:], index & 127),
                lanes(row[:, :128], index & 127),
            )
            joined = joined + jnp.where(side, 0.0, picked)
        out_ref[:, cut] = joined

    @pl.when(has_up)
    def _():
        for copy in [tail] + ups:
            copy.wait_send()

    @pl.when(has_down)
    def _():
        for copy in downs:
            copy.wait_send()

    @pl.when(far_down)
    def _():
        packet.wait_send()

    @pl.when(has_down)
    def _():
        for copy in shared:
            copy.wait_send()

    @pl.when(far_up)
    def _():
        for copy in far_shared:
            copy.wait_send()

    for copy in parts + pools:
        copy.wait_send()


def on_device(*operands):
    f32, i32 = jnp.float32, jnp.int32
    dma = pltpu.SemaphoreType.DMA
    return pl.pallas_call(
        kernel,
        out_shape=pltpu.VMEM((8, 256), f32),
        in_specs=[
            pl.BlockSpec(memory_space=pltpu.SMEM if i == 7 else pltpu.HBM)
            for i in range(10)
        ],
        out_specs=pl.BlockSpec(memory_space=pltpu.VMEM),
        scratch_shapes=[
            pltpu.VMEM((64, 512), f32),
            pltpu.VMEM((64, 192), f32),
            pltpu.VMEM((64, 64), f32),
            pltpu.VMEM((64, 64), f32),
            pltpu.VMEM((64, 256), f32),
            pltpu.VMEM((1, 512), f32),
            pltpu.VMEM((1, 512), i32),
            pltpu.VMEM((8, 256), i32),
            pltpu.VMEM((8, 576), f32),
            pltpu.VMEM((256, 512), jnp.bfloat16),
            pltpu.VMEM((64, 512), f32),
            pltpu.VMEM((1, 256), f32),
            pltpu.VMEM((8, 128), f32),
            pltpu.VMEM((8, 128), f32),
            pltpu.VMEM((8, 8, 256), f32),
            pltpu.VMEM((2, 256), f32),
            pltpu.VMEM((32, 128), f32),
            pltpu.VMEM((16, 128), f32),
            pltpu.VMEM((72, 128), f32),
            pltpu.VMEM((72, 128), f32),
            pltpu.VMEM((8, 128), f32),
            pltpu.VMEM((8, 8, 128), f32),
            pltpu.VMEM((8, 128), f32),
            pltpu.VMEM((8, 8, 128), f32),
            pltpu.VMEM((1, 256), f32),
            pltpu.VMEM((64, 256), f32),
            pltpu.VMEM((16, 64), f32),
            pltpu.VMEM((8, 8, 256), f32),
            pltpu.VMEM((8, 2, 256), f32),
            pltpu.VMEM((8, 8, 256), f32),
            pltpu.VMEM((8, 16, 128), f32),
            pltpu.VMEM((8, 16, 128), f32),
            dma((9,)),
            dma((2,)),
        ]
        + [dma((8,))] * 10
        + [dma((2,))]
        + [dma((8,))] * 4
        + [pltpu.SemaphoreType.REGULAR],
        compiler_params=pltpu.CompilerParams(collective_id=0, has_side_effects=True),
    )(*operands)


def solution(mesh):
    in_specs = (
        P("sensor", None, "cell"),
        P("sensor", None, None),
        P(),
        P(),
        P(None, "cell"),
        P("sensor", "cell"),
        P("sensor", "cell"),
        P("sensor", "cell"),
        P(None, "cell"),
        P(),
    )
    return jax.shard_map(
        on_device,
        mesh=mesh,
        in_specs=in_specs,
        out_specs=P("sensor", "cell"),
        check_vma=False,
    )
```

```python
import functools

import jax
import jax.numpy as jnp
from jax import lax
from jax.experimental import pallas as pl
from jax.experimental.pallas import tpu as pltpu
from jax.sharding import PartitionSpec as P

MESH = pl.DeviceIdType.MESH
FLOOR = -1e30
HIGH, HIGHEST = lax.Precision.HIGH, lax.Precision.HIGHEST
OFFSETS = ((1, 2), (0, 2), (1, 1), (1, 3), (0, 1), (0, 3), (1, 0))


def dot(a, b, dims=((1,), (0,)), precision=HIGHEST):
    return lax.dot_general(
        a, b, (dims, ((), ())), precision=precision, preferred_element_type=jnp.float32
    )


def lanes(values, index):
    return jnp.take_along_axis(values, index, axis=1, mode="promise_in_bounds")


def split3(x):
    high = x.astype(jnp.bfloat16).astype(jnp.float32)
    mid = (x - high).astype(jnp.bfloat16).astype(jnp.float32)
    return high, mid, x - high - mid


def full_dot(a, b):
    a0, a1, a2 = split3(a)
    b0, b1, b2 = split3(b)
    left = jnp.concatenate([a0, a0, a1, a1, a0, a2], axis=1).astype(jnp.bfloat16)
    right = jnp.concatenate([b0, b1, b0, b1, b2, b0], axis=0).astype(jnp.bfloat16)
    return dot(left, right, precision=None)


def gelu(x):
    return 0.5 * x * (1.0 + lax.erf(x * 0.7071067811865476))


def kernel(
    swath_ref,
    enc_ref,
    key_ref,
    value_ref,
    query_ref,
    quality_ref,
    cell_ref,
    live_ref,
    near_ref,
    hp_ref,
    out_ref,
    x_s,
    enc_s,
    key_s,
    value_s,
    query_s,
    quality_s,
    cell_s,
    near_s,
    hp_s,
    hot_s,
    asked_s,
    prior_s,
    tail_s,
    head_s,
    send_s,
    span_s,
    edge_s,
    early_s,
    pack_s,
    packed_s,
    token_s,
    tokens_s,
    far_s,
    fars_s,
    scale_s,
    shift_s,
    side_s,
    part_s,
    spans_s,
    pool_s,
    prev_s,
    next_s,
    in_sem,
    tail_sem,
    part_out,
    part_in,
    span_out,
    span_in,
    pool_out,
    pool_in,
    up_out,
    up_in,
    down_out,
    down_in,
    packet_sem,
    token_out,
    token_in,
    far_out,
    far_in,
    ready,
):
    s = lax.axis_index("sensor")
    c = lax.axis_index("cell")
    z, x = lax.div(s, 4), lax.rem(s, 4)
    up, down = c + 1, c - 1
    has_up, has_down = c < 63, c > 0
    far_up, far_down = has_up & (c % 16 == 15), has_down & (c % 16 == 0)

    rows = (z * 4, (1 - z) * 4)
    columns = [x] + [lax.rem(x + k, 4) for k in range(1, 4)]

    def partner(dz, dx):
        return rows[dz] + columns[dx]

    loads = [
        pltpu.make_async_copy(source, target, in_sem.at[i])
        for i, (source, target) in enumerate(
            (
                (cell_ref, cell_s),
                (swath_ref.at[0], x_s),
                (query_ref, query_s),
                (key_ref, key_s),
                (enc_ref.at[0], enc_s),
                (quality_ref, quality_s),
                (hp_ref.at[pl.ds(pl.multiple_of(s * 8, 8), 8)], hp_s),
                (value_ref, value_s),
                (near_ref, near_s),
            )
        )
    ]
    for load in loads[:6]:
        load.start()

    barrier = pltpu.get_barrier_semaphore()

    for target, there in ((up, has_up), (down, has_down)):

        @pl.when(there)
        def _():
            pl.semaphore_signal(
                barrier, inc=1, device_id=(s, target), device_id_type=MESH
            )

    for dz, dx in OFFSETS:
        pl.semaphore_signal(
            barrier, inc=1, device_id=(partner(dz, dx), c), device_id_type=MESH
        )
    for load in loads[6:]:
        load.start()
    loads[0].wait()
    cell = cell_s[...]
    hot_s[...] = jnp.where(
        lax.broadcasted_iota(jnp.int32, (256, 512), 0) == cell, 1.0, 0.0
    ).astype(jnp.bfloat16)

    for i in range(1, 6):
        loads[i].wait()
    last = jnp.transpose(x_s[:, 384:512])
    row = lax.broadcasted_iota(jnp.int32, (8, 64), 0)
    head_s[...] = jnp.where(
        lax.broadcasted_iota(jnp.int32, (8, 128), 0) < 2,
        jnp.concatenate(
            [
                jnp.where(row == 0, last[126:127], last[127:128]),
                jnp.where(row == 0, last[127:128], 0.0),
            ],
            axis=1,
        ),
        0.0,
    )

    query = query_s[...]
    bilinear = full_dot(jnp.transpose(key_s[...]) * 0.125, query)
    enc = enc_s[...]
    taps = jnp.concatenate([enc[:, 0:64], enc[:, 64:128], enc[:, 128:192]], axis=0)
    mixed = full_dot(taps, x_s[...])
    found = dot(
        jnp.concatenate(split3(bilinear), axis=0).astype(jnp.bfloat16),
        hot_s[...],
        precision=None,
    )
    asked_s[...] = found[0:64] + (found[64:128] + found[128:192])
    prior_s[...] = jnp.sum(query * bilinear, axis=0, keepdims=True)

    two, one, zero = mixed[0:64], mixed[64:128], mixed[128:192]
    slot = lax.broadcasted_iota(jnp.int32, (1, 512), 1)
    one, two = pltpu.roll(one, 1, 1), pltpu.roll(two, 2, 1)
    begin = slot[:, 0:128]
    drawn = zero + jnp.concatenate(
        [
            jnp.where(begin < 1, 0.0, one[:, 0:128])
            + jnp.where(begin < 2, 0.0, two[:, 0:128]),
            one[:, 128:] + two[:, 128:],
        ],
        axis=1,
    )

    cell = cell_s[...]
    quality = quality_s[...]
    live = live_ref[0, 0]
    encoded = gelu(drawn)
    score = jnp.sum(encoded * asked_s[...], axis=0, keepdims=True)
    score = score + quality
    valid = (slot < live) & (slot >= jnp.where(has_down, 2, 0))

    hot = lax.broadcasted_iota(jnp.int32, (256, 512), 0) == cell
    masked = jnp.where(valid, score, FLOOR)
    peak = jnp.max(jnp.where(hot, masked, FLOOR), axis=1, keepdims=True)
    eye = lax.broadcasted_iota(jnp.int32, (128, 128), 0) == lax.broadcasted_iota(
        jnp.int32, (128, 128), 1
    )
    halves = [
        jnp.max(
            jnp.where(eye, peak[h * 128 : (h + 1) * 128], FLOOR), axis=0, keepdims=True
        )
        for h in range(2)
    ]
    slot_peak = []
    for b in range(4):
        index = jnp.broadcast_to(cell[:, b * 128 : (b + 1) * 128], (8, 128))
        low, high = (lanes(jnp.broadcast_to(half, (8, 128)), index & 127) for half in halves)
        slot_peak.append(jnp.where(index >= 128, high, low)[0:1])
    slot_peak = jnp.concatenate(slot_peak, axis=1)
    peak = jnp.concatenate(halves, axis=1)
    weight = jnp.where(valid, jnp.exp(score - slot_peak), 0.0)
    weighted = jnp.concatenate(
        [encoded * weight, jnp.broadcast_to(weight, (16, 512))], axis=0
    )
    one_hot = hot_s[...]
    turned = ((1,), (1,))
    high = weighted.astype(jnp.bfloat16)
    low = (weighted - high.astype(jnp.float32)).astype(jnp.bfloat16)
    sums = dot(jnp.concatenate([high, low], axis=0), one_hot, turned, None)
    sums = sums[0:80] + sums[80:160]
    query = query_s[...]
    prior = prior_s[...]
    prior = jnp.where(s == 0, prior, FLOOR)
    joint = jnp.maximum(peak, prior)
    factor = jnp.exp(peak - joint)
    prior_factor = jnp.exp(prior - joint)
    total = sums[64:65] * factor + prior_factor
    sums = sums[0:64] * factor + query * prior_factor
    peak = joint

    span_s[...] = jnp.concatenate([peak, total], axis=0)
    send_s[...] = sums.reshape(8, 8, 256)

    @pl.when(far_down)
    def _():
        lane = lax.broadcasted_iota(jnp.int32, (64, 128), 1)
        lane8 = lax.broadcasted_iota(jnp.int32, (8, 128), 1)
        row8 = lax.broadcasted_iota(jnp.int32, (8, 128), 0)
        pack_s[0:64] = jnp.where(
            lane < 2, drawn[:, 0:128], pltpu.roll(asked_s[:, 0:128], 2, 1)
        )
        pack_s[64:72] = jnp.where(
            row8 == 0,
            quality[:, 0:128],
            jnp.where(
                row8 == 1,
                cell[:, 0:128].astype(jnp.float32),
                jnp.where(lane8 < live, 1.0, 0.0),
            ),
        )

    pl.semaphore_wait(
        barrier, 7 + has_up.astype(jnp.int32) + has_down.astype(jnp.int32)
    )
    parts = []
    for dz, dx in OFFSETS:
        slot = dz * 4 + dx
        to = partner(dz, dx)
        for source, target, out, into in (
            (send_s.at[to], part_s.at[slot], part_out, part_in),
            (span_s, spans_s.at[slot], span_out, span_in),
        ):
            parts.append(
                pltpu.make_async_remote_copy(
                    src_ref=source,
                    dst_ref=target,
                    send_sem=out.at[slot],
                    recv_sem=into.at[slot],
                    device_id=(to, c),
                    device_id_type=MESH,
                )
            )

    for copy in parts:
        copy.start()

    tail = pltpu.make_async_remote_copy(
        src_ref=head_s,
        dst_ref=tail_s,
        send_sem=tail_sem.at[0],
        recv_sem=tail_sem.at[1],
        device_id=(s, up),
        device_id_type=MESH,
    )

    @pl.when(has_up)
    def _():
        tail.start()

    packet = pltpu.make_async_remote_copy(
        src_ref=pack_s,
        dst_ref=packed_s,
        send_sem=packet_sem.at[0],
        recv_sem=packet_sem.at[1],
        device_id=(s, down),
        device_id_type=MESH,
    )

    @pl.when(far_down)
    def _():
        packet.start()

    for dz, dx in OFFSETS:
        pl.semaphore_signal(
            ready, inc=1, device_id=(partner(dz, dx), c), device_id_type=MESH
        )

    @pl.when(jnp.logical_not(has_down))
    def _():
        tail_s[...] = jnp.zeros((8, 128), jnp.float32)
        prev_s[...] = jnp.ones((8, 16, 128), jnp.float32)

    @pl.when(jnp.logical_not(has_up))
    def _():
        next_s[...] = jnp.ones((8, 16, 128), jnp.float32)

    row = lax.broadcasted_iota(jnp.int32, (32, 256), 0)
    chosen = lax.broadcasted_iota(jnp.int32, (32, 256), 1) == (
        (row & 15) * 16 + jnp.where(row >= 16, 15, 0)
    )
    chosen = jnp.where(chosen, 1.0, 0.0)
    chosen = jnp.concatenate([chosen] * 3, axis=1).astype(jnp.bfloat16)

    def edge_rows(peak, total, sums):
        rows = jnp.concatenate(
            [sums, peak, total, jnp.zeros((62, 256), jnp.float32)], axis=0
        )
        rows = jnp.concatenate(split3(rows), axis=1).astype(jnp.bfloat16)
        return dot(chosen, rows, turned, None)

    def edge_copy(source, k, cell_to, target, out, into):
        dz, dx = (OFFSETS + ((0, 0),))[k]
        slot = dz * 4 + dx
        return pltpu.make_async_remote_copy(
            src_ref=source,
            dst_ref=target.at[slot],
            send_sem=out.at[slot],
            recv_sem=into.at[slot],
            device_id=(partner(dz, dx), cell_to),
            device_id_type=MESH,
        )

    ups = [
        edge_copy(edge_s.at[pl.ds(16, 16)], k, up, prev_s, up_out, up_in)
        for k in range(8)
    ]
    downs, far_downs = (
        [edge_copy(source, k, down, next_s, down_out, down_in) for k in range(8)]
        for source in (edge_s.at[pl.ds(0, 16)], early_s)
    )

    shared, far_shared = (
        [
            pltpu.make_async_remote_copy(
                src_ref=source,
                dst_ref=target.at[dz * 4 + dx],
                send_sem=out.at[dz * 4 + dx],
                recv_sem=into.at[dz * 4 + dx],
                device_id=(partner(dz, dx), c),
                device_id_type=MESH,
            )
            for dz, dx in OFFSETS
        ]
        for source, target, out, into in (
            (token_s, tokens_s, token_out, token_in),
            (far_s, fars_s, far_out, far_in),
        )
    )

    def share(target, copies, made, made_score, cells):
        row = lax.broadcasted_iota(jnp.int32, (8, 64), 0)
        column = lax.broadcasted_iota(jnp.int32, (8, 64), 1)
        marks = [
            jnp.where(row == 0, one[:, 0:1], one[:, 1:2]) for one in (made_score, cells)
        ]
        target[...] = jnp.concatenate(
            [
                jnp.transpose(made)[0:8],
                jnp.where(column == 0, marks[0], jnp.where(column == 1, 1.0, marks[1])),
            ],
            axis=1,
        )
        for copy in copies:
            copy.start()

    @pl.when(far_down)
    def _():
        early_s[...] = edge_rows(peak, total, sums)[0:16]
        pl.semaphore_wait(ready, 7)
        for copy in far_downs:
            copy.start()

    @pl.when(has_down)
    def _():
        tail.wait_recv()

    parity = (lax.broadcasted_iota(jnp.int32, (64, 128), 1) & 1) == 0

    def late_tokens(rows, drawn, asked):
        made = [
            jnp.sum(enc_s[:, 0:128] * rows[t : t + 1], axis=1, keepdims=True)
            + drawn[:, t : t + 1]
            for t in range(2)
        ]
        made = gelu(jnp.where(parity, made[0], made[1]))
        asked = jnp.where(parity, asked[:, 0:1], asked[:, 1:2])
        return made, jnp.sum(made * asked, axis=0, keepdims=True)

    late, late_score = late_tokens(tail_s[...], drawn[:, 0:128], asked_s[:, 0:2])

    def share_own():
        column = lax.broadcasted_iota(jnp.int32, (1, 128), 1)
        share(
            token_s,
            shared,
            late,
            jnp.where(column < live, late_score + quality[:, 0:128], FLOOR),
            cell[:, 0:128].astype(jnp.float32),
        )

    pl.when(far_down)(share_own)
    cells = lax.broadcasted_iota(jnp.int32, (1, 256), 1)
    there = [
        (cells == cell[:, t : t + 1]) & (t < live) & has_down for t in range(2)
    ]
    scores = [
        jnp.where(there[t], late_score[:, t : t + 1] + quality[:, t : t + 1], FLOOR)
        for t in range(2)
    ]
    joint = jnp.maximum(peak, jnp.maximum(scores[0], scores[1]))
    factor = jnp.exp(peak - joint)
    total, sums = total * factor, sums * factor
    for t in range(2):
        weight = jnp.where(there[t], jnp.exp(scores[t] - joint), 0.0)
        total = total + weight
        sums = sums + late[:, t : t + 1] * weight

    edge_s[...] = edge_rows(joint, total, sums)

    @pl.when(jnp.logical_not(far_down))
    def _():
        pl.semaphore_wait(ready, 7)

    @pl.when(has_up)
    def _():
        for copy in ups:
            copy.start()

    @pl.when(has_down & jnp.logical_not(far_down))
    def _():
        for copy in downs:
            copy.start()

    pl.when(has_down & jnp.logical_not(far_down))(share_own)

    for i in range(6, 9):
        loads[i].wait()
    hp = hp_s[...]
    stacked = jnp.concatenate([hp[:, k * 64 : (k + 1) * 64] for k in range(9)], axis=0)
    stencil = dot(stacked, value_s[...])
    part0, part1, _ = split3(stencil)
    stencil_parts = jnp.concatenate([part0, part1, part0], axis=1).astype(jnp.bfloat16)
    near = near_s[...] - c * 256
    near_edge = ((near >> 4) & 15) + jnp.where(near < 0, 16, 0)
    near_side = (near < 0) | (near >= 256)

    @pl.when(far_up)
    def _():
        packet.wait_recv()
        made, made_score = late_tokens(
            head_s[...], packed_s[0:64, 0:2], packed_s[0:64, 2:4]
        )
        share(
            far_s,
            far_shared,
            made,
            jnp.where(packed_s[66:67] > 0.0, made_score + packed_s[64:65], FLOOR),
            packed_s[65:66],
        )

    for copy in parts:
        copy.wait_recv()
    blocks = [send_s[s]] + [part_s[k] for k in range(1, 8)]
    spans = [span_s[...]] + [spans_s[k] for k in range(1, 8)]
    peaks = jnp.concatenate([one[0:1] for one in spans], axis=0)
    totals = jnp.concatenate([one[1:2] for one in spans], axis=0)
    joint = jnp.max(peaks, axis=0, keepdims=True)
    factor = jnp.exp(peaks - joint)
    below = jnp.sum(totals * factor, axis=0, keepdims=True)
    pool_s[s] = sum(blocks[k] * factor[k : k + 1] for k in range(8)) / below

    pools = []
    for dz, dx in OFFSETS:
        slot = dz * 4 + dx
        copy = pltpu.make_async_remote_copy(
            src_ref=pool_s.at[s],
            dst_ref=pool_s.at[s],
            send_sem=pool_out.at[slot],
            recv_sem=pool_in.at[slot],
            device_id=(partner(dz, dx), c),
            device_id_type=MESH,
        )
        copy.start()
        pools.append(copy)

    @pl.when(jnp.logical_not(has_down))
    def _():
        scale_s[...] = jnp.ones((1, 256), jnp.float32)
        shift_s[...] = jnp.zeros((64, 256), jnp.float32)

    @pl.when(has_down)
    def _():
        for copy in shared:
            copy.wait_recv()
        rows = jnp.concatenate(
            [token_s[0:2]] + [tokens_s[k, 0:2] for k in range(1, 8)], axis=0
        )
        cells = lax.broadcasted_iota(jnp.int32, (16, 256), 1).astype(jnp.float32)
        entries = jnp.where(cells == rows[:, 66:67], rows[:, 64:65], FLOOR)
        all_joint = jnp.maximum(joint, jnp.max(entries, axis=0, keepdims=True))
        weight = jnp.exp(entries - all_joint)
        old = below * jnp.exp(joint - all_joint)
        share_of = 1.0 / (old + jnp.sum(weight, axis=0, keepdims=True))
        scale_s[...] = old * share_of
        shift_s[...] = dot(rows[:, 0:64], weight * share_of, ((0,), (0,)))

    @pl.when(has_down)
    def _():
        for copy in ups:
            copy.wait_recv()

    @pl.when(has_up)
    def _():
        for copy in downs:
            copy.wait_recv()

    def mean(blocks):
        joint = functools.reduce(jnp.maximum, blocks)[:, 64:65]
        whole = sum(block * jnp.exp(block[:, 64:65] - joint) for block in blocks)
        return whole[:, 0:64] / whole[:, 65:66]

    below_blocks = [next_s[k] for k in range(8)]

    @pl.when(jnp.logical_not(far_up))
    def _():
        side_s[...] = mean(below_blocks)

    @pl.when(far_up)
    def _():
        for copy in far_shared:
            copy.wait_recv()
        first_cell = lax.broadcasted_iota(jnp.int32, (16, 128), 0).astype(jnp.float32) * 16.0
        more = []
        for tokens in [far_s[...]] + [fars_s[k] for k in range(1, 8)]:
            for t in range(2):
                more.append(
                    jnp.where(
                        first_cell == tokens[t : t + 1, 66:67], tokens[t : t + 1], FLOOR
                    )
                )
        side_s[...] = mean(below_blocks + more)

    edges = jnp.concatenate(
        [
            side_s[...],
            mean([prev_s[k] for k in range(8)]),
            jnp.zeros((96, 64), jnp.float32),
        ],
        axis=0,
    )
    outer = dot(stencil[8:72], edges, turned, HIGH)
    outside = []
    for h in range(2):
        cut = slice(h * 128, (h + 1) * 128)
        part = jnp.zeros((8, 128), jnp.float32)
        for k in range(8):
            index = jnp.broadcast_to(near_edge[k : k + 1, cut], (8, 128))
            side = jnp.broadcast_to(near_side[k : k + 1, cut], (8, 128))
            part = part + jnp.where(
                side, lanes(outer[k * 8 : (k + 1) * 8], index), 0.0
            )
        outside.append(part)

    for copy in pools:
        copy.wait_recv()
    pooled = pool_s[...].reshape(64, 256) * scale_s[...] + shift_s[...]
    part0, part1, _ = split3(pooled)
    inner = dot(
        stencil_parts,
        jnp.concatenate([part0, part0, part1], axis=0).astype(jnp.bfloat16),
        precision=None,
    )
    for h in range(2):
        cut = slice(h * 128, (h + 1) * 128)
        joined = inner[0:8, cut] + outside[h]
        for k in range(8):
            row = inner[8 + k * 8 : 16 + k * 8]
            index = jnp.broadcast_to(near[k : k + 1, cut], (8, 128))
            side = jnp.broadcast_to(near_side[k : k + 1, cut], (8, 128))
            picked = jnp.where(
                (index & 128) > 0,
                lanes(row[:, 128:], index & 127),
                lanes(row[:, :128], index & 127),
            )
            joined = joined + jnp.where(side, 0.0, picked)
        out_ref[:, cut] = joined

    @pl.when(has_up)
    def _():
        for copy in [tail] + ups:
            copy.wait_send()

    @pl.when(has_down)
    def _():
        for copy in downs:
            copy.wait_send()

    @pl.when(far_down)
    def _():
        packet.wait_send()

    @pl.when(has_down)
    def _():
        for copy in shared:
            copy.wait_send()

    @pl.when(far_up)
    def _():
        for copy in far_shared:
            copy.wait_send()

    for copy in parts + pools:
        copy.wait_send()


def on_device(*operands):
    f32, i32 = jnp.float32, jnp.int32
    dma = pltpu.SemaphoreType.DMA
    return pl.pallas_call(
        kernel,
        out_shape=pltpu.VMEM((8, 256), f32),
        in_specs=[
            pl.BlockSpec(memory_space=pltpu.SMEM if i == 7 else pltpu.HBM)
            for i in range(10)
        ],
        out_specs=pl.BlockSpec(memory_space=pltpu.VMEM),
        scratch_shapes=[
            pltpu.VMEM((64, 512), f32),
            pltpu.VMEM((64, 192), f32),
            pltpu.VMEM((64, 64), f32),
            pltpu.VMEM((64, 64), f32),
            pltpu.VMEM((64, 256), f32),
            pltpu.VMEM((1, 512), f32),
            pltpu.VMEM((1, 512), i32),
            pltpu.VMEM((8, 256), i32),
            pltpu.VMEM((8, 576), f32),
            pltpu.VMEM((256, 512), jnp.bfloat16),
            pltpu.VMEM((64, 512), f32),
            pltpu.VMEM((1, 256), f32),
            pltpu.VMEM((8, 128), f32),
            pltpu.VMEM((8, 128), f32),
            pltpu.VMEM((8, 8, 256), f32),
            pltpu.VMEM((2, 256), f32),
            pltpu.VMEM((32, 128), f32),
            pltpu.VMEM((16, 128), f32),
            pltpu.VMEM((72, 128), f32),
            pltpu.VMEM((72, 128), f32),
            pltpu.VMEM((8, 128), f32),
            pltpu.VMEM((8, 8, 128), f32),
            pltpu.VMEM((8, 128), f32),
            pltpu.VMEM((8, 8, 128), f32),
            pltpu.VMEM((1, 256), f32),
            pltpu.VMEM((64, 256), f32),
            pltpu.VMEM((16, 64), f32),
            pltpu.VMEM((8, 8, 256), f32),
            pltpu.VMEM((8, 2, 256), f32),
            pltpu.VMEM((8, 8, 256), f32),
            pltpu.VMEM((8, 16, 128), f32),
            pltpu.VMEM((8, 16, 128), f32),
            dma((9,)),
            dma((2,)),
        ]
        + [dma((8,))] * 10
        + [dma((2,))]
        + [dma((8,))] * 4
        + [pltpu.SemaphoreType.REGULAR],
        compiler_params=pltpu.CompilerParams(collective_id=0, has_side_effects=True),
    )(*operands)


def solution(mesh):
    in_specs = (
        P("sensor", None, "cell"),
        P("sensor", None, None),
        P(),
        P(),
        P(None, "cell"),
        P("sensor", "cell"),
        P("sensor", "cell"),
        P("sensor", "cell"),
        P(None, "cell"),
        P(),
    )
    return jax.shard_map(
        on_device,
        mesh=mesh,
        in_specs=in_specs,
        out_specs=P("sensor", "cell"),
        check_vma=False,
    )
```
